256 devices in a mesh: row: 16 (over x, z_lo), col: 8 (over y, z_hi), ch: 2 (over core).
Axes of the slice: x: 4, y: 4, z: 8 (z_hi: 2, z_lo: 4; z = z_hi * 4 + z_lo), core: 2. Of those that a mesh axis runs over, the one named last changes fastest.
Arguments:
- pair: bfloat16 [384, 384, 128], P('row', 'col'), may hold values from -6 to 6
- cotangent: bfloat16 [384, 384, 128], P('row', 'col', 'ch'), may hold values from -6 to 6
- w_gate_a: bfloat16 [128, 128], P(None, 'ch'), may hold values from -0.5 to 0.5
- w_proj_a: bfloat16 [128, 128], P(None, 'ch'), may hold values from -0.5 to 0.5
- w_gate_b: bfloat16 [128, 128], P(None, 'ch'), may hold values from -0.5 to 0.5
- w_proj_b: bfloat16 [128, 128], P(None, 'ch'), may hold values from -0.5 to 0.5
- w_gate_out: bfloat16 [128, 128], P(None, 'ch'), may hold values from -0.5 to 0.5
- w_out: bfloat16 [128, 128], P(None, 'ch'), may hold values from -0.5 to 0.5
Outputs:
- updated: bfloat16 [384, 384, 128], P('row', 'col', 'ch')
- grad_pair: bfloat16 [384, 384, 128], P('row', 'col', 'ch')
- grad_gate_a: float32 [128, 128], P(None, 'ch')
- grad_proj_a: float32 [128, 128], P(None, 'ch')
- grad_gate_b: float32 [128, 128], P(None, 'ch')
- grad_proj_b: float32 [128, 128], P(None, 'ch')
- grad_gate_out: float32 [128, 128], P(None, 'ch')
- grad_out: float32 [128, 128], P(None, 'ch')
The draws below stay inside these ranges and needn't reach their ends.
All inputs are finite; a program needn't handle non-finite values.
Results may differ from the reference program's by a relative error of at most 0.022.
Values may be sent and summed in bfloat16 or wider, within the bound.
A program may use at most 64 MiB of HBM per device.

```python
import jax
import jax.numpy as jnp
from jax import lax

C = 128
CH = 128
N = 384


def block_scale(key, shape, cuts, low, top_value):
    factor_of = 1.0
    for axis_at, parts in cuts:
        heights = jax.random.uniform(jax.random.fold_in(jax.random.fold_in(key, 6), axis_at), (parts,), jnp.float32, low / len(cuts), top_value / len(cuts))
        factor_of = factor_of * jnp.repeat(jnp.exp(heights), shape[axis_at] // parts).reshape((-1,) + (1,) * (len(shape) - 1 - axis_at))
    return factor_of


def bell_draw(stream_key, dims, deviation, limit, shards=(), dtype=jnp.bfloat16):
    drawn = jax.random.normal(stream_key, dims, jnp.float32) * deviation
    if len(shards) > 0:
        drawn = block_scale(stream_key, dims, shards, -0.22, 0.18) * drawn
    return jnp.clip(drawn, min=-limit, max=limit).astype(dtype)


def setup_inputs(seed: int = 0) -> dict:
    keys = jax.random.split(jax.random.key(seed), 9)
    return {
        "pair": bell_draw(keys[0], (N, N, C), 1.0, 6.0, ((0, 16), (1, 8))),
        "cotangent": bell_draw(keys[1], (N, N, C), 1.0, 6.0, ((0, 16), (1, 8), (2, 2))),
        "w_gate_a": bell_draw(keys[2], (C, CH), C ** -0.5, 0.5, ((1, 2),)),
        "w_proj_a": bell_draw(keys[3], (C, CH), C ** -0.5, 0.5, ((1, 2),)),
        "w_gate_b": bell_draw(keys[4], (C, CH), C ** -0.5, 0.5, ((1, 2),)),
        "w_proj_b": bell_draw(keys[5], (C, CH), C ** -0.5, 0.5, ((1, 2),)),
        "w_gate_out": bell_draw(keys[6], (C, C), C ** -0.5, 0.5, ((1, 2),)),
        "w_out": bell_draw(keys[7], (CH, C), CH ** -0.5, 0.5, ((1, 2),)),
    }


epsilon = 1e-05

def layer_norm(values):
    average = lax.optimization_barrier(jnp.mean(values, -1, keepdims=True))
    centred = values - average
    spread = lax.optimization_barrier(jnp.mean(centred * centred, -1, keepdims=True))
    inverse = lax.rsqrt(spread + epsilon)
    return (centred * inverse, inverse)

def norm_back(grad, hat, inverse):
    return inverse * (grad - lax.optimization_barrier(jnp.mean(grad, -1, keepdims=True)) - hat * lax.optimization_barrier(jnp.mean(grad * hat, -1, keepdims=True)))

def matmul(first, second):
    return jnp.dot(first, second, preferred_element_type=jnp.float32)

def reference(pair, cotangent, w_gate_a, w_proj_a, w_gate_b, w_proj_b, w_gate_out, w_out):
    pair_hat, pair_rstd = layer_norm(pair.astype(jnp.float32))
    flat_norm = pair_hat.astype(jnp.bfloat16).reshape(N * N, C)
    gate_a = jax.nn.sigmoid(matmul(flat_norm, w_gate_a))
    proj_a = matmul(flat_norm, w_proj_a)
    gate_b = jax.nn.sigmoid(matmul(flat_norm, w_gate_b))
    proj_b = matmul(flat_norm, w_proj_b)
    left_edge = (gate_a * proj_a).astype(jnp.bfloat16).reshape(N, N, CH)
    right_edge = (gate_b * proj_b).astype(jnp.bfloat16).reshape(N, N, CH)
    mixed = jnp.einsum('ikh,jkh->ijh', left_edge.astype(jnp.float32), right_edge.astype(jnp.float32))
    hidden_mean = lax.optimization_barrier(jnp.mean(mixed, -1, keepdims=True))
    hidden_var = lax.optimization_barrier(jnp.mean(mixed * mixed, -1, keepdims=True)) - hidden_mean * hidden_mean
    hidden_rstd = lax.rsqrt(hidden_var + epsilon)
    mixed_hat = (mixed - hidden_mean) * hidden_rstd
    mixed_norm = mixed_hat.astype(jnp.bfloat16).reshape(N * N, CH)
    gate_out = jax.nn.sigmoid(matmul(flat_norm, w_gate_out))
    proj_out = matmul(mixed_norm, w_out)
    updated = (gate_out * proj_out).astype(jnp.bfloat16).reshape(N, N, C)
    upstream = cotangent.reshape(N * N, C).astype(jnp.float32)
    d_proj = (upstream * gate_out).astype(jnp.bfloat16)
    d_gate = (upstream * proj_out * gate_out * (1.0 - gate_out)).astype(jnp.bfloat16)
    grad_scale = 1.0 / N
    grad_out = matmul(mixed_norm.T, d_proj) * grad_scale
    grad_gate_out = matmul(flat_norm.T, d_gate) * grad_scale
    d_norm = matmul(d_proj, w_out.T).reshape(N, N, CH)
    d_mixed = norm_back(d_norm, mixed_hat, hidden_rstd).astype(jnp.bfloat16).astype(jnp.float32)
    d_left = jnp.einsum('ijh,jkh->ikh', d_mixed, right_edge.astype(jnp.float32)).reshape(N * N, CH)
    d_right = jnp.einsum('ijh,ikh->jkh', d_mixed, left_edge.astype(jnp.float32)).reshape(N * N, CH)
    grad_pa = (d_left * gate_a).astype(jnp.bfloat16)
    grad_ga = (d_left * proj_a * gate_a * (1.0 - gate_a)).astype(jnp.bfloat16)
    grad_pb = (d_right * gate_b).astype(jnp.bfloat16)
    grad_gb = (d_right * proj_b * gate_b * (1.0 - gate_b)).astype(jnp.bfloat16)
    grad_gate_a = matmul(flat_norm.T, grad_ga) * grad_scale
    grad_proj_a = matmul(flat_norm.T, grad_pa) * grad_scale
    grad_gate_b = matmul(flat_norm.T, grad_gb) * grad_scale
    grad_proj_b = matmul(flat_norm.T, grad_pb) * grad_scale
    d_input = matmul(grad_ga, w_gate_a.T) + matmul(grad_pa, w_proj_a.T)
    d_input = d_input + matmul(grad_gb, w_gate_b.T) + matmul(grad_pb, w_proj_b.T)
    d_input = d_input + matmul(d_gate, w_gate_out.T)
    grad_pair = norm_back(d_input.reshape(N, N, C), pair_hat, pair_rstd).astype(jnp.bfloat16)
    return (updated, grad_pair, grad_gate_a, grad_proj_a, grad_gate_b, grad_proj_b, grad_gate_out, grad_out)
```

```python
import functools

import jax
import jax.numpy as jnp
from jax import lax
from jax.experimental import pallas as pl
from jax.experimental.pallas import tpu as pltpu
from jax.sharding import PartitionSpec as P

MESH = pl.DeviceIdType.MESH
epsilon = 1e-05
VMEM = pl.BlockSpec(memory_space=pltpu.VMEM)


def layer_norm(values):
    average = jnp.mean(values, -1, keepdims=True)
    centred = values - average
    spread = jnp.mean(centred * centred, -1, keepdims=True)
    inverse = lax.rsqrt(spread + epsilon)
    return (centred * inverse, inverse)


def matmul(first, second):
    return jnp.dot(first, second, preferred_element_type=jnp.float32)


def mirror():
    row, col, ch = lax.axis_index("row"), lax.axis_index("col"), lax.axis_index("ch")
    slot = (row % 8) * 8 + col
    half = row // 8

    def peer(t):
        return (8 * ch + t // 8, t % 8, half)

    return slot, half == ch, peer


def swap_kernel(x_ref, y_ref, send_sem, recv_sem, local_sem):
    slot, own, peer = mirror()
    barrier = pltpu.get_barrier_semaphore()

    @pl.loop(1, 64)
    def _(k):
        pl.semaphore_signal(barrier, inc=1, device_id=peer((slot + k) % 64), device_id_type=MESH)

    @pl.when(jnp.logical_not(own))
    def _():
        pl.semaphore_signal(barrier, inc=1, device_id=peer(slot), device_id_type=MESH)
        pl.semaphore_wait(barrier, 64)

    @pl.when(own)
    def _():
        pl.semaphore_wait(barrier, 63)

    def copy(t):
        return pltpu.make_async_remote_copy(
            src_ref=x_ref.at[t],
            dst_ref=y_ref.at[slot],
            send_sem=send_sem,
            recv_sem=recv_sem,
            device_id=peer(t),
            device_id_type=MESH,
        )

    @pl.when(own)
    def _():
        local = pltpu.make_async_copy(x_ref.at[slot], y_ref.at[slot], local_sem)
        local.start()
        local.wait()

    @pl.when(jnp.logical_not(own))
    def _():
        copy(slot).start()

    @pl.loop(1, 64)
    def _(k):
        copy((slot + k) % 64).start()

    whole = pltpu.make_async_copy(x_ref.at[pl.ds(0, 63)], y_ref.at[pl.ds(0, 63)], recv_sem)
    sent = pltpu.make_async_copy(x_ref.at[pl.ds(0, 63)], y_ref.at[pl.ds(0, 63)], send_sem)

    @pl.when(jnp.logical_not(own))
    def _():
        pltpu.make_async_copy(x_ref, y_ref, recv_sem).wait()
        pltpu.make_async_copy(x_ref, y_ref, send_sem).wait()

    @pl.when(own)
    def _():
        whole.wait()
        sent.wait()


def swap(values, tag):
    return pl.pallas_call(
        swap_kernel,
        out_shape=jax.ShapeDtypeStruct(values.shape, values.dtype),
        in_specs=[VMEM],
        out_specs=VMEM,
        scratch_shapes=[pltpu.SemaphoreType.DMA, pltpu.SemaphoreType.DMA, pltpu.SemaphoreType.DMA],
        compiler_params=pltpu.CompilerParams(collective_id=tag, has_side_effects=True),
    )(values)


def partner_kernel(n, *refs):
    xs, ys = refs[:n], refs[n : 2 * n]
    send_sem, recv_sem = refs[2 * n :]
    other = (lax.axis_index("row"), lax.axis_index("col"), 1 - lax.axis_index("ch"))
    barrier = pltpu.get_barrier_semaphore()
    pl.semaphore_signal(barrier, inc=1, device_id=other, device_id_type=MESH)
    pl.semaphore_wait(barrier, 1)
    copies = [
        pltpu.make_async_remote_copy(
            src_ref=xs[k],
            dst_ref=ys[k],
            send_sem=send_sem.at[k],
            recv_sem=recv_sem.at[k],
            device_id=other,
            device_id_type=MESH,
        )
        for k in range(n)
    ]
    for copy in copies:
        copy.start()
    for copy in copies:
        copy.wait()


def partner(arrays, tag):
    n = len(arrays)
    return pl.pallas_call(
        functools.partial(partner_kernel, n),
        out_shape=[jax.ShapeDtypeStruct(a.shape, a.dtype) for a in arrays],
        in_specs=[VMEM] * n,
        out_specs=[VMEM] * n,
        scratch_shapes=[pltpu.SemaphoreType.DMA((n,)), pltpu.SemaphoreType.DMA((n,))],
        compiler_params=pltpu.CompilerParams(collective_id=tag, has_side_effects=True),
    )(*arrays)


def total_kernel(x_ref, y_ref, parts, mine, send_sem, recv_sem, send_two, recv_two, local_sem):
    row, col, ch = lax.axis_index("row"), lax.axis_index("col"), lax.axis_index("ch")
    me = row * 8 + col

    def peer(k):
        t = (me + k) % 128
        return t, (t // 8, t % 8, ch)

    barrier = pltpu.get_barrier_semaphore()

    @pl.loop(1, 128)
    def _(k):
        pl.semaphore_signal(barrier, inc=1, device_id=peer(k)[1], device_id_type=MESH)

    pl.semaphore_wait(barrier, 127)
    local = pltpu.make_async_copy(x_ref.at[me], parts.at[me], local_sem)
    local.start()

    @pl.loop(1, 128)
    def _(k):
        t, device = peer(k)
        pltpu.make_async_remote_copy(
            src_ref=x_ref.at[t],
            dst_ref=parts.at[me],
            send_sem=send_sem,
            recv_sem=recv_sem,
            device_id=device,
            device_id_type=MESH,
        ).start()

    local.wait()
    pltpu.make_async_copy(x_ref.at[pl.ds(0, 127)], parts.at[pl.ds(0, 127)], recv_sem).wait()
    mine[...] = jnp.sum(parts[...], 0)
    y_ref[me] = mine[...]

    @pl.loop(1, 128)
    def _(k):
        t, device = peer(k)
        pltpu.make_async_remote_copy(
            src_ref=mine,
            dst_ref=y_ref.at[me],
            send_sem=send_two,
            recv_sem=recv_two,
            device_id=device,
            device_id_type=MESH,
        ).start()

    pltpu.make_async_copy(x_ref.at[pl.ds(0, 127)], y_ref.at[pl.ds(0, 127)], recv_two).wait()
    pltpu.make_async_copy(x_ref.at[pl.ds(0, 127)], y_ref.at[pl.ds(0, 127)], send_two).wait()
    pltpu.make_async_copy(x_ref.at[pl.ds(0, 127)], y_ref.at[pl.ds(0, 127)], send_sem).wait()


def total(values, tag):
    rows, width = values.shape
    out = pl.pallas_call(
        total_kernel,
        out_shape=jax.ShapeDtypeStruct((rows, 1, width), values.dtype),
        in_specs=[VMEM],
        out_specs=VMEM,
        scratch_shapes=[
            pltpu.VMEM((rows, 1, width), values.dtype),
            pltpu.VMEM((1, width), values.dtype),
        ]
        + [pltpu.SemaphoreType.DMA] * 5,
        compiler_params=pltpu.CompilerParams(collective_id=tag, has_side_effects=True),
    )(values.reshape(rows, 1, width))
    return out.reshape(rows, width)


def on_device(pair, cotangent, w_gate_a, w_proj_a, w_gate_b, w_proj_b, w_gate_out, w_out):
    bf16 = jnp.bfloat16
    row_count, col_count, channels = pair.shape
    pairs = row_count * col_count
    ch = lax.axis_index("ch")
    grad_scale = 1.0 / 384

    def both(mine, others, axis):
        first = jnp.where(ch == 0, mine, others)
        second = jnp.where(ch == 0, others, mine)
        return jnp.concatenate([first, second], axis)

    upstream = cotangent.reshape(pairs, 64)
    w_gate_o, w_o, upstream_o = partner([w_gate_out, w_out, upstream], 0)
    w_gate_all = both(w_gate_out, w_gate_o, 1)
    w_out_all = both(w_out, w_o, 1)
    upstream_all = both(upstream, upstream_o, 1).astype(jnp.float32)

    pair_hat, pair_rstd = layer_norm(pair.astype(jnp.float32).reshape(pairs, channels))
    flat_norm = pair_hat.astype(bf16)
    w_four = jnp.concatenate([w_gate_a, w_proj_a, w_gate_b, w_proj_b], axis=1)
    projected = matmul(w_four.T, flat_norm.T)
    gate_a = jax.nn.sigmoid(projected[0:64])
    proj_a = projected[64:128]
    gate_b = jax.nn.sigmoid(projected[128:192])
    proj_b = projected[192:256]

    def pack(*arrays):
        rows = 9 * len(arrays)
        stacked = jnp.concatenate([a.astype(bf16).reshape(64, 9, 128) for a in arrays], 1)
        return jnp.pad(stacked, ((0, 0), (0, (rows + 7) // 8 * 8 - rows), (0, 0)))

    def grid_of(block):
        block = block.reshape(8, 8, 24, 48)
        return jnp.transpose(block, (0, 2, 1, 3)).reshape(192, 384)

    def blocks_of(grid):
        grid = grid.reshape(8, 24, 8, 48)
        return jnp.transpose(grid, (0, 2, 1, 3)).reshape(64, 1152)

    edges = swap(pack(gate_a * proj_a, gate_b * proj_b), 1)
    left = grid_of(edges[:, 0:9])
    right_mine = grid_of(edges[:, 9:18])
    (right_other,) = partner([right_mine], 2)
    right = both(right_mine, right_other, 0)
    mixed_grid = matmul(left, right.T)
    mixed_mine = swap(pack(blocks_of(mixed_grid)), 3)[:, :9].reshape(64, pairs)
    (mixed_other,) = partner([mixed_mine], 4)
    mixed = both(mixed_mine, mixed_other, 0).astype(jnp.float32)

    mean = jnp.mean(mixed, 0, keepdims=True)
    var = jnp.mean(mixed * mixed, 0, keepdims=True) - mean * mean
    rstd = lax.rsqrt(var + epsilon)
    mixed_hat = (mixed - mean) * rstd
    mixed_norm = mixed_hat.astype(bf16)
    gate_out = jax.nn.sigmoid(matmul(flat_norm, w_gate_all))
    proj_out = matmul(mixed_norm.T, w_out_all)
    updated = (gate_out * proj_out).astype(bf16)
    d_proj = (upstream_all * gate_out).astype(bf16)
    d_gate = (upstream_all * proj_out * gate_out * (1.0 - gate_out)).astype(bf16)
    d_norm = matmul(w_out_all, d_proj.T)
    d_mixed = rstd * (
        d_norm
        - jnp.mean(d_norm, 0, keepdims=True)
        - mixed_hat * jnp.mean(d_norm * mixed_hat, 0, keepdims=True)
    )
    mine = lambda a, axis: lax.dynamic_slice_in_dim(a, ch * 64, 64, axis)
    d_mixed = mine(d_mixed, 0)

    d_grid = grid_of(swap(pack(d_mixed), 5)[:, :9])
    d_left = matmul(d_grid, right)
    d_right_all = matmul(d_grid.T, left).astype(bf16)
    keep = lax.dynamic_slice_in_dim(d_right_all, ch * 192, 192, 0)
    give = lax.dynamic_slice_in_dim(d_right_all, (1 - ch) * 192, 192, 0)
    (got,) = partner([give], 6)
    d_right = keep.astype(jnp.float32) + got.astype(jnp.float32)
    back = swap(pack(blocks_of(d_left), blocks_of(d_right)), 7)
    d_left = back[:, 0:9].reshape(64, pairs).astype(jnp.float32)
    d_right = back[:, 9:18].reshape(64, pairs).astype(jnp.float32)

    grad_pa = (d_left * gate_a).astype(bf16)
    grad_ga = (d_left * proj_a * gate_a * (1.0 - gate_a)).astype(bf16)
    grad_pb = (d_right * gate_b).astype(bf16)
    grad_gb = (d_right * proj_b * gate_b * (1.0 - gate_b)).astype(bf16)
    d_four = jnp.concatenate([grad_ga, grad_pa, grad_gb, grad_pb], axis=0)
    d_gate_mine = mine(d_gate, 1)
    terms = jnp.concatenate(
        [
            matmul(flat_norm.T, d_four.T),
            matmul(flat_norm.T, d_gate_mine),
            matmul(mixed_norm, mine(d_proj, 1)),
        ],
        axis=1,
    )
    summed = total(terms, 8) * grad_scale
    d_flat = matmul(d_four.T, w_four.T) + matmul(d_gate_mine, w_gate_out.T)
    (d_other,) = partner([d_flat.astype(bf16)], 9)
    grad_whole = d_flat + d_other.astype(jnp.float32)
    grad_full = pair_rstd * (
        grad_whole
        - jnp.mean(grad_whole, -1, keepdims=True)
        - pair_hat * jnp.mean(grad_whole * pair_hat, -1, keepdims=True)
    )
    grad_pair = mine(grad_full, 1).astype(bf16).reshape(row_count, col_count, 64)
    return (
        mine(updated, 1).reshape(row_count, col_count, 64),
        grad_pair,
        summed[:, 0:64],
        summed[:, 64:128],
        summed[:, 128:192],
        summed[:, 192:256],
        summed[:, 256:320],
        summed[:, 320:384],
    )


def solution(mesh):
    wide = P("row", "col", "ch")
    narrow = P(None, "ch")
    return jax.shard_map(
        on_device,
        mesh=mesh,
        in_specs=(P("row", "col", None), wide) + (narrow,) * 6,
        out_specs=(wide, wide) + (narrow,) * 6,
        check_vma=False,
    )
```

```python
import jax
import jax.numpy as jnp
from jax import lax
from jax.experimental import pallas as pl
from jax.experimental.pallas import tpu as pltpu
from jax.sharding import PartitionSpec as P

MESH = pl.DeviceIdType.MESH
epsilon = 1e-05
f32, bf16 = jnp.float32, jnp.bfloat16
PAIRS, CHUNKS, LANES = 1152, 9, 128


def nn(a, b):
    return lax.dot_general(a, b, (((1,), (0,)), ((), ())), preferred_element_type=f32)


def nt(a, b):
    return lax.dot_general(a, b, (((1,), (1,)), ((), ())), preferred_element_type=f32)


def tn(a, b):
    return lax.dot_general(a, b, (((0,), (0,)), ((), ())), preferred_element_type=f32)


def sigmoid(x):
    return 1.0 / (1.0 + jnp.exp(-x))


def block_transpose(x):
    groups = x.shape[0] // 8
    x = x.reshape(groups, 8, 384)
    row = lax.broadcasted_iota(jnp.int32, x.shape, 1)
    part = lax.broadcasted_iota(jnp.int32, x.shape, 2) // 48
    for bit in (1, 2, 4):
        low = (row & bit) == 0
        same = low == ((part & bit) == 0)
        up = pltpu.roll(pltpu.roll(x, bit, 1), 384 - 48 * bit, 2)
        down = pltpu.roll(pltpu.roll(x, 8 - bit, 1), 48 * bit, 2)
        x = jnp.where(same, x, jnp.where(low, down, up))
    return x.reshape(groups * 8, 384)


def kernel(
    pair_ref, cot_ref, wga_ref, wpa_ref, wgb_ref, wpb_ref, wgo_ref, wo_ref,
    updated_ref, grad_ref, g0_ref, g1_ref, g2_ref, g3_ref, g4_ref, g5_ref,
    normed, hat, rstd1, acts, flat,
    send1, recv1, send2, recv2, send3, recv3, send4, recv4, send5, recv5, send6, recv6,
    left, right, dr_send, dr_recv, df_send, df_recv, part_send, part_recv,
    wgo_other, wo_other, cot_t, cot_other, gate_out, dproj, dgate, mixn, dfour,
    send_sem, recv_sem, psend_sem, precv_sem,
):
    row, col, ch = lax.axis_index("row"), lax.axis_index("col"), lax.axis_index("ch")
    slot = (row % 8) * 8 + col
    half = row // 8
    own = half == ch
    other = (row, col, 1 - ch)

    def peer(t):
        return (8 * ch + t // 8, t % 8, half)

    barrier = pltpu.get_barrier_semaphore()
    pl.semaphore_signal(barrier, inc=1, device_id=other, device_id_type=MESH)

    @pl.loop(1, 64)
    def _(k):
        pl.semaphore_signal(barrier, inc=1, device_id=peer((slot + k) % 64), device_id_type=MESH)

    @pl.when(jnp.logical_not(own))
    def _():
        pl.semaphore_signal(barrier, inc=1, device_id=peer(slot), device_id_type=MESH)

    def swap_start(n, src, dst, one=False):
        def at(t):
            return src if one else src.at[t]

        def copy(t):
            return pltpu.make_async_remote_copy(
                src_ref=at(t),
                dst_ref=dst.at[slot],
                send_sem=send_sem.at[n],
                recv_sem=recv_sem.at[n],
                device_id=peer(t),
                device_id_type=MESH,
            )

        @pl.when(own)
        def _():
            pltpu.make_async_copy(at(slot), dst.at[slot], recv_sem.at[n]).start()

        @pl.when(jnp.logical_not(own))
        def _():
            copy(slot).start()

        @pl.loop(1, 64)
        def _(k):
            copy((slot + k) % 64).start()

    def swap_wait(n, dst):
        pltpu.make_async_copy(dst, dst, recv_sem.at[n]).wait()

    def swap_drain(n, dst):
        @pl.when(own)
        def _():
            some = dst.at[pl.ds(0, 63)]
            pltpu.make_async_copy(some, some, send_sem.at[n]).wait()

        @pl.when(jnp.logical_not(own))
        def _():
            pltpu.make_async_copy(dst, dst, send_sem.at[n]).wait()

    def partner(n, src, dst):
        return pltpu.make_async_remote_copy(
            src_ref=src,
            dst_ref=dst,
            send_sem=psend_sem.at[n],
            recv_sem=precv_sem.at[n],
            device_id=other,
            device_id_type=MESH,
        )

    def put(t_rows, g, value):
        flat[pl.ds(g, 64, stride=t_rows), :] = value

    def get(t_rows, g):
        return flat[pl.ds(g, 64, stride=t_rows), :]

    def pack(t_rows, dst):
        dst[...] = flat[0 : 64 * t_rows, :].astype(bf16).reshape(dst.shape)

    def unpack(t_rows, src):
        flat[0 : 64 * t_rows, :] = src[...].reshape(64 * t_rows, LANES).astype(f32)

    def grid_of(t_rows, first):
        tiles = [None] * 24
        for gg in range(3):
            x = jnp.concatenate([get(t_rows, first + 3 * gg + q) for q in range(3)], axis=1)
            x = block_transpose(x)
            for r in range(8):
                tiles[r * 3 + gg] = x[8 * r : 8 * r + 8]
        return jnp.concatenate(tiles, axis=0)

    def put_grid(t_rows, first, grid):
        for gg in range(3):
            x = jnp.concatenate([grid[8 * (3 * r + gg) : 8 * (3 * r + gg) + 8] for r in range(8)], axis=0)
            x = block_transpose(x)
            for q in range(3):
                put(t_rows, first + 3 * gg + q, x[:, LANES * q : LANES * q + LANES])

    def chunk(g):
        return pl.ds(g * LANES, LANES)

    w_four = jnp.concatenate([wga_ref[...], wpa_ref[...], wgb_ref[...], wpb_ref[...]], axis=0)
    for g in range(CHUNKS):
        values = pair_ref[chunk(g), :].astype(f32)
        centred = values - jnp.mean(values, -1, keepdims=True)
        spread = jnp.mean(centred * centred, -1, keepdims=True)
        inverse = lax.rsqrt(spread + epsilon)
        hat_g = centred * inverse
        hat[chunk(g), :] = hat_g
        rstd1[chunk(g), :] = inverse
        normed_g = hat_g.astype(bf16)
        normed[chunk(g), :] = normed_g
        projected = nt(w_four, normed_g)
        gate_a = sigmoid(projected[0:64])
        proj_a = projected[64:128]
        gate_b = sigmoid(projected[128:192])
        proj_b = projected[192:256]
        acts[g, 0:64, :] = gate_a
        acts[g, 64:128, :] = proj_a
        acts[g, 128:192, :] = gate_b
        acts[g, 192:256, :] = proj_b
        put(18, g, gate_a * proj_a)
        put(18, 9 + g, gate_b * proj_b)
    pack(18, send1)

    @pl.when(own)
    def _():
        pl.semaphore_wait(barrier, 64)

    @pl.when(jnp.logical_not(own))
    def _():
        pl.semaphore_wait(barrier, 65)

    swap_start(0, send1, recv1)

    copies = [partner(0, wgo_ref, wgo_other), partner(1, wo_ref, wo_other)]
    for copy in copies:
        copy.start()
    for g in range(CHUNKS):
        cot_t[:, chunk(g)] = jnp.transpose(cot_ref[chunk(g), :].astype(f32)).astype(bf16)
    copies.append(partner(2, cot_t, cot_other))
    copies[2].start()
    for copy in copies:
        copy.wait_recv()
    wgo = jnp.concatenate([wgo_ref[...], wgo_other[...]], axis=0)
    for g in range(CHUNKS):
        gate_out[:, chunk(g)] = sigmoid(nt(wgo, normed[chunk(g), :]))
    mine_rows = pl.ds(pl.multiple_of(ch * 64, 64), 64)
    wo_cols = jnp.concatenate([wo_ref[...], wo_other[...]], axis=0).astype(f32)
    wo_t = jnp.where(ch == 0, wo_cols, pltpu.roll(wo_cols, 64, 1))
    wo = jnp.transpose(wo_t).astype(bf16)
    wo_t = wo_t.astype(bf16)

    swap_wait(0, recv1)
    unpack(18, recv1)
    mine_half = pl.ds(pl.multiple_of(ch * 192, 192), 192)
    other_half = pl.ds(pl.multiple_of((1 - ch) * 192, 192), 192)
    right[mine_half, :] = grid_of(18, 9).astype(bf16)
    right_copy = partner(3, right.at[mine_half, :], right.at[mine_half, :])
    right_copy.start()
    left[...] = grid_of(18, 0).astype(bf16)
    right_copy.wait_recv()
    put_grid(10, 0, nt(left[...], right[...]))
    pack(10, send2)
    swap_start(1, send2, recv2.at[0])
    swap_wait(1, recv2.at[0])
    mixed_copy = partner(4, recv2.at[0], recv2.at[1])
    mixed_copy.start()
    mixed_copy.wait_recv()

    flat_two = []
    unpack(10, recv2.at[0])
    first = [get(10, g) for g in range(CHUNKS)]
    for g in range(CHUNKS):
        mixn_f = first[g]
        dfour[0:64, chunk(g)] = mixn_f.astype(bf16)
    unpack(10, recv2.at[1])
    for g in range(CHUNKS):
        mixed = jnp.concatenate([dfour[0:64, chunk(g)].astype(f32), get(10, g)], axis=0)
        mean = jnp.mean(mixed, 0, keepdims=True)
        var = jnp.mean(mixed * mixed, 0, keepdims=True) - mean * mean
        inverse = lax.rsqrt(var + epsilon)
        mixed_hat = (mixed - mean) * inverse
        mixed_norm = mixed_hat.astype(bf16)
        mixn[:, chunk(g)] = mixed_norm
        gate = gate_out[:, chunk(g)]
        proj_out = nn(wo_t, mixed_norm)
        upstream = jnp.concatenate([cot_t[:, chunk(g)], cot_other[:, chunk(g)]], axis=0).astype(f32)
        d_proj = (upstream * gate).astype(bf16)
        d_norm = nn(wo, d_proj)
        d_mean = jnp.mean(d_norm, 0, keepdims=True)
        d_cross = jnp.mean(d_norm * mixed_hat, 0, keepdims=True)
        d_mixed = inverse[:, :] * (d_norm[0:64] - d_mean - mixed_hat[0:64] * d_cross)
        acts_flat = d_mixed
        dmix_rows = acts_flat
        flat_two.append(dmix_rows)
        dproj[:, chunk(g)] = d_proj[0:64]
        gate_mine, proj_mine = gate[0:64], proj_out[0:64]
        dgate[:, chunk(g)] = (upstream[0:64] * proj_mine * gate_mine * (1.0 - gate_mine)).astype(bf16)
        updated_ref[chunk(g), :] = jnp.transpose(gate_mine * proj_mine).astype(bf16)
    for g in range(CHUNKS):
        put(10, g, flat_two[g])
    pack(10, send3)
    swap_start(2, send3, recv3)
    head_gate = nn(dgate[...], normed[...])
    head_out = nt(dproj[...], mixn[...])

    swap_wait(2, recv3)
    unpack(10, recv3)
    d_grid = grid_of(10, 0).astype(bf16)
    d_right = tn(d_grid, left[...])
    dr_send[...] = d_right.astype(bf16)
    dr_copy = partner(5, dr_send.at[other_half, :], dr_recv)
    dr_copy.start()
    put_grid(18, 0, nn(d_grid, right[...]))
    dr_copy.wait_recv()
    put_grid(18, 9, dr_send[mine_half, :].astype(f32) + dr_recv[...].astype(f32))
    pack(18, send4)
    swap_start(3, send4, recv4)
    swap_wait(3, recv4)
    unpack(18, recv4)
    for g in range(CHUNKS):
        d_left, d_right_g = get(18, g), get(18, 9 + g)
        gate_a, proj_a = acts[g, 0:64, :], acts[g, 64:128, :]
        gate_b, proj_b = acts[g, 128:192, :], acts[g, 192:256, :]
        dfour[0:64, chunk(g)] = (d_left * proj_a * gate_a * (1.0 - gate_a)).astype(bf16)
        dfour[64:128, chunk(g)] = (d_left * gate_a).astype(bf16)
        dfour[128:192, chunk(g)] = (d_right_g * proj_b * gate_b * (1.0 - gate_b)).astype(bf16)
        dfour[192:256, chunk(g)] = (d_right_g * gate_b).astype(bf16)
    edge = nn(dfour[...], normed[...])

    for k in range(4):
        put(6, k, edge[64 * k : 64 * k + 64])
    put(6, 4, head_gate)
    put(6, 5, jnp.where(ch == 0, head_out, pltpu.roll(head_out, 64, 1)))
    pack(6, send5)
    swap_start(4, send5, recv5)
    for g in range(CHUNKS):
        d_flat = tn(dfour[:, chunk(g)], w_four) + tn(dgate[:, chunk(g)], wgo_ref[...])
        df_send[chunk(g), :] = d_flat.astype(bf16)
    df_copy = partner(6, df_send, df_recv)
    df_copy.start()
    swap_wait(4, recv5)
    unpack(6, recv5)
    part_send[...] = jnp.zeros_like(part_send)
    for k in range(6):
        part_send[k : k + 1, :] = jnp.sum(get(6, k), 0, keepdims=True)
    part_copy = partner(7, part_send, part_recv)
    part_copy.start()
    part_copy.wait_recv()
    send6[...] = (part_send[...] + part_recv[...])[0:6].astype(bf16).reshape(send6.shape)
    swap_start(5, send6, recv6, one=True)

    df_copy.wait_recv()
    for g in range(CHUNKS):
        grad_whole = df_send[chunk(g), :].astype(f32) + df_recv[chunk(g), :].astype(f32)
        hat_g = hat[chunk(g), :]
        grad_full = rstd1[chunk(g), :] * (
            grad_whole
            - jnp.mean(grad_whole, -1, keepdims=True)
            - hat_g * jnp.mean(grad_whole * hat_g, -1, keepdims=True)
        )
        grad_full = jnp.where(ch == 0, grad_full, pltpu.roll(grad_full, 64, 1))
        grad_ref[chunk(g), :] = grad_full[:, 0:64].astype(bf16)

    swap_wait(5, recv6)
    unpack(6, recv6)
    for k, g_ref in enumerate((g0_ref, g1_ref, g2_ref, g3_ref, g4_ref, g5_ref)):
        g_ref[...] = get(6, k) * (1.0 / 384)

    for n, dst in enumerate((recv1, recv2.at[0], recv3, recv4, recv5, recv6)):
        swap_drain(n, dst)
    for copy in copies + [right_copy, mixed_copy, dr_copy, df_copy, part_copy]:
        copy.wait_send()


def on_device(pair, cotangent, w_gate_a, w_proj_a, w_gate_b, w_proj_b, w_gate_out, w_out):
    rows, cols, channels = pair.shape
    whole = pl.BlockSpec(memory_space=pltpu.VMEM)
    weights = [w.T for w in (w_gate_a, w_proj_a, w_gate_b, w_proj_b, w_gate_out, w_out)]
    vm = pltpu.VMEM
    big, small, tiny = (64, 9, 2, 128), (64, 5, 2, 128), (64, 3, 2, 128)
    outs = pl.pallas_call(
        kernel,
        out_shape=[
            jax.ShapeDtypeStruct((PAIRS, 64), bf16),
            jax.ShapeDtypeStruct((PAIRS, 64), bf16),
        ]
        + [jax.ShapeDtypeStruct((64, 128), f32)] * 6,
        in_specs=[whole] * 8,
        out_specs=[whole] * 8,
        scratch_shapes=[
            vm((PAIRS, 128), bf16),
            vm((PAIRS, 128), f32),
            vm((PAIRS, 1), f32),
            vm((CHUNKS, 256, 128), f32),
            vm((PAIRS, 128), f32),
            vm(big, bf16), vm(big, bf16),
            vm(small, bf16), vm((2,) + small, bf16),
            vm(small, bf16), vm(small, bf16),
            vm(big, bf16), vm(big, bf16),
            vm(tiny, bf16), vm(tiny, bf16),
            vm((3, 2, 128), bf16), vm(tiny, bf16),
            vm((192, 384), bf16), vm((384, 384), bf16),
            vm((384, 384), bf16), vm((192, 384), bf16),
            vm((PAIRS, 128), bf16), vm((PAIRS, 128), bf16),
            vm((8, 128), f32), vm((8, 128), f32),
            vm((64, 128), bf16), vm((64, 128), bf16),
            vm((64, PAIRS), bf16), vm((64, PAIRS), bf16),
            vm((128, PAIRS), f32),
            vm((64, PAIRS), bf16), vm((64, PAIRS), bf16),
            vm((128, PAIRS), bf16),
            vm((256, PAIRS), bf16),
            pltpu.SemaphoreType.DMA((6,)),
            pltpu.SemaphoreType.DMA((6,)),
            pltpu.SemaphoreType.DMA((8,)),
            pltpu.SemaphoreType.DMA((8,)),
        ],
        compiler_params=pltpu.CompilerParams(
            collective_id=0, has_side_effects=True, vmem_limit_bytes=40 << 20
        ),
    )(pair.reshape(PAIRS, channels), cotangent.reshape(PAIRS, 64), *weights)
    updated, grad_pair, ga, pa, gb, pb, go, out = outs
    return (
        updated.reshape(rows, cols, 64),
        grad_pair.reshape(rows, cols, 64),
        ga.T,
        pa.T,
        gb.T,
        pb.T,
        go.T,
        out.T,
    )


def solution(mesh):
    wide = P("row", "col", "ch")
    narrow = P(None, "ch")
    return jax.shard_map(
        on_device,
        mesh=mesh,
        in_specs=(P("row", "col", None), wide) + (narrow,) * 6,
        out_specs=(wide, wide) + (narrow,) * 6,
        check_vma=False,
    )
```

```python
import jax
import jax.numpy as jnp
from jax import lax
from jax.experimental import pallas as pl
from jax.experimental.pallas import tpu as pltpu
from jax.sharding import PartitionSpec as P

MESH = pl.DeviceIdType.MESH
epsilon = 1e-05
f32, bf16 = jnp.float32, jnp.bfloat16
PAIRS, CHUNKS, LANES = 1152, 9, 128


def nn(a, b):
    return lax.dot_general(a, b, (((1,), (0,)), ((), ())), preferred_element_type=f32)


def nt(a, b):
    return lax.dot_general(a, b, (((1,), (1,)), ((), ())), preferred_element_type=f32)


def tn(a, b):
    return lax.dot_general(a, b, (((0,), (0,)), ((), ())), preferred_element_type=f32)


def sigmoid(x):
    return 1.0 / (1.0 + jnp.exp(-x))


def block_transpose(x):
    groups = x.shape[0] // 8
    x = x.reshape(groups, 8, 384)
    row = lax.broadcasted_iota(jnp.int32, x.shape, 1)
    part = lax.broadcasted_iota(jnp.int32, x.shape, 2) // 48
    for bit in (1, 2, 4):
        low = (row & bit) == 0
        same = low == ((part & bit) == 0)
        up = pltpu.roll(pltpu.roll(x, bit, 1), 384 - 48 * bit, 2)
        down = pltpu.roll(pltpu.roll(x, 8 - bit, 1), 48 * bit, 2)
        x = jnp.where(same, x, jnp.where(low, down, up))
    return x.reshape(groups * 8, 384)


def kernel(
    pair_hbm, cot_hbm, wga_hbm, wpa_hbm, wgb_hbm, wpb_hbm, wgo_hbm, wo_hbm,
    updated_ref, grad_ref, g0_ref, g1_ref, g2_ref, g3_ref, g4_ref, g5_ref,
    pair_ref, cot_ref, weights, load_sem, normed, hat, rstd1, acts, flat,
    send1, recv1, send2, recv2, send3, recv3, send4, recv4,
    send5, recv5, sendz, recvz, send6, recv6,
    left, right, dr_send, dr_recv, df_send, df_recv,
    wgo_other, wo_other, cot_t, cot_other, gate_out, dproj, dgate, mixn, dfour,
    send_sem, recv_sem, psend_sem, precv_sem, gsend_sem, grecv_sem,
):
    loads = [
        pltpu.make_async_copy(src, weights.at[pl.ds(64 * n, 64), :], load_sem.at[n])
        for n, src in enumerate((wga_hbm, wpa_hbm, wgb_hbm, wpb_hbm, wgo_hbm, wo_hbm))
    ]
    loads += [
        pltpu.make_async_copy(pair_hbm.at[rows, :], pair_ref.at[rows, :], load_sem.at[6 + n])
        for n, rows in enumerate(pl.ds(384 * k, 384) for k in range(3))
    ]
    loads.append(pltpu.make_async_copy(cot_hbm, cot_ref, load_sem.at[9]))
    for load in loads:
        load.start()
    wgo_ref, wo_ref = weights.at[pl.ds(256, 64), :], weights.at[pl.ds(320, 64), :]

    row, col, ch = lax.axis_index("row"), lax.axis_index("col"), lax.axis_index("ch")
    x, y, z = row // 4, col // 2, (col % 2) * 4 + row % 4
    slot = (row % 8) * 8 + col
    half = row // 8
    own = half == ch
    other = (row, col, 1 - ch)

    def peer(t):
        return (8 * ch + t // 8, t % 8, half)

    barrier = pltpu.get_barrier_semaphore()
    pl.semaphore_signal(barrier, inc=1, device_id=other, device_id_type=MESH)

    def each_peer(act):
        @pl.loop(0, 8)
        def _(k):
            away = (4 + (1 - 2 * (k % 2)) * ((k + 1) // 2)) % 8
            z_to = (z + away) % 8
            for dy in (2, 1, 3, 0):
                for dx in (1, 0):
                    t = ((x + dx) % 2) * 32 + (z_to % 4) * 8 + ((y + dy) % 4) * 2 + z_to // 4
                    if dy == 0 and dx == 0:

                        @pl.when(k < 7)
                        def _():
                            act(t)
                    else:
                        act(t)

    plane = [(2, 2), (2, 1), (2, 3), (1, 2), (3, 2), (2, 0), (0, 2), (1, 1), (1, 3), (3, 1), (3, 3)]
    plane += [(1, 0), (3, 0), (0, 1), (0, 3)]

    def plane_peer(dx, dy):
        x_to, y_to = (x + dx) % 4, (y + dy) % 4
        return x_to * 4 + y_to, (x_to * 4 + row % 4, y_to * 2 + col % 2, ch)

    def line_peer(dz):
        z_to = (z + dz) % 8
        return (x * 4 + z_to % 4, y * 2 + z_to // 4, ch)

    def greet(device):
        pl.semaphore_signal(barrier, inc=1, device_id=device, device_id_type=MESH)

    each_peer(lambda t: greet(peer(t)))

    @pl.when(jnp.logical_not(own))
    def _():
        greet(peer(slot))

    for dx, dy in plane:
        greet(plane_peer(dx, dy)[1])
    for dz in (4, 3, 5, 2, 6, 1, 7):
        greet(line_peer(dz))

    def swap_start(n, src, dst, part):
        def copy(t):
            return pltpu.make_async_remote_copy(
                src_ref=src.at[t, part],
                dst_ref=dst.at[slot, part],
                send_sem=send_sem.at[n],
                recv_sem=recv_sem.at[n],
                device_id=peer(t),
                device_id_type=MESH,
            )

        each_peer(lambda t: copy(t).start())

        @pl.when(own)
        def _():
            pltpu.make_async_copy(src.at[slot, part], dst.at[slot, part], recv_sem.at[n]).start()

        @pl.when(jnp.logical_not(own))
        def _():
            copy(slot).start()

    def swap_wait(n, dst, part):
        whole = dst.at[:, part]
        pltpu.make_async_copy(whole, whole, recv_sem.at[n]).wait()

    def swap_drain(n, dst, part):
        @pl.when(own)
        def _():
            some = dst.at[pl.ds(0, 63), part]
            pltpu.make_async_copy(some, some, send_sem.at[n]).wait()

        @pl.when(jnp.logical_not(own))
        def _():
            whole = dst.at[:, part]
            pltpu.make_async_copy(whole, whole, send_sem.at[n]).wait()

    def group_copy(n, src, dst, device):
        return pltpu.make_async_remote_copy(
            src_ref=src,
            dst_ref=dst,
            send_sem=gsend_sem.at[n],
            recv_sem=grecv_sem.at[n],
            device_id=device,
            device_id_type=MESH,
        )

    def partner(n, src, dst):
        return pltpu.make_async_remote_copy(
            src_ref=src,
            dst_ref=dst,
            send_sem=psend_sem.at[n],
            recv_sem=precv_sem.at[n],
            device_id=other,
            device_id_type=MESH,
        )

    def put(t_rows, g, value):
        flat[pl.ds(g, 64, stride=t_rows), :] = value

    def get(t_rows, g):
        return flat[pl.ds(g, 64, stride=t_rows), :]

    def pack(t_rows, dst):
        dst[...] = flat[0 : 64 * t_rows, :].astype(bf16).reshape(dst.shape)

    ten, early, late = pl.ds(0, 5), pl.ds(0, 5), pl.ds(5, 4)
    head, tail = pl.ds(0, 4), pl.ds(4, 5)

    def unpack(t_rows, src):
        flat[0 : 64 * t_rows, :] = src[...].reshape(64 * t_rows, LANES).astype(f32)

    def grid_of(t_rows, first):
        tiles = [None] * 24
        for gg in range(3):
            x = jnp.concatenate([get(t_rows, first + 3 * gg + q) for q in range(3)], axis=1)
            x = block_transpose(x)
            for r in range(8):
                tiles[r * 3 + gg] = x[8 * r : 8 * r + 8]
        return jnp.concatenate(tiles, axis=0)

    def put_grid(t_rows, first, grid):
        for gg in range(3):
            x = jnp.concatenate([grid[8 * (3 * r + gg) : 8 * (3 * r + gg) + 8] for r in range(8)], axis=0)
            x = block_transpose(x)
            for q in range(3):
                put(t_rows, first + 3 * gg + q, x[:, LANES * q : LANES * q + LANES])

    def chunk(g):
        return pl.ds(g * LANES, LANES)

    for load in loads[0:6]:
        load.wait()
    w_four = weights[0:256, :]
    for g in range(CHUNKS):
        if g % 3 == 0:
            loads[6 + g // 3].wait()
        values = pair_ref[chunk(g), :].astype(f32)
        centred = values - jnp.mean(values, -1, keepdims=True)
        spread = jnp.mean(centred * centred, -1, keepdims=True)
        inverse = lax.rsqrt(spread + epsilon)
        hat_g = centred * inverse
        hat[chunk(g), :] = hat_g
        rstd1[chunk(g), :] = inverse
        normed_g = hat_g.astype(bf16)
        normed[chunk(g), :] = normed_g
        projected = nt(w_four, normed_g)
        gate_a = sigmoid(projected[0:64])
        proj_a = projected[64:128]
        gate_b = sigmoid(projected[128:192])
        proj_b = projected[192:256]
        acts[g, 0:64, :] = gate_a
        acts[g, 64:128, :] = proj_a
        acts[g, 128:192, :] = gate_b
        acts[g, 192:256, :] = proj_b
        put(18, g, gate_b * proj_b)
        put(18, 9 + g, gate_a * proj_a)
    pack(18, send1)

    @pl.when(own)
    def _():
        pl.semaphore_wait(barrier, 86)

    @pl.when(jnp.logical_not(own))
    def _():
        pl.semaphore_wait(barrier, 87)

    swap_start(0, send1, recv1, early)
    swap_start(1, send1, recv1, late)

    copies = [partner(0, wgo_ref, wgo_other), partner(1, wo_ref, wo_other)]
    for copy in copies:
        copy.start()
    loads[9].wait()
    for g in range(CHUNKS):
        cot_t[:, chunk(g)] = jnp.transpose(cot_ref[chunk(g), :].astype(f32)).astype(bf16)
    copies.append(partner(2, cot_t, cot_other))
    copies[2].start()
    for copy in copies:
        copy.wait_recv()
    wgo = jnp.concatenate([wgo_ref[...], wgo_other[...]], axis=0)
    for g in range(CHUNKS):
        gate_out[:, chunk(g)] = sigmoid(nt(wgo, normed[chunk(g), :]))
    mine_rows = pl.ds(pl.multiple_of(ch * 64, 64), 64)
    wo_cols = jnp.concatenate([wo_ref[...], wo_other[...]], axis=0).astype(f32)
    wo_t = jnp.where(ch == 0, wo_cols, pltpu.roll(wo_cols, 64, 1))
    wo = jnp.transpose(wo_t).astype(bf16)
    wo_t = wo_t.astype(bf16)

    swap_wait(0, recv1, early)
    mine_half = pl.ds(pl.multiple_of(ch * 192, 192), 192)
    other_half = pl.ds(pl.multiple_of((1 - ch) * 192, 192), 192)
    flat[0:640, :] = recv1[:, early].reshape(640, LANES).astype(f32)
    right[mine_half, :] = grid_of(10, 0).astype(bf16)
    right_copy = partner(3, right.at[mine_half, :], right.at[mine_half, :])
    right_copy.start()
    swap_wait(1, recv1, late)
    unpack(18, recv1)
    left[...] = grid_of(18, 9).astype(bf16)
    right_copy.wait_recv()
    put_grid(10, 0, nt(left[...], right[...]))
    pack(10, send2)
    swap_start(2, send2, recv2.at[0], ten)
    swap_wait(2, recv2.at[0], ten)
    mixed_copy = partner(4, recv2.at[0], recv2.at[1])
    mixed_copy.start()
    mixed_copy.wait_recv()

    flat_two = []
    unpack(10, recv2.at[0])
    first = [get(10, g) for g in range(CHUNKS)]
    for g in range(CHUNKS):
        mixn_f = first[g]
        dfour[0:64, chunk(g)] = mixn_f.astype(bf16)
    unpack(10, recv2.at[1])
    for g in range(CHUNKS):
        mixed = jnp.concatenate([dfour[0:64, chunk(g)].astype(f32), get(10, g)], axis=0)
        mean = jnp.mean(mixed, 0, keepdims=True)
        var = jnp.mean(mixed * mixed, 0, keepdims=True) - mean * mean
        inverse = lax.rsqrt(var + epsilon)
        mixed_hat = (mixed - mean) * inverse
        mixed_norm = mixed_hat.astype(bf16)
        mixn[:, chunk(g)] = mixed_norm
        gate = gate_out[:, chunk(g)]
        proj_out = nn(wo_t, mixed_norm)
        upstream = jnp.concatenate([cot_t[:, chunk(g)], cot_other[:, chunk(g)]], axis=0).astype(f32)
        d_proj = (upstream * gate).astype(bf16)
        d_norm = nn(wo, d_proj)
        d_mean = jnp.mean(d_norm, 0, keepdims=True)
        d_cross = jnp.mean(d_norm * mixed_hat, 0, keepdims=True)
        d_mixed = inverse[:, :] * (d_norm[0:64] - d_mean - mixed_hat[0:64] * d_cross)
        acts_flat = d_mixed
        dmix_rows = acts_flat
        flat_two.append(dmix_rows)
        dproj[:, chunk(g)] = d_proj[0:64]
        gate_mine, proj_mine = gate[0:64], proj_out[0:64]
        dgate[:, chunk(g)] = (upstream[0:64] * proj_mine * gate_mine * (1.0 - gate_mine)).astype(bf16)
        updated_ref[chunk(g), :] = jnp.transpose(gate_mine * proj_mine).astype(bf16)
    for g in range(CHUNKS):
        put(10, g, flat_two[g])
    pack(10, send3)
    swap_start(3, send3, recv3, ten)
    head_gate = nn(dgate[...], normed[...])
    head_out = nt(dproj[...], mixn[...])

    swap_wait(3, recv3, ten)
    unpack(10, recv3)
    d_grid = grid_of(10, 0).astype(bf16)
    d_right = tn(d_grid, left[...])
    dr_send[...] = d_right.astype(bf16)
    dr_copy = partner(5, dr_send.at[other_half, :], dr_recv)
    dr_copy.start()
    put_grid(18, 0, nn(d_grid, right[...]))
    send4[:, head] = flat[...].astype(bf16).reshape(send4.shape)[:, 0:4]
    swap_start(4, send4, recv4, head)
    dr_copy.wait_recv()
    put_grid(18, 9, dr_send[mine_half, :].astype(f32) + dr_recv[...].astype(f32))
    send4[:, tail] = flat[...].astype(bf16).reshape(send4.shape)[:, 4:9]
    swap_start(5, send4, recv4, tail)
    swap_wait(4, recv4, head)
    swap_wait(5, recv4, tail)
    unpack(18, recv4)
    for g in range(CHUNKS):
        d_left, d_right_g = get(18, g), get(18, 9 + g)
        gate_a, proj_a = acts[g, 0:64, :], acts[g, 64:128, :]
        gate_b, proj_b = acts[g, 128:192, :], acts[g, 192:256, :]
        dfour[0:64, chunk(g)] = (d_left * proj_a * gate_a * (1.0 - gate_a)).astype(bf16)
        dfour[64:128, chunk(g)] = (d_left * gate_a).astype(bf16)
        dfour[128:192, chunk(g)] = (d_right_g * proj_b * gate_b * (1.0 - gate_b)).astype(bf16)
        dfour[192:256, chunk(g)] = (d_right_g * gate_b).astype(bf16)
    edge = nn(dfour[...], normed[...])

    for k in range(4):
        put(6, k, edge[64 * k : 64 * k + 64])
    put(6, 4, head_gate)
    put(6, 5, jnp.where(ch == 0, head_out, pltpu.roll(head_out, 64, 1)))
    pack(6, send5)
    e_me, _ = plane_peer(0, 0)
    for dx, dy in plane:
        e, device = plane_peer(dx, dy)
        group_copy(0, send5.at[e], recv5.at[e_me], device).start()
    pltpu.make_async_copy(send5.at[e_me], recv5.at[e_me], grecv_sem.at[0]).start()
    for g in range(CHUNKS):
        d_flat = tn(dfour[:, chunk(g)], w_four) + tn(dgate[:, chunk(g)], wgo_ref[...])
        df_send[chunk(g), :] = d_flat.astype(bf16)
    df_copy = partner(6, df_send, df_recv)
    df_copy.start()
    pltpu.make_async_copy(recv5, recv5, grecv_sem.at[0]).wait()
    sendz[...] = jnp.sum(recv5[...].astype(f32), 0).astype(bf16)
    for dz in (4, 3, 5, 2, 6, 1, 7):
        group_copy(1, sendz, recvz.at[z], line_peer(dz)).start()
    pltpu.make_async_copy(sendz, recvz.at[z], grecv_sem.at[1]).start()
    df_copy.wait_recv()
    for g in range(CHUNKS):
        grad_whole = df_send[chunk(g), :].astype(f32) + df_recv[chunk(g), :].astype(f32)
        hat_g = hat[chunk(g), :]
        grad_full = rstd1[chunk(g), :] * (
            grad_whole
            - jnp.mean(grad_whole, -1, keepdims=True)
            - hat_g * jnp.mean(grad_whole * hat_g, -1, keepdims=True)
        )
        grad_full = jnp.where(ch == 0, grad_full, pltpu.roll(grad_full, 64, 1))
        grad_ref[chunk(g), :] = grad_full[:, 0:64].astype(bf16)

    pltpu.make_async_copy(recvz, recvz, grecv_sem.at[1]).wait()
    send6[...] = jnp.sum(recvz[...].astype(f32), 0).astype(bf16)
    for dx, dy in plane:
        _, device = plane_peer(dx, dy)
        group_copy(2, send6, recv6.at[e_me], device).start()
    pltpu.make_async_copy(send6, recv6.at[e_me], grecv_sem.at[2]).start()
    pltpu.make_async_copy(recv6, recv6, grecv_sem.at[2]).wait()
    flat[0:384, :] = recv6[...].reshape(384, LANES).astype(f32)
    for k, g_ref in enumerate((g0_ref, g1_ref, g2_ref, g3_ref, g4_ref, g5_ref)):
        g_ref[...] = get(6, k) * (1.0 / 384)

    swap_drain(0, recv1, early)
    swap_drain(1, recv1, late)
    swap_drain(2, recv2.at[0], ten)
    swap_drain(3, recv3, ten)
    swap_drain(4, recv4, head)
    swap_drain(5, recv4, tail)
    pltpu.make_async_copy(recv5.at[pl.ds(0, 15)], recv5.at[pl.ds(0, 15)], gsend_sem.at[0]).wait()
    pltpu.make_async_copy(recvz.at[pl.ds(0, 7)], recvz.at[pl.ds(0, 7)], gsend_sem.at[1]).wait()
    pltpu.make_async_copy(recv6.at[pl.ds(0, 15)], recv6.at[pl.ds(0, 15)], gsend_sem.at[2]).wait()
    for copy in copies + [right_copy, mixed_copy, dr_copy, df_copy]:
        copy.wait_send()


def write_kernel(*refs):
    copies = [pltpu.make_async_copy(refs[n], refs[8 + n], refs[16].at[n]) for n in range(8)]
    for copy in copies:
        copy.start()
    for copy in copies:
        copy.wait()


def on_device(pair, cotangent, w_gate_a, w_proj_a, w_gate_b, w_proj_b, w_gate_out, w_out):
    rows, cols, channels = pair.shape
    whole = pl.BlockSpec(memory_space=pltpu.VMEM)
    weights = [w.T for w in (w_gate_a, w_proj_a, w_gate_b, w_proj_b, w_gate_out, w_out)]
    vm = pltpu.VMEM
    big, small = (64, 9, 2, 128), (64, 5, 2, 128)
    sixteen, eight, one = (16, 24, 128), (8, 24, 128), (24, 128)
    shapes = [jax.ShapeDtypeStruct((PAIRS, 64), bf16)] * 2 + [jax.ShapeDtypeStruct((64, 128), f32)] * 6
    outs = pl.pallas_call(
        kernel,
        out_shape=shapes,
        in_specs=[pl.BlockSpec(memory_space=pl.ANY)] * 8,
        out_specs=[whole] * 8,
        scratch_shapes=[
            vm((PAIRS, 128), bf16), vm((PAIRS, 64), bf16), vm((384, 128), bf16),
            pltpu.SemaphoreType.DMA((10,)),
            vm((PAIRS, 128), bf16),
            vm((PAIRS, 128), f32),
            vm((PAIRS, 1), f32),
            vm((CHUNKS, 256, 128), f32),
            vm((PAIRS, 128), f32),
            vm(big, bf16), vm(big, bf16),
            vm(small, bf16), vm((2,) + small, bf16),
            vm(small, bf16), vm(small, bf16),
            vm(big, bf16), vm(big, bf16),
            vm(sixteen, bf16), vm(sixteen, bf16),
            vm(one, bf16), vm(eight, bf16),
            vm(one, bf16), vm(sixteen, bf16),
            vm((192, 384), bf16), vm((384, 384), bf16),
            vm((384, 384), bf16), vm((192, 384), bf16),
            vm((PAIRS, 128), bf16), vm((PAIRS, 128), bf16),
            vm((64, 128), bf16), vm((64, 128), bf16),
            vm((64, PAIRS), bf16), vm((64, PAIRS), bf16),
            vm((128, PAIRS), f32),
            vm((64, PAIRS), bf16), vm((64, PAIRS), bf16),
            vm((128, PAIRS), bf16),
            vm((256, PAIRS), bf16),
            pltpu.SemaphoreType.DMA((6,)),
            pltpu.SemaphoreType.DMA((6,)),
            pltpu.SemaphoreType.DMA((8,)),
            pltpu.SemaphoreType.DMA((8,)),
            pltpu.SemaphoreType.DMA((3,)),
            pltpu.SemaphoreType.DMA((3,)),
        ],
        compiler_params=pltpu.CompilerParams(
            collective_id=0, has_side_effects=True, vmem_limit_bytes=40 << 20
        ),
    )(pair.reshape(PAIRS, channels), cotangent.reshape(PAIRS, 64), *weights)
    outs = pl.pallas_call(
        write_kernel,
        out_shape=shapes,
        in_specs=[whole] * 8,
        out_specs=[pl.BlockSpec(memory_space=pl.ANY)] * 8,
        scratch_shapes=[pltpu.SemaphoreType.DMA((8,))],
    )(*outs)
    updated, grad_pair, ga, pa, gb, pb, go, out = outs
    return (
        updated.reshape(rows, cols, 64),
        grad_pair.reshape(rows, cols, 64),
        ga.T,
        pa.T,
        gb.T,
        pb.T,
        go.T,
        out.T,
    )


def solution(mesh):
    wide = P("row", "col", "ch")
    narrow = P(None, "ch")
    return jax.shard_map(
        on_device,
        mesh=mesh,
        in_specs=(P("row", "col", None), wide) + (narrow,) * 6,
        out_specs=(wide, wide) + (narrow,) * 6,
        check_vma=False,
    )
```

```python
import jax
import jax.numpy as jnp
from jax import lax
from jax.experimental import pallas as pl
from jax.experimental.pallas import tpu as pltpu
from jax.sharding import PartitionSpec as P

MESH = pl.DeviceIdType.MESH
epsilon = 1e-05
f32, bf16 = jnp.float32, jnp.bfloat16
PAIRS, CHUNKS, LANES = 1152, 9, 128


def nn(a, b):
    return lax.dot_general(a, b, (((1,), (0,)), ((), ())), preferred_element_type=f32)


def nt(a, b):
    return lax.dot_general(a, b, (((1,), (1,)), ((), ())), preferred_element_type=f32)


def tn(a, b):
    return lax.dot_general(a, b, (((0,), (0,)), ((), ())), preferred_element_type=f32)


def sigmoid(x):
    return 1.0 / (1.0 + jnp.exp(-x))


def block_transpose(x):
    groups = x.shape[0] // 8
    x = x.reshape(groups, 8, 384)
    row = lax.broadcasted_iota(jnp.int32, x.shape, 1)
    part = lax.broadcasted_iota(jnp.int32, x.shape, 2) // 48
    for bit in (1, 2, 4):
        low = (row & bit) == 0
        same = low == ((part & bit) == 0)
        up = pltpu.roll(pltpu.roll(x, bit, 1), 384 - 48 * bit, 2)
        down = pltpu.roll(pltpu.roll(x, 8 - bit, 1), 48 * bit, 2)
        x = jnp.where(same, x, jnp.where(low, down, up))
    return x.reshape(groups * 8, 384)


def kernel(
    pair_hbm, cot_hbm, wga_hbm, wpa_hbm, wgb_hbm, wpb_hbm, wgo_hbm, wo_hbm,
    updated_ref, grad_ref, g0_ref, g1_ref, g2_ref, g3_ref, g4_ref, g5_ref,
    pair_ref, cot_ref, weights, load_sem, normed, hat, rstd1, acts, flat,
    send1, recv1, send2, recv2, send3, recv3, send4, recv4,
    send5, recv5, sendz, recvz, send6, recv6,
    left, right, dr_send, dr_recv, df_send, df_recv,
    wgo_other, wo_other, cot_t, cot_other, gate_out, dproj, dgate, mixn, dfour,
    send_sem, recv_sem, psend_sem, precv_sem, gsend_sem, grecv_sem,
):
    loads = [
        pltpu.make_async_copy(src, weights.at[pl.ds(64 * n, 64), :], load_sem.at[n])
        for n, src in enumerate((wga_hbm, wpa_hbm, wgb_hbm, wpb_hbm, wgo_hbm, wo_hbm))
    ]
    loads += [
        pltpu.make_async_copy(pair_hbm.at[rows, :], pair_ref.at[rows, :], load_sem.at[6 + n])
        for n, rows in enumerate(pl.ds(384 * k, 384) for k in range(3))
    ]
    loads.append(pltpu.make_async_copy(cot_hbm, cot_ref, load_sem.at[9]))
    for load in loads:
        load.start()
    wgo_ref, wo_ref = weights.at[pl.ds(256, 64), :], weights.at[pl.ds(320, 64), :]

    row, col, ch = lax.axis_index("row"), lax.axis_index("col"), lax.axis_index("ch")
    x, y, z = row // 4, col // 2, (col % 2) * 4 + row % 4
    slot = (row % 8) * 8 + col
    half = row // 8
    own = half == ch
    other = (row, col, 1 - ch)

    def peer(t):
        return (8 * ch + t // 8, t % 8, half)

    barrier = pltpu.get_barrier_semaphore()
    pl.semaphore_signal(barrier, inc=1, device_id=other, device_id_type=MESH)

    def each_peer(act):
        @pl.loop(0, 8)
        def _(k):
            away = (4 + (1 - 2 * (k % 2)) * ((k + 1) // 2)) % 8
            z_to = (z + away) % 8
            for dy in (2, 1, 3, 0):
                for dx in (1, 0):
                    t = ((x + dx) % 2) * 32 + (z_to % 4) * 8 + ((y + dy) % 4) * 2 + z_to // 4
                    if dy == 0 and dx == 0:

                        @pl.when(k < 7)
                        def _():
                            act(t)
                    else:
                        act(t)

    plane = [(2, 2), (2, 1), (2, 3), (1, 2), (3, 2), (2, 0), (0, 2), (1, 1), (1, 3), (3, 1), (3, 3)]
    plane += [(1, 0), (3, 0), (0, 1), (0, 3)]

    def plane_peer(dx, dy):
        x_to, y_to = (x + dx) % 4, (y + dy) % 4
        return x_to * 4 + y_to, (x_to * 4 + row % 4, y_to * 2 + col % 2, ch)

    def line_peer(dz):
        z_to = (z + dz) % 8
        return (x * 4 + z_to % 4, y * 2 + z_to // 4, ch)

    def greet(device):
        pl.semaphore_signal(barrier, inc=1, device_id=device, device_id_type=MESH)

    each_peer(lambda t: greet(peer(t)))

    @pl.when(jnp.logical_not(own))
    def _():
        greet(peer(slot))

    for dx, dy in plane:
        greet(plane_peer(dx, dy)[1])
    for dz in (4, 3, 5, 2, 6, 1, 7):
        greet(line_peer(dz))

    def swap_start(n, src, dst, part):
        def copy(t):
            return pltpu.make_async_remote_copy(
                src_ref=src.at[t, part],
                dst_ref=dst.at[slot, part],
                send_sem=send_sem.at[n],
                recv_sem=recv_sem.at[n],
                device_id=peer(t),
                device_id_type=MESH,
            )

        each_peer(lambda t: copy(t).start())

        @pl.when(own)
        def _():
            pltpu.make_async_copy(src.at[slot, part], dst.at[slot, part], recv_sem.at[n]).start()

        @pl.when(jnp.logical_not(own))
        def _():
            copy(slot).start()

    def swap_wait(n, dst, part):
        whole = dst.at[:, part]
        pltpu.make_async_copy(whole, whole, recv_sem.at[n]).wait()

    def swap_drain(n, dst, part):
        @pl.when(own)
        def _():
            some = dst.at[pl.ds(0, 63), part]
            pltpu.make_async_copy(some, some, send_sem.at[n]).wait()

        @pl.when(jnp.logical_not(own))
        def _():
            whole = dst.at[:, part]
            pltpu.make_async_copy(whole, whole, send_sem.at[n]).wait()

    def group_copy(n, src, dst, device):
        return pltpu.make_async_remote_copy(
            src_ref=src,
            dst_ref=dst,
            send_sem=gsend_sem.at[n],
            recv_sem=grecv_sem.at[n],
            device_id=device,
            device_id_type=MESH,
        )

    def partner(n, src, dst):
        return pltpu.make_async_remote_copy(
            src_ref=src,
            dst_ref=dst,
            send_sem=psend_sem.at[n],
            recv_sem=precv_sem.at[n],
            device_id=other,
            device_id_type=MESH,
        )

    def put(t_rows, g, value):
        flat[pl.ds(g, 64, stride=t_rows), :] = value

    def get(t_rows, g):
        return flat[pl.ds(g, 64, stride=t_rows), :]

    def pack(t_rows, dst):
        dst[...] = flat[0 : 64 * t_rows, :].astype(bf16).reshape(dst.shape)

    ten, early, late = pl.ds(0, 5), pl.ds(0, 5), pl.ds(5, 4)
    head, tail = pl.ds(0, 4), pl.ds(4, 5)

    def unpack(t_rows, src):
        flat[0 : 64 * t_rows, :] = src[...].reshape(64 * t_rows, LANES).astype(f32)

    def grid_of(t_rows, first):
        tiles = [None] * 24
        for gg in range(3):
            x = jnp.concatenate([get(t_rows, first + 3 * gg + q) for q in range(3)], axis=1)
            x = block_transpose(x)
            for r in range(8):
                tiles[r * 3 + gg] = x[8 * r : 8 * r + 8]
        return jnp.concatenate(tiles, axis=0)

    def put_grid(t_rows, first, grid):
        for gg in range(3):
            x = jnp.concatenate([grid[8 * (3 * r + gg) : 8 * (3 * r + gg) + 8] for r in range(8)], axis=0)
            x = block_transpose(x)
            for q in range(3):
                put(t_rows, first + 3 * gg + q, x[:, LANES * q : LANES * q + LANES])

    def chunk(g):
        return pl.ds(g * LANES, LANES)

    for load in loads[0:6]:
        load.wait()
    w_four = weights[0:256, :]
    for g in range(CHUNKS):
        if g % 3 == 0:
            loads[6 + g // 3].wait()
        values = pair_ref[chunk(g), :].astype(f32)
        centred = values - jnp.mean(values, -1, keepdims=True)
        spread = jnp.mean(centred * centred, -1, keepdims=True)
        inverse = lax.rsqrt(spread + epsilon)
        hat_g = centred * inverse
        hat[chunk(g), :] = hat_g
        rstd1[chunk(g), :] = inverse
        normed_g = hat_g.astype(bf16)
        normed[chunk(g), :] = normed_g
        projected = nt(w_four, normed_g)
        gate_a = sigmoid(projected[0:64])
        proj_a = projected[64:128]
        gate_b = sigmoid(projected[128:192])
        proj_b = projected[192:256]
        acts[g, 0:64, :] = gate_a
        acts[g, 64:128, :] = proj_a
        acts[g, 128:192, :] = gate_b
        acts[g, 192:256, :] = proj_b
        put(18, g, gate_b * proj_b)
        put(18, 9 + g, gate_a * proj_a)
    pack(18, send1)

    @pl.when(own)
    def _():
        pl.semaphore_wait(barrier, 86)

    @pl.when(jnp.logical_not(own))
    def _():
        pl.semaphore_wait(barrier, 87)

    swap_start(0, send1, recv1, early)
    swap_start(1, send1, recv1, late)

    copies = [partner(0, wgo_ref, wgo_other), partner(1, wo_ref, wo_other)]
    for copy in copies:
        copy.start()
    loads[9].wait()
    for g in range(CHUNKS):
        cot_t[:, chunk(g)] = jnp.transpose(cot_ref[chunk(g), :].astype(f32)).astype(bf16)
    copies.append(partner(2, cot_t, cot_other))
    copies[2].start()
    for copy in copies:
        copy.wait_recv()
    wgo = jnp.concatenate([wgo_ref[...], wgo_other[...]], axis=0)
    for g in range(CHUNKS):
        gate_out[:, chunk(g)] = sigmoid(nt(wgo, normed[chunk(g), :]))
    mine_rows = pl.ds(pl.multiple_of(ch * 64, 64), 64)
    wo_cols = jnp.concatenate([wo_ref[...], wo_other[...]], axis=0).astype(f32)
    wo_t = jnp.where(ch == 0, wo_cols, pltpu.roll(wo_cols, 64, 1))
    wo = jnp.transpose(wo_t).astype(bf16)
    wo_t = wo_t.astype(bf16)

    swap_wait(0, recv1, early)
    mine_half = pl.ds(pl.multiple_of(ch * 192, 192), 192)
    other_half = pl.ds(pl.multiple_of((1 - ch) * 192, 192), 192)
    flat[0:640, :] = recv1[:, early].reshape(640, LANES).astype(f32)
    right[mine_half, :] = grid_of(10, 0).astype(bf16)
    right_copy = partner(3, right.at[mine_half, :], right.at[mine_half, :])
    right_copy.start()
    swap_wait(1, recv1, late)
    unpack(18, recv1)
    left[...] = grid_of(18, 9).astype(bf16)
    right_copy.wait_recv()
    put_grid(10, 0, nt(left[...], right[...]))
    pack(10, send2)
    swap_start(2, send2, recv2.at[0], ten)
    swap_wait(2, recv2.at[0], ten)
    mixed_copy = partner(4, recv2.at[0], recv2.at[1])
    mixed_copy.start()
    mixed_copy.wait_recv()

    flat_two = []
    unpack(10, recv2.at[0])
    first = [get(10, g) for g in range(CHUNKS)]
    for g in range(CHUNKS):
        mixn_f = first[g]
        dfour[0:64, chunk(g)] = mixn_f.astype(bf16)
    unpack(10, recv2.at[1])
    for g in range(CHUNKS):
        mixed = jnp.concatenate([dfour[0:64, chunk(g)].astype(f32), get(10, g)], axis=0)
        mean = jnp.mean(mixed, 0, keepdims=True)
        var = jnp.mean(mixed * mixed, 0, keepdims=True) - mean * mean
        inverse = lax.rsqrt(var + epsilon)
        mixed_hat = (mixed - mean) * inverse
        mixed_norm = mixed_hat.astype(bf16)
        mixn[:, chunk(g)] = mixed_norm
        gate = gate_out[:, chunk(g)]
        proj_out = nn(wo_t, mixed_norm)
        upstream = jnp.concatenate([cot_t[:, chunk(g)], cot_other[:, chunk(g)]], axis=0).astype(f32)
        d_proj = (upstream * gate).astype(bf16)
        d_norm = nn(wo, d_proj)
        d_mean = jnp.mean(d_norm, 0, keepdims=True)
        d_cross = jnp.mean(d_norm * mixed_hat, 0, keepdims=True)
        d_mixed = inverse[:, :] * (d_norm[0:64] - d_mean - mixed_hat[0:64] * d_cross)
        acts_flat = d_mixed
        dmix_rows = acts_flat
        flat_two.append(dmix_rows)
        dproj[:, chunk(g)] = d_proj[0:64]
        gate_mine, proj_mine = gate[0:64], proj_out[0:64]
        dgate[:, chunk(g)] = (upstream[0:64] * proj_mine * gate_mine * (1.0 - gate_mine)).astype(bf16)
        updated_ref[chunk(g), :] = jnp.transpose(gate_mine * proj_mine).astype(bf16)
    for g in range(CHUNKS):
        put(10, g, flat_two[g])
    pack(10, send3)
    swap_start(3, send3, recv3, ten)
    head_gate = nn(dgate[...], normed[...])
    head_out = nt(dproj[...], mixn[...])

    swap_wait(3, recv3, ten)
    unpack(10, recv3)
    d_grid = grid_of(10, 0).astype(bf16)
    d_right = tn(d_grid, left[...])
    dr_send[...] = d_right.astype(bf16)
    dr_copy = partner(5, dr_send.at[other_half, :], dr_recv)
    dr_copy.start()
    put_grid(18, 0, nn(d_grid, right[...]))
    send4[:, head] = flat[...].astype(bf16).reshape(send4.shape)[:, 0:4]
    swap_start(4, send4, recv4, head)
    dr_copy.wait_recv()
    put_grid(18, 9, dr_send[mine_half, :].astype(f32) + dr_recv[...].astype(f32))
    send4[:, tail] = flat[...].astype(bf16).reshape(send4.shape)[:, 4:9]
    swap_start(5, send4, recv4, tail)
    swap_wait(4, recv4, head)
    swap_wait(5, recv4, tail)
    unpack(18, recv4)
    for g in range(CHUNKS):
        d_left, d_right_g = get(18, g), get(18, 9 + g)
        gate_a, proj_a = acts[g, 0:64, :], acts[g, 64:128, :]
        gate_b, proj_b = acts[g, 128:192, :], acts[g, 192:256, :]
        dfour[0:64, chunk(g)] = (d_left * proj_a * gate_a * (1.0 - gate_a)).astype(bf16)
        dfour[64:128, chunk(g)] = (d_left * gate_a).astype(bf16)
        dfour[128:192, chunk(g)] = (d_right_g * proj_b * gate_b * (1.0 - gate_b)).astype(bf16)
        dfour[192:256, chunk(g)] = (d_right_g * gate_b).astype(bf16)
    edge = nn(dfour[...], normed[...])

    for k in range(4):
        put(6, k, edge[64 * k : 64 * k + 64])
    put(6, 4, head_gate)
    put(6, 5, jnp.where(ch == 0, head_out, pltpu.roll(head_out, 64, 1)))
    pack(6, send5)
    e_me, _ = plane_peer(0, 0)
    for dx, dy in plane:
        e, device = plane_peer(dx, dy)
        group_copy(0, send5.at[e], recv5.at[e_me], device).start()
    pltpu.make_async_copy(send5.at[e_me], recv5.at[e_me], grecv_sem.at[0]).start()
    for g in range(CHUNKS):
        d_flat = tn(dfour[:, chunk(g)], w_four) + tn(dgate[:, chunk(g)], wgo_ref[...])
        df_send[chunk(g), :] = d_flat.astype(bf16)
    df_copy = partner(6, df_send, df_recv)
    df_copy.start()
    pltpu.make_async_copy(recv5, recv5, grecv_sem.at[0]).wait()
    sendz[...] = jnp.sum(recv5[...].astype(f32), 0).astype(bf16)
    for dz in (4, 3, 5, 2, 6, 1, 7):
        group_copy(1, sendz, recvz.at[z], line_peer(dz)).start()
    pltpu.make_async_copy(sendz, recvz.at[z], grecv_sem.at[1]).start()
    df_copy.wait_recv()
    for g in range(CHUNKS):
        grad_whole = df_send[chunk(g), :].astype(f32) + df_recv[chunk(g), :].astype(f32)
        hat_g = hat[chunk(g), :]
        grad_full = rstd1[chunk(g), :] * (
            grad_whole
            - jnp.mean(grad_whole, -1, keepdims=True)
            - hat_g * jnp.mean(grad_whole * hat_g, -1, keepdims=True)
        )
        grad_full = jnp.where(ch == 0, grad_full, pltpu.roll(grad_full, 64, 1))
        grad_ref[chunk(g), :] = grad_full[:, 0:64].astype(bf16)

    pltpu.make_async_copy(recvz, recvz, grecv_sem.at[1]).wait()
    send6[...] = jnp.sum(recvz[...].astype(f32), 0).astype(bf16)
    for dx, dy in plane:
        _, device = plane_peer(dx, dy)
        group_copy(2, send6, recv6.at[e_me], device).start()
    pltpu.make_async_copy(send6, recv6.at[e_me], grecv_sem.at[2]).start()
    pltpu.make_async_copy(recv6, recv6, grecv_sem.at[2]).wait()
    flat[0:384, :] = recv6[...].reshape(384, LANES).astype(f32)
    for k, g_ref in enumerate((g0_ref, g1_ref, g2_ref, g3_ref, g4_ref, g5_ref)):
        g_ref[...] = get(6, k) * (1.0 / 384)

    swap_drain(0, recv1, early)
    swap_drain(1, recv1, late)
    swap_drain(2, recv2.at[0], ten)
    swap_drain(3, recv3, ten)
    swap_drain(4, recv4, head)
    swap_drain(5, recv4, tail)
    pltpu.make_async_copy(recv5.at[pl.ds(0, 15)], recv5.at[pl.ds(0, 15)], gsend_sem.at[0]).wait()
    pltpu.make_async_copy(recvz.at[pl.ds(0, 7)], recvz.at[pl.ds(0, 7)], gsend_sem.at[1]).wait()
    pltpu.make_async_copy(recv6.at[pl.ds(0, 15)], recv6.at[pl.ds(0, 15)], gsend_sem.at[2]).wait()
    for copy in copies + [right_copy, mixed_copy, dr_copy, df_copy]:
        copy.wait_send()


def write_kernel(*refs):
    copies = [pltpu.make_async_copy(refs[n], refs[8 + n], refs[16].at[n]) for n in range(8)]
    for copy in copies:
        copy.start()
    for copy in copies:
        copy.wait()


def on_device(pair, cotangent, w_gate_a, w_proj_a, w_gate_b, w_proj_b, w_gate_out, w_out):
    rows, cols, channels = pair.shape
    whole = pl.BlockSpec(memory_space=pltpu.VMEM)
    weights = [w.T for w in (w_gate_a, w_proj_a, w_gate_b, w_proj_b, w_gate_out, w_out)]
    vm = pltpu.VMEM
    big, small = (64, 9, 2, 128), (64, 5, 2, 128)
    sixteen, eight, one = (16, 24, 128), (8, 24, 128), (24, 128)
    shapes = [jax.ShapeDtypeStruct((PAIRS, 64), bf16)] * 2 + [jax.ShapeDtypeStruct((64, 128), f32)] * 6
    outs = pl.pallas_call(
        kernel,
        out_shape=shapes,
        in_specs=[pl.BlockSpec(memory_space=pltpu.HBM)] * 8,
        out_specs=[whole] * 8,
        scratch_shapes=[
            vm((PAIRS, 128), bf16), vm((PAIRS, 64), bf16), vm((384, 128), bf16),
            pltpu.SemaphoreType.DMA((10,)),
            vm((PAIRS, 128), bf16),
            vm((PAIRS, 128), f32),
            vm((PAIRS, 1), f32),
            vm((CHUNKS, 256, 128), f32),
            vm((PAIRS, 128), f32),
            vm(big, bf16), vm(big, bf16),
            vm(small, bf16), vm((2,) + small, bf16),
            vm(small, bf16), vm(small, bf16),
            vm(big, bf16), vm(big, bf16),
            vm(sixteen, bf16), vm(sixteen, bf16),
            vm(one, bf16), vm(eight, bf16),
            vm(one, bf16), vm(sixteen, bf16),
            vm((192, 384), bf16), vm((384, 384), bf16),
            vm((384, 384), bf16), vm((192, 384), bf16),
            vm((PAIRS, 128), bf16), vm((PAIRS, 128), bf16),
            vm((64, 128), bf16), vm((64, 128), bf16),
            vm((64, PAIRS), bf16), vm((64, PAIRS), bf16),
            vm((128, PAIRS), f32),
            vm((64, PAIRS), bf16), vm((64, PAIRS), bf16),
            vm((128, PAIRS), bf16),
            vm((256, PAIRS), bf16),
            pltpu.SemaphoreType.DMA((6,)),
            pltpu.SemaphoreType.DMA((6,)),
            pltpu.SemaphoreType.DMA((8,)),
            pltpu.SemaphoreType.DMA((8,)),
            pltpu.SemaphoreType.DMA((3,)),
            pltpu.SemaphoreType.DMA((3,)),
        ],
        compiler_params=pltpu.CompilerParams(
            collective_id=0, has_side_effects=True, vmem_limit_bytes=40 << 20
        ),
    )(*[pltpu.with_memory_space_constraint(a, pltpu.HBM) for a in (pair.reshape(PAIRS, channels), cotangent.reshape(PAIRS, 64), *weights)])
    outs = pl.pallas_call(
        write_kernel,
        out_shape=shapes,
        in_specs=[whole] * 8,
        out_specs=[pl.BlockSpec(memory_space=pltpu.HBM)] * 8,
        scratch_shapes=[pltpu.SemaphoreType.DMA((8,))],
        compiler_params=pltpu.CompilerParams(vmem_limit_bytes=4 << 20),
    )(*outs)
    updated, grad_pair, ga, pa, gb, pb, go, out = outs
    return (
        updated.reshape(rows, cols, 64),
        grad_pair.reshape(rows, cols, 64),
        ga.T,
        pa.T,
        gb.T,
        pb.T,
        go.T,
        out.T,
    )


def solution(mesh):
    wide = P("row", "col", "ch")
    narrow = P(None, "ch")
    return jax.shard_map(
        on_device,
        mesh=mesh,
        in_specs=(P("row", "col", None), wide) + (narrow,) * 6,
        out_specs=(wide, wide) + (narrow,) * 6,
        check_vma=False,
    )
```

```python
import jax
import jax.numpy as jnp
from jax import lax
from jax.experimental import pallas as pl
from jax.experimental.pallas import tpu as pltpu
from jax.sharding import PartitionSpec as P

LOGICAL = pl.DeviceIdType.LOGICAL
epsilon = 1e-05
f32, bf16 = jnp.float32, jnp.bfloat16
PAIRS, CHUNKS, LANES = 1152, 9, 128


def nn(a, b):
    return lax.dot_general(a, b, (((1,), (0,)), ((), ())), preferred_element_type=f32)


def nt(a, b):
    return lax.dot_general(a, b, (((1,), (1,)), ((), ())), preferred_element_type=f32)


def tn(a, b):
    return lax.dot_general(a, b, (((0,), (0,)), ((), ())), preferred_element_type=f32)


def sigmoid(x):
    return 1.0 / (1.0 + jnp.exp(-x))


def hops(d):
    return min(d[0], 8 - d[0]) + min(d[1], 4 - d[1]) + d[2]


FAR_FIRST = sorted(
    [(dz, dy, dx) for dz in range(8) for dy in range(4) for dx in range(2) if dz + dy + dx],
    key=lambda d: -hops(d),
)


def block_transpose(x):
    groups = x.shape[0] // 8
    x = x.reshape(groups, 8, 384)
    row = lax.broadcasted_iota(jnp.int32, x.shape, 1)
    part = lax.broadcasted_iota(jnp.int32, x.shape, 2) // 48
    for bit in (1, 2, 4):
        low = (row & bit) == 0
        same = low == ((part & bit) == 0)
        up = pltpu.roll(pltpu.roll(x, bit, 1), 384 - 48 * bit, 2)
        down = pltpu.roll(pltpu.roll(x, 8 - bit, 1), 48 * bit, 2)
        x = jnp.where(same, x, jnp.where(low, down, up))
    return x.reshape(groups * 8, 384)


def kernel(
    pair_hbm, cot_hbm, wga_hbm, wpa_hbm, wgb_hbm, wpb_hbm, wgo_hbm, wo_hbm,
    updated_ref, grad_ref, g0_ref, g1_ref, g2_ref, g3_ref, g4_ref, g5_ref,
    pair_ref, cot_ref, weights, load_sem, normed, hat, rstd1, acts, flat_a, flat_b, flat_c,
    send1a, recv1a, send1b, recv1b, send2, recv2, send3, recv3, send4a, recv4a, send4b, recv4b,
    send5, recv5, sendz, recvz, send6, recv6,
    left, right, dgrid_t, dr_send, dr_recv, df_send, df_recv,
    wgo_other, wo_other, cot_t, cot_other, gate_out, proj_mine, dproj, dgate, mixn, dfour,
    send_sem, recv_sem, psend_sem, precv_sem, gsend_sem, grecv_sem,
):
    loads = [
        pltpu.make_async_copy(src, weights.at[pl.ds(64 * n, 64), :], load_sem.at[n])
        for n, src in enumerate((wga_hbm, wpa_hbm, wgb_hbm, wpb_hbm, wgo_hbm, wo_hbm))
    ]
    loads += [
        pltpu.make_async_copy(pair_hbm.at[rows, :], pair_ref.at[rows, :], load_sem.at[6 + n])
        for n, rows in enumerate(pl.ds(384 * k, 384) for k in range(3))
    ]
    loads.append(pltpu.make_async_copy(cot_hbm, cot_ref, load_sem.at[9]))
    for load in loads:
        load.start()
    wgo_ref, wo_ref = weights.at[pl.ds(256, 64), :], weights.at[pl.ds(320, 64), :]

    row, col, ch = lax.axis_index("row"), lax.axis_index("col"), lax.axis_index("ch")
    x, y, z = row // 4, col // 2, (col % 2) * 4 + row % 4
    slot = (row % 8) * 8 + col
    half = row // 8
    own = half == ch
    other = row * 16 + col * 2 + 1 - ch

    slot_z = [((z + dz) % 8 % 4) * 8 + (z + dz) % 8 // 4 for dz in range(8)]
    slot_y = [((y + dy) % 4) * 2 for dy in range(4)]
    slot_x = [((x + dx) % 2) * 32 for dx in range(2)]
    base = 128 * ch + half

    def peer(t):
        return base + 2 * t

    barrier = pltpu.get_barrier_semaphore()
    pl.semaphore_signal(barrier, inc=1, device_id=other, device_id_type=LOGICAL)

    def each_peer(act):
        for dz, dy, dx in FAR_FIRST:
            act(slot_z[dz] + slot_y[dy] + slot_x[dx])

    plane = [(2, 2), (2, 1), (2, 3), (1, 2), (3, 2), (2, 0), (0, 2), (1, 1), (1, 3), (3, 1), (3, 3)]
    plane += [(1, 0), (3, 0), (0, 1), (0, 3)]

    def plane_peer(dx, dy):
        x_to, y_to = (x + dx) % 4, (y + dy) % 4
        return x_to * 4 + y_to, (x_to * 4 + row % 4) * 16 + (y_to * 2 + col % 2) * 2 + ch

    def line_peer(dz):
        z_to = (z + dz) % 8
        return (x * 4 + z_to % 4) * 16 + (y * 2 + z_to // 4) * 2 + ch

    def greet(device):
        pl.semaphore_signal(barrier, inc=1, device_id=device, device_id_type=LOGICAL)

    each_peer(lambda t: greet(peer(t)))

    @pl.when(jnp.logical_not(own))
    def _():
        greet(peer(slot))

    for dx, dy in plane:
        greet(plane_peer(dx, dy)[1])
    for dz in (4, 3, 5, 2, 6, 1, 7):
        greet(line_peer(dz))

    def swap_start(n, src, dst):
        def copy(t):
            return pltpu.make_async_remote_copy(
                src_ref=src.at[t],
                dst_ref=dst.at[slot],
                send_sem=send_sem.at[n],
                recv_sem=recv_sem.at[n],
                device_id=peer(t),
                device_id_type=LOGICAL,
            )

        each_peer(lambda t: copy(t).start())

        @pl.when(own)
        def _():
            pltpu.make_async_copy(src.at[slot], dst.at[slot], recv_sem.at[n]).start()

        @pl.when(jnp.logical_not(own))
        def _():
            copy(slot).start()

    def swap_wait(n, dst):
        pltpu.make_async_copy(dst, dst, recv_sem.at[n]).wait()

    def swap_drain(n, dst):
        @pl.when(own)
        def _():
            some = dst.at[pl.ds(0, 63)]
            pltpu.make_async_copy(some, some, send_sem.at[n]).wait()

        @pl.when(jnp.logical_not(own))
        def _():
            pltpu.make_async_copy(dst, dst, send_sem.at[n]).wait()

    def group_copy(n, src, dst, device):
        return pltpu.make_async_remote_copy(
            src_ref=src,
            dst_ref=dst,
            send_sem=gsend_sem.at[n],
            recv_sem=grecv_sem.at[n],
            device_id=device,
            device_id_type=LOGICAL,
        )

    def partner(n, src, dst):
        return pltpu.make_async_remote_copy(
            src_ref=src,
            dst_ref=dst,
            send_sem=psend_sem.at[n],
            recv_sem=precv_sem.at[n],
            device_id=other,
            device_id_type=LOGICAL,
        )

    def put(flat, rows, k, value):
        flat[pl.ds(k, 64, stride=rows), :] = value

    def get(flat, rows, k):
        return flat[pl.ds(k, 64, stride=rows), :]

    def pack(flat, rows, dst):
        dst[...] = flat[0 : 64 * rows, :].astype(bf16).reshape(dst.shape)

    def unpack(flat, rows, src):
        flat[0 : 64 * rows, :] = src[...].reshape(64 * rows, LANES).astype(f32)

    def grid_of(row_of):
        tiles = [None] * 24
        for gg in range(3):
            x = jnp.concatenate([row_of(3 * gg + q) for q in range(3)], axis=1)
            x = block_transpose(x)
            for r in range(8):
                tiles[r * 3 + gg] = x[8 * r : 8 * r + 8]
        return jnp.concatenate(tiles, axis=0)

    def put_grid(put_row, grid):
        for gg in range(3):
            x = jnp.concatenate([grid[8 * (3 * r + gg) : 8 * (3 * r + gg) + 8] for r in range(8)], axis=0)
            x = block_transpose(x)
            for q in range(3):
                put_row(3 * gg + q, x[:, LANES * q : LANES * q + LANES])

    def put_left(k, value):
        put(*((flat_a, 10, 9) if k == 0 else (flat_b, 8, k - 1)), value)

    def get_left(k):
        return get(flat_a, 10, 9) if k == 0 else get(flat_b, 8, k - 1)

    def put_d_left(k, value):
        put(*((flat_a, 8, k) if k < 8 else (flat_b, 10, 0)), value)

    def chunk(g):
        return pl.ds(g * LANES, LANES)

    for load in loads[0:6]:
        load.wait()
    w_four = weights[0:256, :]
    for g in range(CHUNKS):
        if g % 3 == 0:
            loads[6 + g // 3].wait()
        values = pair_ref[chunk(g), :].astype(f32)
        centred = values - jnp.mean(values, -1, keepdims=True)
        spread = jnp.mean(centred * centred, -1, keepdims=True)
        inverse = lax.rsqrt(spread + epsilon)
        hat_g = centred * inverse
        hat[chunk(g), :] = hat_g
        rstd1[chunk(g), :] = inverse
        normed_g = hat_g.astype(bf16)
        normed[chunk(g), :] = normed_g
        projected = nt(w_four, normed_g)
        gate_a = sigmoid(projected[0:64])
        proj_a = projected[64:128]
        gate_b = sigmoid(projected[128:192])
        proj_b = projected[192:256]
        acts[g, 0:64, :] = gate_a
        acts[g, 64:128, :] = proj_a
        acts[g, 128:192, :] = gate_b
        acts[g, 192:256, :] = proj_b
        put(flat_a, 10, g, gate_b * proj_b)
        put_left(g, gate_a * proj_a)
    pack(flat_a, 10, send1a)
    pack(flat_b, 8, send1b)
    put(flat_c, 10, 9, jnp.zeros((64, LANES), f32))

    @pl.when(own)
    def _():
        pl.semaphore_wait(barrier, 86)

    @pl.when(jnp.logical_not(own))
    def _():
        pl.semaphore_wait(barrier, 87)

    swap_start(0, send1a, recv1a)
    swap_start(1, send1b, recv1b)

    copies = [partner(0, wgo_ref, wgo_other), partner(1, wo_ref, wo_other)]
    for copy in copies:
        copy.start()
    loads[9].wait()
    for g in range(CHUNKS):
        cot_t[:, chunk(g)] = jnp.transpose(cot_ref[chunk(g), :].astype(f32)).astype(bf16)
    copies.append(partner(2, cot_t, cot_other))
    copies[2].start()
    for copy in copies:
        copy.wait_recv()
    wgo = jnp.concatenate([wgo_ref[...], wgo_other[...]], axis=0)
    for g in range(CHUNKS):
        gate_out[:, chunk(g)] = sigmoid(nt(wgo, normed[chunk(g), :]))
    mine_rows = pl.ds(pl.multiple_of(ch * 64, 64), 64)
    wo_cols = jnp.concatenate([wo_ref[...], wo_other[...]], axis=0).astype(f32)
    wo_t = jnp.where(ch == 0, wo_cols, pltpu.roll(wo_cols, 64, 1))
    wo = jnp.transpose(wo_t).astype(bf16)
    wo_t = wo_t.astype(bf16)

    swap_wait(0, recv1a)
    mine_half = pl.ds(pl.multiple_of(ch * 192, 192), 192)
    other_half = pl.ds(pl.multiple_of((1 - ch) * 192, 192), 192)
    unpack(flat_a, 10, recv1a)
    right[mine_half, :] = grid_of(lambda k: get(flat_a, 10, k)).astype(bf16)
    right_copy = partner(3, right.at[mine_half, :], right.at[mine_half, :])
    right_copy.start()
    swap_wait(1, recv1b)
    unpack(flat_b, 8, recv1b)
    left[...] = grid_of(get_left).astype(bf16)
    right_copy.wait_recv()
    put_grid(lambda k, row: put(flat_c, 10, k, row), nt(left[...], right[...]))
    pack(flat_c, 10, send2)
    swap_start(2, send2, recv2.at[0])
    swap_wait(2, recv2.at[0])
    mixed_copy = partner(4, recv2.at[0], recv2.at[1])
    mixed_copy.start()
    mixed_copy.wait_recv()

    unpack(flat_a, 10, recv2.at[0])
    unpack(flat_b, 10, recv2.at[1])
    for g in range(CHUNKS):
        mixed = jnp.concatenate([get(flat_a, 10, g), get(flat_b, 10, g)], axis=0)
        mean = jnp.mean(mixed, 0, keepdims=True)
        var = jnp.mean(mixed * mixed, 0, keepdims=True) - mean * mean
        inverse = lax.rsqrt(var + epsilon)
        mixed_hat = (mixed - mean) * inverse
        mixed_norm = mixed_hat.astype(bf16)
        mixn[:, chunk(g)] = mixed_norm
        upstream = jnp.concatenate([cot_t[:, chunk(g)], cot_other[:, chunk(g)]], axis=0).astype(f32)
        d_proj = (upstream * gate_out[:, chunk(g)]).astype(bf16)
        dproj[:, chunk(g)] = d_proj[0:64]
        d_norm = nn(wo, d_proj)
        d_mean = jnp.mean(d_norm, 0, keepdims=True)
        d_cross = jnp.mean(d_norm * mixed_hat, 0, keepdims=True)
        put(flat_c, 10, g, inverse * (d_norm[0:64] - d_mean - mixed_hat[0:64] * d_cross))
    pack(flat_c, 10, send3)
    swap_start(3, send3, recv3)
    for g in range(CHUNKS):
        proj_out = nn(wo_t[0:64], mixn[:, chunk(g)])
        gate = gate_out[0:64, chunk(g)]
        upstream = cot_t[:, chunk(g)].astype(f32)
        dgate[:, chunk(g)] = (upstream * proj_out * gate * (1.0 - gate)).astype(bf16)
        updated_ref[chunk(g), :] = jnp.transpose(gate * proj_out).astype(bf16)
    head_gate = nn(dgate[...], normed[...])
    head_out = nt(dproj[...], mixn[...])

    swap_wait(3, recv3)
    unpack(flat_a, 10, recv3)
    d_grid = grid_of(lambda k: get(flat_a, 10, k))
    dgrid_t[...] = jnp.transpose(d_grid).astype(bf16)
    dr_send[...] = nn(dgrid_t[other_half, :], left[...]).astype(bf16)
    dr_copy = partner(5, dr_send, dr_recv)
    dr_copy.start()
    put_grid(put_d_left, nn(d_grid.astype(bf16), right[...]))
    pack(flat_a, 8, send4a)
    swap_start(4, send4a, recv4a)
    d_right = nn(dgrid_t[mine_half, :], left[...])
    dr_copy.wait_recv()
    put_grid(lambda k, row: put(flat_b, 10, 1 + k, row), d_right + dr_recv[...].astype(f32))
    pack(flat_b, 10, send4b)
    swap_start(5, send4b, recv4b)
    swap_wait(4, recv4a)

    def left_terms(g, d_left):
        gate_a, proj_a = acts[g, 0:64, :], acts[g, 64:128, :]
        dfour[0:64, chunk(g)] = (d_left * proj_a * gate_a * (1.0 - gate_a)).astype(bf16)
        dfour[64:128, chunk(g)] = (d_left * gate_a).astype(bf16)

    unpack(flat_a, 8, recv4a)
    for g in range(CHUNKS - 1):
        left_terms(g, get(flat_a, 8, g))
    edge_left = nn(dfour[0:128, 0:1024], normed[0:1024, :])
    swap_wait(5, recv4b)
    unpack(flat_b, 10, recv4b)
    left_terms(8, get(flat_b, 10, 0))
    for g in range(CHUNKS):
        d_right_g = get(flat_b, 10, 1 + g)
        gate_b, proj_b = acts[g, 128:192, :], acts[g, 192:256, :]
        dfour[128:192, chunk(g)] = (d_right_g * proj_b * gate_b * (1.0 - gate_b)).astype(bf16)
        dfour[192:256, chunk(g)] = (d_right_g * gate_b).astype(bf16)
    edge_left += nn(dfour[0:128, 1024:1152], normed[1024:1152, :])
    edge_right = nn(dfour[128:256, :], normed[...])

    for k in range(2):
        put(flat_c, 6, k, edge_left[64 * k : 64 * k + 64])
        put(flat_c, 6, 2 + k, edge_right[64 * k : 64 * k + 64])
    put(flat_c, 6, 4, head_gate)
    put(flat_c, 6, 5, jnp.where(ch == 0, head_out, pltpu.roll(head_out, 64, 1)))
    pack(flat_c, 6, send5)
    e_me, _ = plane_peer(0, 0)
    for dx, dy in plane:
        e, device = plane_peer(dx, dy)
        group_copy(0, send5.at[e], recv5.at[e_me], device).start()
    pltpu.make_async_copy(send5.at[e_me], recv5.at[e_me], grecv_sem.at[0]).start()
    for g in range(CHUNKS):
        d_flat = tn(dfour[:, chunk(g)], w_four) + tn(dgate[:, chunk(g)], wgo_ref[...])
        df_send[chunk(g), :] = d_flat.astype(bf16)
    df_copy = partner(6, df_send, df_recv)
    df_copy.start()
    pltpu.make_async_copy(recv5, recv5, grecv_sem.at[0]).wait()
    sendz[...] = jnp.sum(recv5[...].astype(f32), 0).astype(bf16)
    for dz in (4, 3, 5, 2, 6, 1, 7):
        group_copy(1, sendz, recvz.at[z], line_peer(dz)).start()
    pltpu.make_async_copy(sendz, recvz.at[z], grecv_sem.at[1]).start()
    df_copy.wait_recv()
    for g in range(CHUNKS):
        grad_whole = df_send[chunk(g), :].astype(f32) + df_recv[chunk(g), :].astype(f32)
        hat_g = hat[chunk(g), :]
        grad_full = rstd1[chunk(g), :] * (
            grad_whole
            - jnp.mean(grad_whole, -1, keepdims=True)
            - hat_g * jnp.mean(grad_whole * hat_g, -1, keepdims=True)
        )
        grad_full = jnp.where(ch == 0, grad_full, pltpu.roll(grad_full, 64, 1))
        grad_ref[chunk(g), :] = grad_full[:, 0:64].astype(bf16)

    pltpu.make_async_copy(recvz, recvz, grecv_sem.at[1]).wait()
    send6[...] = jnp.sum(recvz[...].astype(f32), 0).astype(bf16)
    for dx, dy in plane:
        _, device = plane_peer(dx, dy)
        group_copy(2, send6, recv6.at[e_me], device).start()
    pltpu.make_async_copy(send6, recv6.at[e_me], grecv_sem.at[2]).start()
    pltpu.make_async_copy(recv6, recv6, grecv_sem.at[2]).wait()
    unpack(flat_c, 6, recv6)
    for k, g_ref in enumerate((g0_ref, g1_ref, g2_ref, g3_ref, g4_ref, g5_ref)):
        g_ref[...] = get(flat_c, 6, k) * (1.0 / 384)

    for n, dst in enumerate((recv1a, recv1b, recv2.at[0], recv3, recv4a, recv4b)):
        swap_drain(n, dst)
    pltpu.make_async_copy(recv5.at[pl.ds(0, 15)], recv5.at[pl.ds(0, 15)], gsend_sem.at[0]).wait()
    pltpu.make_async_copy(recvz.at[pl.ds(0, 7)], recvz.at[pl.ds(0, 7)], gsend_sem.at[1]).wait()
    pltpu.make_async_copy(recv6.at[pl.ds(0, 15)], recv6.at[pl.ds(0, 15)], gsend_sem.at[2]).wait()
    for copy in copies + [right_copy, mixed_copy, dr_copy, df_copy]:
        copy.wait_send()


def write_kernel(*refs):
    copies = [pltpu.make_async_copy(refs[n], refs[8 + n], refs[16].at[n]) for n in range(8)]
    for copy in copies:
        copy.start()
    for copy in copies:
        copy.wait()


def on_device(pair, cotangent, w_gate_a, w_proj_a, w_gate_b, w_proj_b, w_gate_out, w_out):
    rows, cols, channels = pair.shape
    whole = pl.BlockSpec(memory_space=pltpu.VMEM)
    weights = [w.T for w in (w_gate_a, w_proj_a, w_gate_b, w_proj_b, w_gate_out, w_out)]
    vm = pltpu.VMEM
    four, five = (64, 4, 2, 128), (64, 5, 2, 128)
    sixteen, eight, one = (16, 24, 128), (8, 24, 128), (24, 128)
    shapes = [jax.ShapeDtypeStruct((PAIRS, 64), bf16)] * 2 + [jax.ShapeDtypeStruct((64, 128), f32)] * 6
    outs = pl.pallas_call(
        kernel,
        out_shape=shapes,
        in_specs=[pl.BlockSpec(memory_space=pltpu.HBM)] * 8,
        out_specs=[whole] * 8,
        scratch_shapes=[
            vm((PAIRS, 128), bf16), vm((PAIRS, 64), bf16), vm((384, 128), bf16),
            pltpu.SemaphoreType.DMA((10,)),
            vm((PAIRS, 128), bf16),
            vm((PAIRS, 128), f32),
            vm((PAIRS, 1), f32),
            vm((CHUNKS, 256, 128), f32),
            vm((640, 128), f32), vm((640, 128), f32), vm((640, 128), f32),
            vm(five, bf16), vm(five, bf16), vm(four, bf16), vm(four, bf16),
            vm(five, bf16), vm((2,) + five, bf16),
            vm(five, bf16), vm(five, bf16),
            vm(four, bf16), vm(four, bf16), vm(five, bf16), vm(five, bf16),
            vm(sixteen, bf16), vm(sixteen, bf16),
            vm(one, bf16), vm(eight, bf16),
            vm(one, bf16), vm(sixteen, bf16),
            vm((192, 384), bf16), vm((384, 384), bf16),
            vm((384, 192), bf16), vm((192, 384), bf16), vm((192, 384), bf16),
            vm((PAIRS, 128), bf16), vm((PAIRS, 128), bf16),
            vm((64, 128), bf16), vm((64, 128), bf16),
            vm((64, PAIRS), bf16), vm((64, PAIRS), bf16),
            vm((128, PAIRS), f32), vm((64, PAIRS), f32),
            vm((64, PAIRS), bf16), vm((64, PAIRS), bf16),
            vm((128, PAIRS), bf16),
            vm((256, PAIRS), bf16),
            pltpu.SemaphoreType.DMA((6,)),
            pltpu.SemaphoreType.DMA((6,)),
            pltpu.SemaphoreType.DMA((8,)),
            pltpu.SemaphoreType.DMA((8,)),
            pltpu.SemaphoreType.DMA((3,)),
            pltpu.SemaphoreType.DMA((3,)),
        ],
        compiler_params=pltpu.CompilerParams(
            collective_id=0, has_side_effects=True, vmem_limit_bytes=40 << 20
        ),
    )(*[pltpu.with_memory_space_constraint(a, pltpu.HBM) for a in (pair.reshape(PAIRS, channels), cotangent.reshape(PAIRS, 64), *weights)])
    outs = pl.pallas_call(
        write_kernel,
        out_shape=shapes,
        in_specs=[whole] * 8,
        out_specs=[pl.BlockSpec(memory_space=pltpu.HBM)] * 8,
        scratch_shapes=[pltpu.SemaphoreType.DMA((8,))],
        compiler_params=pltpu.CompilerParams(vmem_limit_bytes=4 << 20),
    )(*outs)
    updated, grad_pair, ga, pa, gb, pb, go, out = outs
    return (
        updated.reshape(rows, cols, 64),
        grad_pair.reshape(rows, cols, 64),
        ga.T,
        pa.T,
        gb.T,
        pb.T,
        go.T,
        out.T,
    )


def solution(mesh):
    wide = P("row", "col", "ch")
    narrow = P(None, "ch")
    return jax.shard_map(
        on_device,
        mesh=mesh,
        in_specs=(P("row", "col", None), wide) + (narrow,) * 6,
        out_specs=(wide, wide) + (narrow,) * 6,
        check_vma=False,
    )
```

```python
import jax
import jax.numpy as jnp
from jax import lax
from jax.experimental import pallas as pl
from jax.experimental.pallas import tpu as pltpu
from jax.sharding import PartitionSpec as P

LOGICAL = pl.DeviceIdType.LOGICAL
epsilon = 1e-05
f32, bf16 = jnp.float32, jnp.bfloat16
PAIRS, CHUNKS, LANES = 1152, 9, 128


def nn(a, b):
    return lax.dot_general(a, b, (((1,), (0,)), ((), ())), preferred_element_type=f32)


def nt(a, b):
    return lax.dot_general(a, b, (((1,), (1,)), ((), ())), preferred_element_type=f32)


def tn(a, b):
    return lax.dot_general(a, b, (((0,), (0,)), ((), ())), preferred_element_type=f32)


def sigmoid(x):
    return 1.0 / (1.0 + jnp.exp(-x))


def hops(d):
    return min(d[0], 8 - d[0]) + min(d[1], 4 - d[1]) + d[2]


FAR_FIRST = sorted(
    [(dz, dy, dx) for dz in range(8) for dy in range(4) for dx in range(2) if dz + dy + dx],
    key=lambda d: -hops(d),
)


def block_transpose(x):
    groups = x.shape[0] // 8
    x = x.reshape(groups, 8, 384)
    row = lax.broadcasted_iota(jnp.int32, x.shape, 1)
    part = lax.broadcasted_iota(jnp.int32, x.shape, 2) // 48
    for bit in (1, 2, 4):
        low = (row & bit) == 0
        same = low == ((part & bit) == 0)
        up = pltpu.roll(pltpu.roll(x, bit, 1), 384 - 48 * bit, 2)
        down = pltpu.roll(pltpu.roll(x, 8 - bit, 1), 48 * bit, 2)
        x = jnp.where(same, x, jnp.where(low, down, up))
    return x.reshape(groups * 8, 384)


def kernel(
    pair_hbm, cot_hbm, wga_hbm, wpa_hbm, wgb_hbm, wpb_hbm, wgo_hbm, wo_hbm,
    updated_ref, grad_ref, g0_ref, g1_ref, g2_ref, g3_ref, g4_ref, g5_ref,
    pair_ref, cot_ref, weights, load_sem, normed, hat, rstd1, acts, flat_a, flat_b, flat_c, pad_four, pad_ten,
    send1a, recv1a, send1b, recv1b, send2a, recv2a, send2b, recv2b, send3a, recv3a, send3b, recv3b,
    send4a, recv4a, send4b, recv4b, send4c, recv4c,
    send5, recv5, sendz, recvz, send6, recv6,
    left, right, dgrid_t, dr_sum, dr_send, dr_recv, df_send, df_recv,
    wgo_other, wo_other, cot_t, cot_other, gate_out, dproj, dgate, mixn, dfour,
    send_sem, recv_sem, psend_sem, precv_sem, gsend_sem, grecv_sem,
):
    loads = [
        pltpu.make_async_copy(src, weights.at[pl.ds(64 * n, 64), :], load_sem.at[n])
        for n, src in enumerate((wga_hbm, wpa_hbm, wgb_hbm, wpb_hbm, wgo_hbm, wo_hbm))
    ]
    loads += [
        pltpu.make_async_copy(pair_hbm.at[rows, :], pair_ref.at[rows, :], load_sem.at[6 + n])
        for n, rows in enumerate(pl.ds(LANES * k, LANES) for k in range(CHUNKS))
    ]
    loads.append(pltpu.make_async_copy(cot_hbm, cot_ref, load_sem.at[15]))
    for load in loads:
        load.start()
    wgo_ref, wo_ref = weights.at[pl.ds(256, 64), :], weights.at[pl.ds(320, 64), :]

    row, col, ch = lax.axis_index("row"), lax.axis_index("col"), lax.axis_index("ch")
    x, y, z = row // 4, col // 2, (col % 2) * 4 + row % 4
    slot = (row % 8) * 8 + col
    half = row // 8
    own = half == ch
    other = row * 16 + col * 2 + 1 - ch

    slot_z = [((z + dz) % 8 % 4) * 8 + (z + dz) % 8 // 4 for dz in range(8)]
    slot_y = [((y + dy) % 4) * 2 for dy in range(4)]
    slot_x = [((x + dx) % 2) * 32 for dx in range(2)]
    base = 128 * ch + half

    def peer(t):
        return base + 2 * t

    barrier = pltpu.get_barrier_semaphore()
    pl.semaphore_signal(barrier, inc=1, device_id=other, device_id_type=LOGICAL)

    def each_peer(act):
        for dz, dy, dx in FAR_FIRST:
            act(slot_z[dz] + slot_y[dy] + slot_x[dx])

    plane = [(2, 2), (2, 1), (2, 3), (1, 2), (3, 2), (2, 0), (0, 2), (1, 1), (1, 3), (3, 1), (3, 3)]
    plane += [(1, 0), (3, 0), (0, 1), (0, 3)]

    def plane_peer(dx, dy):
        x_to, y_to = (x + dx) % 4, (y + dy) % 4
        return x_to * 4 + y_to, (x_to * 4 + row % 4) * 16 + (y_to * 2 + col % 2) * 2 + ch

    def line_peer(dz):
        z_to = (z + dz) % 8
        return (x * 4 + z_to % 4) * 16 + (y * 2 + z_to // 4) * 2 + ch

    def greet(device):
        pl.semaphore_signal(barrier, inc=1, device_id=device, device_id_type=LOGICAL)

    each_peer(lambda t: greet(peer(t)))

    @pl.when(jnp.logical_not(own))
    def _():
        greet(peer(slot))

    for dx, dy in plane:
        greet(plane_peer(dx, dy)[1])
    for dz in (4, 3, 5, 2, 6, 1, 7):
        greet(line_peer(dz))

    def swap_start(n, src, dst):
        def copy(t):
            return pltpu.make_async_remote_copy(
                src_ref=src.at[t],
                dst_ref=dst.at[slot],
                send_sem=send_sem.at[n],
                recv_sem=recv_sem.at[n],
                device_id=peer(t),
                device_id_type=LOGICAL,
            )

        each_peer(lambda t: copy(t).start())

        @pl.when(own)
        def _():
            pltpu.make_async_copy(src.at[slot], dst.at[slot], recv_sem.at[n]).start()

        @pl.when(jnp.logical_not(own))
        def _():
            copy(slot).start()

    def swap_wait(n, dst):
        pltpu.make_async_copy(dst, dst, recv_sem.at[n]).wait()

    def swap_drain(n, dst):
        @pl.when(own)
        def _():
            some = dst.at[pl.ds(0, 63)]
            pltpu.make_async_copy(some, some, send_sem.at[n]).wait()

        @pl.when(jnp.logical_not(own))
        def _():
            pltpu.make_async_copy(dst, dst, send_sem.at[n]).wait()

    def group_copy(n, src, dst, device):
        return pltpu.make_async_remote_copy(
            src_ref=src,
            dst_ref=dst,
            send_sem=gsend_sem.at[n],
            recv_sem=grecv_sem.at[n],
            device_id=device,
            device_id_type=LOGICAL,
        )

    def partner(n, src, dst):
        return pltpu.make_async_remote_copy(
            src_ref=src,
            dst_ref=dst,
            send_sem=psend_sem.at[n],
            recv_sem=precv_sem.at[n],
            device_id=other,
            device_id_type=LOGICAL,
        )

    def put(flat, rows, k, value):
        flat[pl.ds(k, 64, stride=rows), :] = value

    def get(flat, rows, k):
        return flat[pl.ds(k, 64, stride=rows), :]

    def pack(flat, rows, dst):
        dst[...] = flat[0 : 64 * rows, :].astype(bf16).reshape(dst.shape)

    def unpack(flat, rows, src):
        flat[0 : 64 * rows, :] = src[...].reshape(64 * rows, LANES).astype(f32)

    def rows_at(flat, rows, k):
        return block_transpose(jnp.concatenate([get(flat, rows, k + q) for q in range(3)], axis=1))

    def put_rows(flat, rows, k, grid):
        grid = block_transpose(grid)
        for q in range(3):
            put(flat, rows, k + q, grid[:, LANES * q : LANES * q + LANES])

    def chunk(g):
        return pl.ds(g * LANES, LANES)

    for load in loads[0:6]:
        load.wait()
    w_four = weights[0:256, :]
    for g in range(CHUNKS):
        loads[6 + g].wait()
        values = pair_ref[chunk(g), :].astype(f32)
        centred = values - jnp.mean(values, -1, keepdims=True)
        spread = jnp.mean(centred * centred, -1, keepdims=True)
        inverse = lax.rsqrt(spread + epsilon)
        hat_g = centred * inverse
        hat[chunk(g), :] = hat_g
        rstd1[chunk(g), :] = inverse
        normed_g = hat_g.astype(bf16)
        normed[chunk(g), :] = normed_g
        projected = nt(w_four, normed_g)
        gate_a = sigmoid(projected[0:64])
        proj_a = projected[64:128]
        gate_b = sigmoid(projected[128:192])
        proj_b = projected[192:256]
        acts[g, 0:64, :] = gate_a
        acts[g, 64:128, :] = proj_a
        acts[g, 128:192, :] = gate_b
        acts[g, 192:256, :] = proj_b
        put(flat_a, 12, g, gate_b * proj_b)
        put(*((flat_a, 12, 9 + g) if g < 3 else (flat_b, 6, g - 3)), gate_a * proj_a)
    pack(flat_a, 12, send1a)
    pack(flat_b, 6, send1b)
    put(pad_four, 4, 3, jnp.zeros((64, LANES), f32))
    put(pad_ten, 10, 9, jnp.zeros((64, LANES), f32))

    @pl.when(own)
    def _():
        pl.semaphore_wait(barrier, 86)

    @pl.when(jnp.logical_not(own))
    def _():
        pl.semaphore_wait(barrier, 87)

    swap_start(0, send1a, recv1a)
    swap_start(1, send1b, recv1b)

    copies = [partner(0, wgo_ref, wgo_other), partner(1, wo_ref, wo_other)]
    for copy in copies:
        copy.start()
    loads[15].wait()
    for g in range(CHUNKS):
        cot_t[:, chunk(g)] = jnp.transpose(cot_ref[chunk(g), :].astype(f32)).astype(bf16)
    copies.append(partner(2, cot_t, cot_other))
    copies[2].start()
    for copy in copies:
        copy.wait_recv()
    wgo = jnp.concatenate([wgo_ref[...], wgo_other[...]], axis=0)
    for g in range(CHUNKS):
        gate_out[:, chunk(g)] = sigmoid(nt(wgo, normed[chunk(g), :]))
    mine_rows = pl.ds(pl.multiple_of(ch * 64, 64), 64)
    wo_cols = jnp.concatenate([wo_ref[...], wo_other[...]], axis=0).astype(f32)
    wo_t = jnp.where(ch == 0, wo_cols, pltpu.roll(wo_cols, 64, 1))
    wo = jnp.transpose(wo_t).astype(bf16)
    wo_t = wo_t.astype(bf16)

    swap_wait(0, recv1a)
    mine_half = pl.ds(pl.multiple_of(ch * 192, 192), 192)
    other_half = pl.ds(pl.multiple_of((1 - ch) * 192, 192), 192)
    unpack(flat_a, 12, recv1a)
    runs = [rows_at(flat_a, 12, 3 * gg) for gg in range(3)]
    tiles = [runs[gg][8 * r : 8 * r + 8] for r in range(8) for gg in range(3)]
    right[mine_half, :] = jnp.concatenate(tiles, axis=0).astype(bf16)
    right_copy = partner(3, right.at[mine_half, :], right.at[mine_half, :])
    right_copy.start()
    left[0:64, :] = rows_at(flat_a, 12, 9).astype(bf16)
    right_copy.wait_recv()
    put_rows(pad_four, 4, 0, nt(left[0:64, :], right[...]))
    pack(pad_four, 4, send2a)
    swap_start(2, send2a, recv2a.at[0])
    swap_wait(1, recv1b)
    unpack(flat_b, 6, recv1b)
    for k in range(2):
        left[64 + 64 * k : 128 + 64 * k, :] = rows_at(flat_b, 6, 3 * k).astype(bf16)
    mixed_b = nt(left[64:192, :], right[...])
    for k in range(2):
        put_rows(flat_c, 6, 3 * k, mixed_b[64 * k : 64 * k + 64])
    pack(flat_c, 6, send2b)
    swap_start(3, send2b, recv2b.at[0])

    def middle(g, first, second, rows, k, dst):
        mixed = jnp.concatenate([get(first, rows, k), get(second, rows, k)], axis=0)
        mean = jnp.mean(mixed, 0, keepdims=True)
        var = jnp.mean(mixed * mixed, 0, keepdims=True) - mean * mean
        inverse = lax.rsqrt(var + epsilon)
        mixed_hat = (mixed - mean) * inverse
        mixed_norm = mixed_hat.astype(bf16)
        mixn[:, chunk(g)] = mixed_norm
        upstream = jnp.concatenate([cot_t[:, chunk(g)], cot_other[:, chunk(g)]], axis=0).astype(f32)
        d_proj = (upstream * gate_out[:, chunk(g)]).astype(bf16)
        dproj[:, chunk(g)] = d_proj[0:64]
        d_norm = nn(wo, d_proj)
        d_mean = jnp.mean(d_norm, 0, keepdims=True)
        d_cross = jnp.mean(d_norm * mixed_hat, 0, keepdims=True)
        put(dst, rows, k, inverse * (d_norm[0:64] - d_mean - mixed_hat[0:64] * d_cross))

    swap_wait(2, recv2a.at[0])
    mixed_copy_a = partner(4, recv2a.at[0], recv2a.at[1])
    mixed_copy_a.start()
    mixed_copy_a.wait_recv()
    swap_wait(3, recv2b.at[0])
    mixed_copy_b = partner(8, recv2b.at[0], recv2b.at[1])
    mixed_copy_b.start()
    unpack(flat_a, 4, recv2a.at[0])
    unpack(flat_b, 4, recv2a.at[1])
    for k in range(3):
        middle(k, flat_a, flat_b, 4, k, pad_four)
    pack(pad_four, 4, send3a)
    swap_start(4, send3a, recv3a)
    mixed_copy_b.wait_recv()
    unpack(flat_a, 6, recv2b.at[0])
    unpack(flat_b, 6, recv2b.at[1])
    for k in range(6):
        middle(3 + k, flat_a, flat_b, 6, k, flat_c)
    pack(flat_c, 6, send3b)
    swap_start(5, send3b, recv3b)
    for g in range(CHUNKS):
        proj_out = nn(wo_t[0:64], mixn[:, chunk(g)])
        gate = gate_out[0:64, chunk(g)]
        upstream = cot_t[:, chunk(g)].astype(f32)
        dgate[:, chunk(g)] = (upstream * proj_out * gate * (1.0 - gate)).astype(bf16)
        updated_ref[chunk(g), :] = jnp.transpose(gate * proj_out).astype(bf16)
    head_gate = nn(dgate[...], normed[...])
    head_out = nt(dproj[...], mixn[...])

    swap_wait(4, recv3a)
    unpack(flat_a, 4, recv3a)
    d_grid = rows_at(flat_a, 4, 0).astype(bf16)
    put_rows(pad_four, 4, 0, nn(d_grid, right[...]))
    pack(pad_four, 4, send4a)
    swap_start(6, send4a, recv4a)
    dr_sum[...] = tn(d_grid, left[0:64, :])
    swap_wait(5, recv3b)
    unpack(flat_a, 6, recv3b)
    d_grid = jnp.concatenate([rows_at(flat_a, 6, 3 * k) for k in range(2)], axis=0)
    dgrid_t[...] = jnp.transpose(d_grid).astype(bf16)
    dr_send[...] = (dr_sum[other_half, :] + nn(dgrid_t[other_half, :], left[64:192, :])).astype(bf16)
    dr_copy = partner(5, dr_send, dr_recv)
    dr_copy.start()
    d_left = nn(d_grid.astype(bf16), right[...])
    for k in range(2):
        put_rows(flat_c, 6, 3 * k, d_left[64 * k : 64 * k + 64])
    pack(flat_c, 6, send4b)
    swap_start(7, send4b, recv4b)
    d_right = dr_sum[mine_half, :] + nn(dgrid_t[mine_half, :], left[64:192, :])
    dr_copy.wait_recv()
    d_right = d_right + dr_recv[...].astype(f32)
    for gg in range(3):
        tiles = [d_right[8 * (3 * r + gg) : 8 * (3 * r + gg) + 8] for r in range(8)]
        put_rows(pad_ten, 10, 3 * gg, jnp.concatenate(tiles, axis=0))
    pack(pad_ten, 10, send4c)
    swap_start(8, send4c, recv4c)

    def left_terms(g, d_left):
        gate_a, proj_a = acts[g, 0:64, :], acts[g, 64:128, :]
        dfour[0:64, chunk(g)] = (d_left * proj_a * gate_a * (1.0 - gate_a)).astype(bf16)
        dfour[64:128, chunk(g)] = (d_left * gate_a).astype(bf16)

    swap_wait(6, recv4a)
    unpack(flat_a, 4, recv4a)
    for g in range(3):
        left_terms(g, get(flat_a, 4, g))
    swap_wait(7, recv4b)
    unpack(flat_b, 6, recv4b)
    for g in range(6):
        left_terms(3 + g, get(flat_b, 6, g))
    edge_left = nn(dfour[0:128, :], normed[...])
    swap_wait(8, recv4c)
    unpack(pad_ten, 10, recv4c)
    for g in range(CHUNKS):
        d_right_g = get(pad_ten, 10, g)
        gate_b, proj_b = acts[g, 128:192, :], acts[g, 192:256, :]
        dfour[128:192, chunk(g)] = (d_right_g * proj_b * gate_b * (1.0 - gate_b)).astype(bf16)
        dfour[192:256, chunk(g)] = (d_right_g * gate_b).astype(bf16)
    edge_right = nn(dfour[128:256, :], normed[...])

    for k in range(2):
        put(flat_c, 6, k, edge_left[64 * k : 64 * k + 64])
        put(flat_c, 6, 2 + k, edge_right[64 * k : 64 * k + 64])
    put(flat_c, 6, 4, head_gate)
    put(flat_c, 6, 5, jnp.where(ch == 0, head_out, pltpu.roll(head_out, 64, 1)))
    pack(flat_c, 6, send5)
    e_me, _ = plane_peer(0, 0)
    for dx, dy in plane:
        e, device = plane_peer(dx, dy)
        group_copy(0, send5.at[e], recv5.at[e_me], device).start()
    pltpu.make_async_copy(send5.at[e_me], recv5.at[e_me], grecv_sem.at[0]).start()
    for g in range(CHUNKS):
        d_flat = tn(dfour[:, chunk(g)], w_four) + tn(dgate[:, chunk(g)], wgo_ref[...])
        df_send[chunk(g), :] = d_flat.astype(bf16)
    df_copy = partner(6, df_send, df_recv)
    df_copy.start()
    pltpu.make_async_copy(recv5, recv5, grecv_sem.at[0]).wait()
    sendz[...] = jnp.sum(recv5[...].astype(f32), 0).astype(bf16)
    for dz in (4, 3, 5, 2, 6, 1, 7):
        group_copy(1, sendz, recvz.at[z], line_peer(dz)).start()
    pltpu.make_async_copy(sendz, recvz.at[z], grecv_sem.at[1]).start()
    df_copy.wait_recv()
    for g in range(CHUNKS):
        grad_whole = df_send[chunk(g), :].astype(f32) + df_recv[chunk(g), :].astype(f32)
        hat_g = hat[chunk(g), :]
        grad_full = rstd1[chunk(g), :] * (
            grad_whole
            - jnp.mean(grad_whole, -1, keepdims=True)
            - hat_g * jnp.mean(grad_whole * hat_g, -1, keepdims=True)
        )
        grad_full = jnp.where(ch == 0, grad_full, pltpu.roll(grad_full, 64, 1))
        grad_ref[chunk(g), :] = grad_full[:, 0:64].astype(bf16)

    pltpu.make_async_copy(recvz, recvz, grecv_sem.at[1]).wait()
    send6[...] = jnp.sum(recvz[...].astype(f32), 0).astype(bf16)
    for dx, dy in plane:
        _, device = plane_peer(dx, dy)
        group_copy(2, send6, recv6.at[e_me], device).start()
    pltpu.make_async_copy(send6, recv6.at[e_me], grecv_sem.at[2]).start()
    pltpu.make_async_copy(recv6, recv6, grecv_sem.at[2]).wait()
    unpack(flat_c, 6, recv6)
    for k, g_ref in enumerate((g0_ref, g1_ref, g2_ref, g3_ref, g4_ref, g5_ref)):
        g_ref[...] = get(flat_c, 6, k) * (1.0 / 384)

    for n, dst in enumerate(
        (recv1a, recv1b, recv2a.at[0], recv2b.at[0], recv3a, recv3b, recv4a, recv4b, recv4c)
    ):
        swap_drain(n, dst)
    pltpu.make_async_copy(recv5.at[pl.ds(0, 15)], recv5.at[pl.ds(0, 15)], gsend_sem.at[0]).wait()
    pltpu.make_async_copy(recvz.at[pl.ds(0, 7)], recvz.at[pl.ds(0, 7)], gsend_sem.at[1]).wait()
    pltpu.make_async_copy(recv6.at[pl.ds(0, 15)], recv6.at[pl.ds(0, 15)], gsend_sem.at[2]).wait()
    for copy in copies + [right_copy, mixed_copy_a, mixed_copy_b, dr_copy, df_copy]:
        copy.wait_send()


def write_kernel(*refs):
    copies = [pltpu.make_async_copy(refs[n], refs[8 + n], refs[16].at[n]) for n in range(8)]
    for copy in copies:
        copy.start()
    for copy in copies:
        copy.wait()


def on_device(pair, cotangent, w_gate_a, w_proj_a, w_gate_b, w_proj_b, w_gate_out, w_out):
    rows, cols, channels = pair.shape
    whole = pl.BlockSpec(memory_space=pltpu.VMEM)
    weights = [w.T for w in (w_gate_a, w_proj_a, w_gate_b, w_proj_b, w_gate_out, w_out)]
    vm = pltpu.VMEM
    two, three, five, six = [(64, n, 2, 128) for n in (2, 3, 5, 6)]
    sixteen, eight, one = (16, 24, 128), (8, 24, 128), (24, 128)
    shapes = [jax.ShapeDtypeStruct((PAIRS, 64), bf16)] * 2 + [jax.ShapeDtypeStruct((64, 128), f32)] * 6
    outs = pl.pallas_call(
        kernel,
        out_shape=shapes,
        in_specs=[pl.BlockSpec(memory_space=pltpu.HBM)] * 8,
        out_specs=[whole] * 8,
        scratch_shapes=[
            vm((PAIRS, 128), bf16), vm((PAIRS, 64), bf16), vm((384, 128), bf16),
            pltpu.SemaphoreType.DMA((16,)),
            vm((PAIRS, 128), bf16),
            vm((PAIRS, 128), f32),
            vm((PAIRS, 1), f32),
            vm((CHUNKS, 256, 128), f32),
            vm((768, 128), f32), vm((768, 128), f32), vm((384, 128), f32),
            vm((256, 128), f32), vm((640, 128), f32),
            vm(six, bf16), vm(six, bf16), vm(three, bf16), vm(three, bf16),
            vm(two, bf16), vm((2,) + two, bf16), vm(three, bf16), vm((2,) + three, bf16),
            vm(two, bf16), vm(two, bf16), vm(three, bf16), vm(three, bf16),
            vm(two, bf16), vm(two, bf16), vm(three, bf16), vm(three, bf16), vm(five, bf16), vm(five, bf16),
            vm(sixteen, bf16), vm(sixteen, bf16),
            vm(one, bf16), vm(eight, bf16),
            vm(one, bf16), vm(sixteen, bf16),
            vm((192, 384), bf16), vm((384, 384), bf16),
            vm((384, 128), bf16), vm((384, 384), f32), vm((192, 384), bf16), vm((192, 384), bf16),
            vm((PAIRS, 128), bf16), vm((PAIRS, 128), bf16),
            vm((64, 128), bf16), vm((64, 128), bf16),
            vm((64, PAIRS), bf16), vm((64, PAIRS), bf16),
            vm((128, PAIRS), f32),
            vm((64, PAIRS), bf16), vm((64, PAIRS), bf16),
            vm((128, PAIRS), bf16),
            vm((256, PAIRS), bf16),
            pltpu.SemaphoreType.DMA((9,)),
            pltpu.SemaphoreType.DMA((9,)),
            pltpu.SemaphoreType.DMA((9,)),
            pltpu.SemaphoreType.DMA((9,)),
            pltpu.SemaphoreType.DMA((3,)),
            pltpu.SemaphoreType.DMA((3,)),
        ],
        compiler_params=pltpu.CompilerParams(
            collective_id=0, has_side_effects=True, vmem_limit_bytes=40 << 20
        ),
    )(*[pltpu.with_memory_space_constraint(a, pltpu.HBM) for a in (pair.reshape(PAIRS, channels), cotangent.reshape(PAIRS, 64), *weights)])
    outs = pl.pallas_call(
        write_kernel,
        out_shape=shapes,
        in_specs=[whole] * 8,
        out_specs=[pl.BlockSpec(memory_space=pltpu.HBM)] * 8,
        scratch_shapes=[pltpu.SemaphoreType.DMA((8,))],
        compiler_params=pltpu.CompilerParams(vmem_limit_bytes=4 << 20),
    )(*outs)
    updated, grad_pair, ga, pa, gb, pb, go, out = outs
    return (
        updated.reshape(rows, cols, 64),
        grad_pair.reshape(rows, cols, 64),
        ga.T,
        pa.T,
        gb.T,
        pb.T,
        go.T,
        out.T,
    )


def solution(mesh):
    wide = P("row", "col", "ch")
    narrow = P(None, "ch")
    return jax.shard_map(
        on_device,
        mesh=mesh,
        in_specs=(P("row", "col", None), wide) + (narrow,) * 6,
        out_specs=(wide, wide) + (narrow,) * 6,
        check_vma=False,
    )
```

```python
import jax
import jax.numpy as jnp
from jax import lax
from jax.experimental import pallas as pl
from jax.experimental.pallas import tpu as pltpu
from jax.sharding import PartitionSpec as P

LOGICAL = pl.DeviceIdType.LOGICAL
epsilon = 1e-05
f32, bf16 = jnp.float32, jnp.bfloat16
PAIRS, CHUNKS, LANES = 1152, 9, 128


def nn(a, b):
    return lax.dot_general(a, b, (((1,), (0,)), ((), ())), preferred_element_type=f32)


def nt(a, b):
    return lax.dot_general(a, b, (((1,), (1,)), ((), ())), preferred_element_type=f32)


def tn(a, b):
    return lax.dot_general(a, b, (((0,), (0,)), ((), ())), preferred_element_type=f32)


def sigmoid(x):
    return 1.0 / (1.0 + jnp.exp(-x))


def hops(d):
    return min(d[0], 8 - d[0]) + min(d[1], 4 - d[1]) + d[2]


FAR_FIRST = sorted(
    [(dz, dy, dx) for dz in range(8) for dy in range(4) for dx in range(2) if dz + dy + dx],
    key=lambda d: -hops(d),
)


def trade(arrays):
    arrays = list(arrays)
    part = lax.broadcasted_iota(jnp.int32, arrays[0].shape, 1) // 48
    for bit in (1, 2, 4):
        high = (part & bit) != 0
        for c in range(8):
            if c & bit == 0:
                a, b = arrays[c], arrays[c | bit]
                arrays[c] = jnp.where(high, pltpu.roll(b, 48 * bit, 1), a)
                arrays[c | bit] = jnp.where(high, b, pltpu.roll(a, 384 - 48 * bit, 1))
    return arrays


def kernel(
    pair_hbm, cot_hbm, wga_hbm, wpa_hbm, wgb_hbm, wpb_hbm, wgo_hbm, wo_hbm,
    updated_ref, grad_ref, g0_ref, g1_ref, g2_ref, g3_ref, g4_ref, g5_ref,
    pair_ref, cot_ref, weights, load_sem, normed, hat, rstd1, acts, flat_a, flat_b, flat_c, pad_four, pad_ten, grid,
    send1a, recv1a, send1b, recv1b, send1c, recv1c, send2a, recv2a, send2b, recv2b, send3a, recv3a, send3b, recv3b,
    send4a, recv4a, send4b, recv4b, send4c, recv4c,
    send5, recv5, sendz, recvz, send6, recv6,
    left, right, dgrid_t, dr_sum, dr_send, dr_recv, df_send, df_recv,
    wgo_other, wo_other, cot_t, cot_other, gate_out, dproj, dgate, mixn, dfour,
    send_sem, recv_sem, psend_sem, precv_sem, gsend_sem, grecv_sem,
):
    loads = [
        pltpu.make_async_copy(pair_hbm.at[rows, :], pair_ref.at[rows, :], load_sem.at[n])
        for n, rows in enumerate(pl.ds(384 * k, 384) for k in range(3))
    ]
    loads += [
        pltpu.make_async_copy(src, weights.at[pl.ds(64 * n, 64), :], load_sem.at[3 + n])
        for n, src in enumerate((wga_hbm, wpa_hbm, wgb_hbm, wpb_hbm, wgo_hbm, wo_hbm))
    ]
    loads.append(pltpu.make_async_copy(cot_hbm, cot_ref, load_sem.at[9]))
    for load in loads:
        load.start()
    wgo_ref, wo_ref = weights.at[pl.ds(256, 64), :], weights.at[pl.ds(320, 64), :]

    row, col, ch = lax.axis_index("row"), lax.axis_index("col"), lax.axis_index("ch")
    x, y, z = row // 4, col // 2, (col % 2) * 4 + row % 4
    slot = (row % 8) * 8 + col
    half = row // 8
    own = half == ch
    other = row * 16 + col * 2 + 1 - ch

    slot_z = [((z + dz) % 8 % 4) * 8 + (z + dz) % 8 // 4 for dz in range(8)]
    slot_y = [((y + dy) % 4) * 2 for dy in range(4)]
    slot_x = [((x + dx) % 2) * 32 for dx in range(2)]
    base = 128 * ch + half

    def peer(t):
        return base + 2 * t

    barrier = pltpu.get_barrier_semaphore()
    pl.semaphore_signal(barrier, inc=1, device_id=other, device_id_type=LOGICAL)

    def each_peer(act):
        for dz, dy, dx in FAR_FIRST:
            act(slot_z[dz] + slot_y[dy] + slot_x[dx])

    plane = [(2, 2), (2, 1), (2, 3), (1, 2), (3, 2), (2, 0), (0, 2), (1, 1), (1, 3), (3, 1), (3, 3)]
    plane += [(1, 0), (3, 0), (0, 1), (0, 3)]

    def plane_peer(dx, dy):
        x_to, y_to = (x + dx) % 4, (y + dy) % 4
        return x_to * 4 + y_to, (x_to * 4 + row % 4) * 16 + (y_to * 2 + col % 2) * 2 + ch

    def line_peer(dz):
        z_to = (z + dz) % 8
        return (x * 4 + z_to % 4) * 16 + (y * 2 + z_to // 4) * 2 + ch

    def greet(device):
        pl.semaphore_signal(barrier, inc=1, device_id=device, device_id_type=LOGICAL)

    each_peer(lambda t: greet(peer(t)))

    @pl.when(jnp.logical_not(own))
    def _():
        greet(peer(slot))

    for dx, dy in plane:
        greet(plane_peer(dx, dy)[1])
    for dz in (4, 3, 5, 2, 6, 1, 7):
        greet(line_peer(dz))

    def swap_start(n, src, dst):
        def copy(t):
            return pltpu.make_async_remote_copy(
                src_ref=src.at[t],
                dst_ref=dst.at[slot],
                send_sem=send_sem.at[n],
                recv_sem=recv_sem.at[n],
                device_id=peer(t),
                device_id_type=LOGICAL,
            )

        each_peer(lambda t: copy(t).start())

        @pl.when(own)
        def _():
            pltpu.make_async_copy(src.at[slot], dst.at[slot], recv_sem.at[n]).start()

        @pl.when(jnp.logical_not(own))
        def _():
            copy(slot).start()

    def swap_wait(n, dst):
        pltpu.make_async_copy(dst, dst, recv_sem.at[n]).wait()

    def swap_drain(n, dst):
        @pl.when(own)
        def _():
            some = dst.at[pl.ds(0, 63)]
            pltpu.make_async_copy(some, some, send_sem.at[n]).wait()

        @pl.when(jnp.logical_not(own))
        def _():
            pltpu.make_async_copy(dst, dst, send_sem.at[n]).wait()

    def group_copy(n, src, dst, device):
        return pltpu.make_async_remote_copy(
            src_ref=src,
            dst_ref=dst,
            send_sem=gsend_sem.at[n],
            recv_sem=grecv_sem.at[n],
            device_id=device,
            device_id_type=LOGICAL,
        )

    def partner(n, src, dst):
        return pltpu.make_async_remote_copy(
            src_ref=src,
            dst_ref=dst,
            send_sem=psend_sem.at[n],
            recv_sem=precv_sem.at[n],
            device_id=other,
            device_id_type=LOGICAL,
        )

    def put(flat, rows, k, value):
        flat[pl.ds(k, 64, stride=rows), :] = value

    def get(flat, rows, k):
        return flat[pl.ds(k, 64, stride=rows), :]

    def pack(flat, rows, dst):
        dst[...] = flat[0 : 64 * rows, :].astype(bf16).reshape(dst.shape)

    def unpack(flat, rows, src):
        flat[0 : 64 * rows, :] = src[...].reshape(64 * rows, LANES).astype(f32)

    def run_of(three):
        def piece(flat, rows, k, c):
            return flat[pl.ds(c * rows + k, 8, stride=8 * rows), :]

        return trade([jnp.concatenate([piece(*at, c) for at in three], axis=1) for c in range(8)])

    def rows_at(flat, rows, k):
        return jnp.concatenate(run_of([(flat, rows, k + q) for q in range(3)]), axis=0)

    def put_run(three, arrays):
        for c, array in enumerate(trade(arrays)):
            for q, (flat, rows, k) in enumerate(three):
                flat[pl.ds(c * rows + k, 8, stride=8 * rows), :] = array[:, LANES * q : LANES * q + LANES]

    def eight(grid):
        return [grid[8 * m : 8 * m + 8] for m in range(8)]

    def put_rows(flat, rows, k, grid):
        put_run([(flat, rows, k + q) for q in range(3)], eight(grid))

    def chunk(g):
        return pl.ds(g * LANES, LANES)

    for load in loads[0:9]:
        load.wait()
    w_four = weights[0:256, :]
    for g in range(CHUNKS):
        values = pair_ref[chunk(g), :].astype(f32)
        centred = values - jnp.mean(values, -1, keepdims=True)
        spread = jnp.mean(centred * centred, -1, keepdims=True)
        inverse = lax.rsqrt(spread + epsilon)
        hat_g = centred * inverse
        hat[chunk(g), :] = hat_g
        rstd1[chunk(g), :] = inverse
        normed_g = hat_g.astype(bf16)
        normed[chunk(g), :] = normed_g
        projected = nt(w_four, normed_g)
        gate_a = sigmoid(projected[0:64])
        proj_a = projected[64:128]
        gate_b = sigmoid(projected[128:192])
        proj_b = projected[192:256]
        acts[g, 0:64, :] = gate_a
        acts[g, 64:128, :] = proj_a
        acts[g, 128:192, :] = gate_b
        acts[g, 192:256, :] = proj_b
        put(flat_a, 10, g, gate_b * proj_b)
        put(*((flat_a, 10, 9) if g == 0 else (pad_ten, 2, g - 1) if g < 3 else (flat_b, 6, g - 3)), gate_a * proj_a)
    pack(flat_a, 10, send1a)
    pack(pad_ten, 2, send1c)
    pack(flat_b, 6, send1b)
    put(pad_four, 4, 3, jnp.zeros((64, LANES), f32))

    @pl.when(own)
    def _():
        pl.semaphore_wait(barrier, 86)

    @pl.when(jnp.logical_not(own))
    def _():
        pl.semaphore_wait(barrier, 87)

    swap_start(0, send1a, recv1a)
    swap_start(9, send1c, recv1c)
    swap_start(1, send1b, recv1b)

    copies = [partner(0, wgo_ref, wgo_other), partner(1, wo_ref, wo_other)]
    for copy in copies:
        copy.start()
    loads[9].wait()
    for g in range(CHUNKS):
        cot_t[:, chunk(g)] = jnp.transpose(cot_ref[chunk(g), :].astype(f32)).astype(bf16)
    copies.append(partner(2, cot_t, cot_other))
    copies[2].start()
    for copy in copies:
        copy.wait_recv()
    wgo = jnp.concatenate([wgo_ref[...], wgo_other[...]], axis=0)
    for g in range(CHUNKS):
        gate_out[:, chunk(g)] = sigmoid(nt(wgo, normed[chunk(g), :]))
    mine_rows = pl.ds(pl.multiple_of(ch * 64, 64), 64)
    wo_cols = jnp.concatenate([wo_ref[...], wo_other[...]], axis=0).astype(f32)
    wo_t = jnp.where(ch == 0, wo_cols, pltpu.roll(wo_cols, 64, 1))
    wo = jnp.transpose(wo_t).astype(bf16)
    wo_t = wo_t.astype(bf16)

    swap_wait(0, recv1a)
    mine_half = pl.ds(pl.multiple_of(ch * 192, 192), 192)
    other_half = pl.ds(pl.multiple_of((1 - ch) * 192, 192), 192)
    unpack(flat_a, 10, recv1a)
    for gg in range(3):
        for m, array in enumerate(run_of([(flat_a, 10, 3 * gg + q) for q in range(3)])):
            for q in range(3):
                grid[q, pl.ds(8 * gg + m, 8, stride=24), :] = array[:, LANES * q : LANES * q + LANES]
    for q in range(3):
        right[mine_half, LANES * q : LANES * q + LANES] = grid[q].astype(bf16)
    right_copy = partner(3, right.at[mine_half, :], right.at[mine_half, :])
    right_copy.start()
    swap_wait(9, recv1c)
    unpack(flat_c, 2, recv1c)
    left[0:64, :] = jnp.concatenate(run_of([(flat_a, 10, 9), (flat_c, 2, 0), (flat_c, 2, 1)]), axis=0).astype(bf16)
    right_copy.wait_recv()
    put_rows(pad_four, 4, 0, nt(left[0:64, :], right[...]))
    pack(pad_four, 4, send2a)
    swap_start(2, send2a, recv2a.at[0])
    swap_wait(1, recv1b)
    unpack(flat_b, 6, recv1b)
    for k in range(2):
        left[64 + 64 * k : 128 + 64 * k, :] = rows_at(flat_b, 6, 3 * k).astype(bf16)
    mixed_b = nt(left[64:192, :], right[...])
    for k in range(2):
        put_rows(flat_c, 6, 3 * k, mixed_b[64 * k : 64 * k + 64])
    pack(flat_c, 6, send2b)
    swap_start(3, send2b, recv2b.at[0])

    def middle(g, first, second, rows, k, dst):
        mixed = jnp.concatenate([get(first, rows, k), get(second, rows, k)], axis=0)
        mean = jnp.mean(mixed, 0, keepdims=True)
        var = jnp.mean(mixed * mixed, 0, keepdims=True) - mean * mean
        inverse = lax.rsqrt(var + epsilon)
        mixed_hat = (mixed - mean) * inverse
        mixed_norm = mixed_hat.astype(bf16)
        mixn[:, chunk(g)] = mixed_norm
        upstream = jnp.concatenate([cot_t[:, chunk(g)], cot_other[:, chunk(g)]], axis=0).astype(f32)
        d_proj = (upstream * gate_out[:, chunk(g)]).astype(bf16)
        dproj[:, chunk(g)] = d_proj[0:64]
        d_norm = nn(wo, d_proj)
        d_mean = jnp.mean(d_norm, 0, keepdims=True)
        d_cross = jnp.mean(d_norm * mixed_hat, 0, keepdims=True)
        put(dst, rows, k, inverse * (d_norm[0:64] - d_mean - mixed_hat[0:64] * d_cross))

    swap_wait(2, recv2a.at[0])
    mixed_copy_a = partner(4, recv2a.at[0], recv2a.at[1])
    mixed_copy_a.start()
    mixed_copy_a.wait_recv()
    swap_wait(3, recv2b.at[0])
    mixed_copy_b = partner(8, recv2b.at[0], recv2b.at[1])
    mixed_copy_b.start()
    unpack(flat_a, 4, recv2a.at[0])
    unpack(flat_b, 4, recv2a.at[1])
    for k in range(3):
        middle(k, flat_a, flat_b, 4, k, pad_four)
    pack(pad_four, 4, send3a)
    swap_start(4, send3a, recv3a)
    mixed_copy_b.wait_recv()
    unpack(flat_a, 6, recv2b.at[0])
    unpack(flat_b, 6, recv2b.at[1])
    for k in range(6):
        middle(3 + k, flat_a, flat_b, 6, k, flat_c)
    pack(flat_c, 6, send3b)
    swap_start(5, send3b, recv3b)
    for g in range(CHUNKS):
        proj_out = nn(wo_t[0:64], mixn[:, chunk(g)])
        gate = gate_out[0:64, chunk(g)]
        upstream = cot_t[:, chunk(g)].astype(f32)
        dgate[:, chunk(g)] = (upstream * proj_out * gate * (1.0 - gate)).astype(bf16)
        updated_ref[chunk(g), :] = jnp.transpose(gate * proj_out).astype(bf16)
    head_gate = nn(dgate[...], normed[...])
    head_out = nt(dproj[...], mixn[...])

    swap_wait(4, recv3a)
    unpack(flat_a, 4, recv3a)
    d_grid = rows_at(flat_a, 4, 0).astype(bf16)
    put_run([(flat_b, 2, 0), (flat_b, 2, 1), (flat_c, 6, 0)], eight(nn(d_grid, right[...])))
    pack(flat_b, 2, send4a)
    swap_start(6, send4a, recv4a)
    dr_sum[...] = tn(d_grid, left[0:64, :])
    swap_wait(5, recv3b)
    unpack(flat_a, 6, recv3b)
    d_grid = jnp.concatenate([rows_at(flat_a, 6, 3 * k) for k in range(2)], axis=0)
    dgrid_t[...] = jnp.transpose(d_grid).astype(bf16)
    dr_send[...] = (dr_sum[other_half, :] + nn(dgrid_t[other_half, :], left[64:192, :])).astype(bf16)
    dr_copy = partner(5, dr_send, dr_recv)
    dr_copy.start()
    d_left = nn(d_grid.astype(bf16), right[...])
    put_rows(flat_c, 6, 1, d_left[0:64])
    put_run([(flat_c, 6, 4), (flat_c, 6, 5), (pad_ten, 10, 0)], eight(d_left[64:128]))
    pack(flat_c, 6, send4b)
    swap_start(7, send4b, recv4b)
    d_right = dr_sum[mine_half, :] + nn(dgrid_t[mine_half, :], left[64:192, :])
    dr_copy.wait_recv()
    d_right = d_right + dr_recv[...].astype(f32)
    for q in range(3):
        grid[q] = d_right[:, LANES * q : LANES * q + LANES]
    for gg in range(3):
        arrays = [
            jnp.concatenate([grid[q, pl.ds(8 * gg + m, 8, stride=24), :] for q in range(3)], axis=1)
            for m in range(8)
        ]
        put_run([(pad_ten, 10, 1 + 3 * gg + q) for q in range(3)], arrays)
    pack(pad_ten, 10, send4c)
    swap_start(8, send4c, recv4c)

    def left_terms(g, d_left):
        gate_a, proj_a = acts[g, 0:64, :], acts[g, 64:128, :]
        dfour[0:64, chunk(g)] = (d_left * proj_a * gate_a * (1.0 - gate_a)).astype(bf16)
        dfour[64:128, chunk(g)] = (d_left * gate_a).astype(bf16)

    swap_wait(6, recv4a)
    unpack(flat_a, 2, recv4a)
    for g in range(2):
        left_terms(g, get(flat_a, 2, g))
    swap_wait(7, recv4b)
    unpack(flat_b, 6, recv4b)
    for g in range(6):
        left_terms(2 + g, get(flat_b, 6, g))
    edge_left = nn(dfour[0:128, 0:1024], normed[0:1024, :])
    swap_wait(8, recv4c)
    unpack(pad_ten, 10, recv4c)
    left_terms(8, get(pad_ten, 10, 0))
    for g in range(CHUNKS):
        d_right_g = get(pad_ten, 10, 1 + g)
        gate_b, proj_b = acts[g, 128:192, :], acts[g, 192:256, :]
        dfour[128:192, chunk(g)] = (d_right_g * proj_b * gate_b * (1.0 - gate_b)).astype(bf16)
        dfour[192:256, chunk(g)] = (d_right_g * gate_b).astype(bf16)
    edge_left += nn(dfour[0:128, 1024:1152], normed[1024:1152, :])
    edge_right = nn(dfour[128:256, :], normed[...])

    for k in range(2):
        put(flat_c, 6, k, edge_left[64 * k : 64 * k + 64])
        put(flat_c, 6, 2 + k, edge_right[64 * k : 64 * k + 64])
    put(flat_c, 6, 4, head_gate)
    put(flat_c, 6, 5, jnp.where(ch == 0, head_out, pltpu.roll(head_out, 64, 1)))
    pack(flat_c, 6, send5)
    e_me, _ = plane_peer(0, 0)
    for dx, dy in plane:
        e, device = plane_peer(dx, dy)
        group_copy(0, send5.at[e], recv5.at[e_me], device).start()
    pltpu.make_async_copy(send5.at[e_me], recv5.at[e_me], grecv_sem.at[0]).start()
    for g in range(CHUNKS):
        d_flat = tn(dfour[:, chunk(g)], w_four) + tn(dgate[:, chunk(g)], wgo_ref[...])
        df_send[chunk(g), :] = d_flat.astype(bf16)
    df_copy = partner(6, df_send, df_recv)
    df_copy.start()
    pltpu.make_async_copy(recv5, recv5, grecv_sem.at[0]).wait()
    sendz[...] = jnp.sum(recv5[...].astype(f32), 0).astype(bf16)
    for dz in (4, 3, 5, 2, 6, 1, 7):
        group_copy(1, sendz, recvz.at[z], line_peer(dz)).start()
    pltpu.make_async_copy(sendz, recvz.at[z], grecv_sem.at[1]).start()
    df_copy.wait_recv()
    for g in range(CHUNKS):
        grad_whole = df_send[chunk(g), :].astype(f32) + df_recv[chunk(g), :].astype(f32)
        hat_g = hat[chunk(g), :]
        grad_full = rstd1[chunk(g), :] * (
            grad_whole
            - jnp.mean(grad_whole, -1, keepdims=True)
            - hat_g * jnp.mean(grad_whole * hat_g, -1, keepdims=True)
        )
        grad_full = jnp.where(ch == 0, grad_full, pltpu.roll(grad_full, 64, 1))
        grad_ref[chunk(g), :] = grad_full[:, 0:64].astype(bf16)

    pltpu.make_async_copy(recvz, recvz, grecv_sem.at[1]).wait()
    send6[...] = jnp.sum(recvz[...].astype(f32), 0).astype(bf16)
    for dx, dy in plane:
        _, device = plane_peer(dx, dy)
        group_copy(2, send6, recv6.at[e_me], device).start()
    pltpu.make_async_copy(send6, recv6.at[e_me], grecv_sem.at[2]).start()
    pltpu.make_async_copy(recv6, recv6, grecv_sem.at[2]).wait()
    unpack(flat_c, 6, recv6)
    for k, g_ref in enumerate((g0_ref, g1_ref, g2_ref, g3_ref, g4_ref, g5_ref)):
        g_ref[...] = get(flat_c, 6, k) * (1.0 / 384)

    for n, dst in enumerate(
        (recv1a, recv1b, recv2a.at[0], recv2b.at[0], recv3a, recv3b, recv4a, recv4b, recv4c, recv1c)
    ):
        swap_drain(n, dst)
    pltpu.make_async_copy(recv5.at[pl.ds(0, 15)], recv5.at[pl.ds(0, 15)], gsend_sem.at[0]).wait()
    pltpu.make_async_copy(recvz.at[pl.ds(0, 7)], recvz.at[pl.ds(0, 7)], gsend_sem.at[1]).wait()
    pltpu.make_async_copy(recv6.at[pl.ds(0, 15)], recv6.at[pl.ds(0, 15)], gsend_sem.at[2]).wait()
    for copy in copies + [right_copy, mixed_copy_a, mixed_copy_b, dr_copy, df_copy]:
        copy.wait_send()


def write_kernel(*refs):
    copies = [pltpu.make_async_copy(refs[n], refs[8 + n], refs[16].at[n]) for n in range(8)]
    for copy in copies:
        copy.start()
    for copy in copies:
        copy.wait()


def on_device(pair, cotangent, w_gate_a, w_proj_a, w_gate_b, w_proj_b, w_gate_out, w_out):
    rows, cols, channels = pair.shape
    whole = pl.BlockSpec(memory_space=pltpu.VMEM)
    weights = [w.T for w in (w_gate_a, w_proj_a, w_gate_b, w_proj_b, w_gate_out, w_out)]
    vm = pltpu.VMEM
    one, two, three, five = [(64, n, 2, 128) for n in (1, 2, 3, 5)]
    sixteen, eight, block = (16, 24, 128), (8, 24, 128), (24, 128)
    shapes = [jax.ShapeDtypeStruct((PAIRS, 64), bf16)] * 2 + [jax.ShapeDtypeStruct((64, 128), f32)] * 6
    outs = pl.pallas_call(
        kernel,
        out_shape=shapes,
        in_specs=[pl.BlockSpec(memory_space=pltpu.HBM)] * 8,
        out_specs=[whole] * 8,
        scratch_shapes=[
            vm((PAIRS, 128), bf16), vm((PAIRS, 64), bf16), vm((384, 128), bf16),
            pltpu.SemaphoreType.DMA((10,)),
            vm((PAIRS, 128), bf16),
            vm((PAIRS, 128), f32),
            vm((PAIRS, 1), f32),
            vm((CHUNKS, 256, 128), f32),
            vm((768, 128), f32), vm((768, 128), f32), vm((384, 128), f32),
            vm((256, 128), f32), vm((640, 128), f32), vm((3, 192, 128), f32),
            vm(five, bf16), vm(five, bf16), vm(three, bf16), vm(three, bf16), vm(one, bf16), vm(one, bf16),
            vm(two, bf16), vm((2,) + two, bf16), vm(three, bf16), vm((2,) + three, bf16),
            vm(two, bf16), vm(two, bf16), vm(three, bf16), vm(three, bf16),
            vm(one, bf16), vm(one, bf16), vm(three, bf16), vm(three, bf16), vm(five, bf16), vm(five, bf16),
            vm(sixteen, bf16), vm(sixteen, bf16),
            vm(block, bf16), vm(eight, bf16),
            vm(block, bf16), vm(sixteen, bf16),
            vm((192, 384), bf16), vm((384, 384), bf16),
            vm((384, 128), bf16), vm((384, 384), f32), vm((192, 384), bf16), vm((192, 384), bf16),
            vm((PAIRS, 128), bf16), vm((PAIRS, 128), bf16),
            vm((64, 128), bf16), vm((64, 128), bf16),
            vm((64, PAIRS), bf16), vm((64, PAIRS), bf16),
            vm((128, PAIRS), f32),
            vm((64, PAIRS), bf16), vm((64, PAIRS), bf16),
            vm((128, PAIRS), bf16),
            vm((256, PAIRS), bf16),
            pltpu.SemaphoreType.DMA((10,)),
            pltpu.SemaphoreType.DMA((10,)),
            pltpu.SemaphoreType.DMA((9,)),
            pltpu.SemaphoreType.DMA((9,)),
            pltpu.SemaphoreType.DMA((3,)),
            pltpu.SemaphoreType.DMA((3,)),
        ],
        compiler_params=pltpu.CompilerParams(
            collective_id=0, has_side_effects=True, vmem_limit_bytes=40 << 20
        ),
    )(*[pltpu.with_memory_space_constraint(a, pltpu.HBM) for a in (pair.reshape(PAIRS, channels), cotangent.reshape(PAIRS, 64), *weights)])
    outs = pl.pallas_call(
        write_kernel,
        out_shape=shapes,
        in_specs=[whole] * 8,
        out_specs=[pl.BlockSpec(memory_space=pltpu.HBM)] * 8,
        scratch_shapes=[pltpu.SemaphoreType.DMA((8,))],
        compiler_params=pltpu.CompilerParams(vmem_limit_bytes=4 << 20),
    )(*outs)
    updated, grad_pair, ga, pa, gb, pb, go, out = outs
    return (
        updated.reshape(rows, cols, 64),
        grad_pair.reshape(rows, cols, 64),
        ga.T,
        pa.T,
        gb.T,
        pb.T,
        go.T,
        out.T,
    )


def solution(mesh):
    wide = P("row", "col", "ch")
    narrow = P(None, "ch")
    return jax.shard_map(
        on_device,
        mesh=mesh,
        in_specs=(P("row", "col", None), wide) + (narrow,) * 6,
        out_specs=(wide, wide) + (narrow,) * 6,
        check_vma=False,
    )
```

```python
import jax
import jax.numpy as jnp
from jax import lax
from jax.experimental import pallas as pl
from jax.experimental.pallas import tpu as pltpu
from jax.sharding import PartitionSpec as P

LOGICAL = pl.DeviceIdType.LOGICAL
epsilon = 1e-05
f32, bf16 = jnp.float32, jnp.bfloat16
PAIRS, CHUNKS, LANES = 1152, 9, 128


def nn(a, b):
    return lax.dot_general(a, b, (((1,), (0,)), ((), ())), preferred_element_type=f32)


def nt(a, b):
    return lax.dot_general(a, b, (((1,), (1,)), ((), ())), preferred_element_type=f32)


def tn(a, b):
    return lax.dot_general(a, b, (((0,), (0,)), ((), ())), preferred_element_type=f32)


def sigmoid(x):
    return 1.0 / (1.0 + jnp.exp(-x))


def hops(d):
    return min(d[0], 8 - d[0]) + min(d[1], 4 - d[1]) + d[2]


FAR_FIRST = sorted(
    [(dz, dy, dx) for dz in range(8) for dy in range(4) for dx in range(2) if dz + dy + dx],
    key=lambda d: -hops(d),
)


def trade(arrays):
    arrays = list(arrays)
    part = lax.broadcasted_iota(jnp.int32, arrays[0].shape, 1) // 48
    for bit in (1, 2, 4):
        high = (part & bit) != 0
        for c in range(8):
            if c & bit == 0:
                a, b = arrays[c], arrays[c | bit]
                arrays[c] = jnp.where(high, pltpu.roll(b, 48 * bit, 1), a)
                arrays[c | bit] = jnp.where(high, b, pltpu.roll(a, 384 - 48 * bit, 1))
    return arrays


def kernel(
    pair_hbm, cot_hbm, wga_hbm, wpa_hbm, wgb_hbm, wpb_hbm, wgo_hbm, wo_hbm,
    updated_ref, grad_ref, g0_ref, g1_ref, g2_ref, g3_ref, g4_ref, g5_ref,
    pair_ref, cot_ref, weights, load_sem, normed, hat, rstd1, acts, flat_a, flat_b, flat_c, pad_four, pad_ten, grid,
    send1a, recv1a, send1b, recv1b, send1c, recv1c, send2a, recv2a, send2b, recv2b, send3a, recv3a, send3b, recv3b,
    send4a, recv4a, send4b, recv4b, send4c, recv4c,
    send5, recv5, sendz, recvz, send6, recv6,
    left, right, dgrid_t, dr_sum, dr_send, dr_recv, df_send, df_recv,
    wgo_other, wo_other, cot_t, cot_other, gate_out, dproj, dgate, mixn, dfour,
    send_sem, recv_sem, psend_sem, precv_sem, gsend_sem, grecv_sem,
):
    loads = [
        pltpu.make_async_copy(pair_hbm.at[rows, :], pair_ref.at[rows, :], load_sem.at[n])
        for n, rows in enumerate(pl.ds(384 * k, 384) for k in range(3))
    ]
    loads += [
        pltpu.make_async_copy(src, weights.at[pl.ds(64 * n, 64), :], load_sem.at[3 + n])
        for n, src in enumerate((wga_hbm, wpa_hbm, wgb_hbm, wpb_hbm, wgo_hbm, wo_hbm))
    ]
    loads.append(pltpu.make_async_copy(cot_hbm, cot_ref, load_sem.at[9]))
    for load in loads:
        load.start()
    wgo_ref, wo_ref = weights.at[pl.ds(256, 64), :], weights.at[pl.ds(320, 64), :]

    row, col, ch = lax.axis_index("row"), lax.axis_index("col"), lax.axis_index("ch")
    x, y, z = row // 4, col // 2, (col % 2) * 4 + row % 4
    slot = (row % 8) * 8 + col
    half = row // 8
    own = half == ch
    other = row * 16 + col * 2 + 1 - ch

    slot_z = [((z + dz) % 8 % 4) * 8 + (z + dz) % 8 // 4 for dz in range(8)]
    slot_y = [((y + dy) % 4) * 2 for dy in range(4)]
    slot_x = [((x + dx) % 2) * 32 for dx in range(2)]
    base = 128 * ch + half

    def peer(t):
        return base + 2 * t

    barrier = pltpu.get_barrier_semaphore()
    pl.semaphore_signal(barrier, inc=1, device_id=other, device_id_type=LOGICAL)

    def each_peer(act):
        for dz, dy, dx in FAR_FIRST:
            act(slot_z[dz] + slot_y[dy] + slot_x[dx])

    plane = [(2, 2), (2, 1), (2, 3), (1, 2), (3, 2), (2, 0), (0, 2), (1, 1), (1, 3), (3, 1), (3, 3)]
    plane += [(1, 0), (3, 0), (0, 1), (0, 3)]

    def plane_peer(dx, dy):
        x_to, y_to = (x + dx) % 4, (y + dy) % 4
        return x_to * 4 + y_to, (x_to * 4 + row % 4) * 16 + (y_to * 2 + col % 2) * 2 + ch

    def line_peer(dz):
        z_to = (z + dz) % 8
        return (x * 4 + z_to % 4) * 16 + (y * 2 + z_to // 4) * 2 + ch

    def greet(device):
        pl.semaphore_signal(barrier, inc=1, device_id=device, device_id_type=LOGICAL)

    each_peer(lambda t: greet(peer(t)))

    @pl.when(jnp.logical_not(own))
    def _():
        greet(peer(slot))

    for dx, dy in plane:
        greet(plane_peer(dx, dy)[1])
    for dz in (4, 3, 5, 2, 6, 1, 7):
        greet(line_peer(dz))

    def swap_start(n, src, dst):
        def copy(t):
            return pltpu.make_async_remote_copy(
                src_ref=src.at[t],
                dst_ref=dst.at[slot],
                send_sem=send_sem.at[n],
                recv_sem=recv_sem.at[n],
                device_id=peer(t),
                device_id_type=LOGICAL,
            )

        each_peer(lambda t: copy(t).start())

        @pl.when(own)
        def _():
            pltpu.make_async_copy(src.at[slot], dst.at[slot], recv_sem.at[n]).start()

        @pl.when(jnp.logical_not(own))
        def _():
            copy(slot).start()

    def swap_wait(n, dst):
        pltpu.make_async_copy(dst, dst, recv_sem.at[n]).wait()

    def swap_drain(n, dst):
        @pl.when(own)
        def _():
            some = dst.at[pl.ds(0, 63)]
            pltpu.make_async_copy(some, some, send_sem.at[n]).wait()

        @pl.when(jnp.logical_not(own))
        def _():
            pltpu.make_async_copy(dst, dst, send_sem.at[n]).wait()

    def group_copy(n, src, dst, device):
        return pltpu.make_async_remote_copy(
            src_ref=src,
            dst_ref=dst,
            send_sem=gsend_sem.at[n],
            recv_sem=grecv_sem.at[n],
            device_id=device,
            device_id_type=LOGICAL,
        )

    def partner(n, src, dst):
        return pltpu.make_async_remote_copy(
            src_ref=src,
            dst_ref=dst,
            send_sem=psend_sem.at[n],
            recv_sem=precv_sem.at[n],
            device_id=other,
            device_id_type=LOGICAL,
        )

    def put(flat, rows, k, value):
        flat[pl.ds(k, 64, stride=rows), :] = value

    def get(flat, rows, k):
        return flat[pl.ds(k, 64, stride=rows), :]

    def pack(flat, rows, dst):
        dst[...] = flat[0 : 64 * rows, :].astype(bf16).reshape(dst.shape)

    def unpack(flat, rows, src):
        flat[0 : 64 * rows, :] = src[...].reshape(64 * rows, LANES).astype(f32)

    def run_of(three):
        def piece(flat, rows, k, c):
            return flat[pl.ds(c * rows + k, 8, stride=8 * rows), :]

        return trade([jnp.concatenate([piece(*at, c) for at in three], axis=1) for c in range(8)])

    def rows_at(flat, rows, k):
        return jnp.concatenate(run_of([(flat, rows, k + q) for q in range(3)]), axis=0)

    def put_run(three, arrays):
        for c, array in enumerate(trade(arrays)):
            for q, (flat, rows, k) in enumerate(three):
                flat[pl.ds(c * rows + k, 8, stride=8 * rows), :] = array[:, LANES * q : LANES * q + LANES]

    def eight(grid):
        return [grid[8 * m : 8 * m + 8] for m in range(8)]

    def put_rows(flat, rows, k, grid):
        put_run([(flat, rows, k + q) for q in range(3)], eight(grid))

    def chunk(g):
        return pl.ds(g * LANES, LANES)

    for load in loads[0:9]:
        load.wait()
    w_four = weights[0:256, :]
    for g in range(CHUNKS):
        values = pair_ref[chunk(g), :].astype(f32)
        centred = values - jnp.mean(values, -1, keepdims=True)
        spread = jnp.mean(centred * centred, -1, keepdims=True)
        inverse = lax.rsqrt(spread + epsilon)
        hat_g = centred * inverse
        hat[chunk(g), :] = hat_g
        rstd1[chunk(g), :] = inverse
        normed_g = hat_g.astype(bf16)
        normed[chunk(g), :] = normed_g
        projected = nt(w_four, normed_g)
        gate_a = sigmoid(projected[0:64])
        proj_a = projected[64:128]
        gate_b = sigmoid(projected[128:192])
        proj_b = projected[192:256]
        acts[g, 0:64, :] = gate_a
        acts[g, 64:128, :] = proj_a
        acts[g, 128:192, :] = gate_b
        acts[g, 192:256, :] = proj_b
        put(flat_a, 10, g, gate_b * proj_b)
        put(*((flat_a, 10, 9) if g == 0 else (pad_ten, 2, g - 1) if g < 3 else (flat_b, 6, g - 3)), gate_a * proj_a)
    pack(flat_a, 10, send1a)
    pack(pad_ten, 2, send1c)
    pack(flat_b, 6, send1b)
    put(pad_four, 4, 3, jnp.zeros((64, LANES), f32))

    @pl.when(own)
    def _():
        pl.semaphore_wait(barrier, 86)

    @pl.when(jnp.logical_not(own))
    def _():
        pl.semaphore_wait(barrier, 87)

    swap_start(0, send1a, recv1a)

    copies = [partner(0, wgo_ref, wgo_other), partner(1, wo_ref, wo_other)]
    for copy in copies:
        copy.start()
    loads[9].wait()
    for g in range(CHUNKS):
        cot_t[:, chunk(g)] = jnp.transpose(cot_ref[chunk(g), :].astype(f32)).astype(bf16)
    copies.append(partner(2, cot_t, cot_other))
    copies[2].start()
    for copy in copies:
        copy.wait_recv()
    wgo = jnp.concatenate([wgo_ref[...], wgo_other[...]], axis=0)
    for g in range(CHUNKS):
        gate_out[:, chunk(g)] = sigmoid(nt(wgo, normed[chunk(g), :]))
    mine_rows = pl.ds(pl.multiple_of(ch * 64, 64), 64)
    wo_cols = jnp.concatenate([wo_ref[...], wo_other[...]], axis=0).astype(f32)
    wo_t = jnp.where(ch == 0, wo_cols, pltpu.roll(wo_cols, 64, 1))
    wo = jnp.transpose(wo_t).astype(bf16)
    wo_t = wo_t.astype(bf16)

    swap_start(9, send1c, recv1c)
    swap_start(1, send1b, recv1b)
    swap_wait(0, recv1a)
    mine_half = pl.ds(pl.multiple_of(ch * 192, 192), 192)
    other_half = pl.ds(pl.multiple_of((1 - ch) * 192, 192), 192)
    unpack(flat_a, 10, recv1a)
    for gg in range(3):
        for m, array in enumerate(run_of([(flat_a, 10, 3 * gg + q) for q in range(3)])):
            for q in range(3):
                grid[q, pl.ds(8 * gg + m, 8, stride=24), :] = array[:, LANES * q : LANES * q + LANES]
    for q in range(3):
        right[mine_half, LANES * q : LANES * q + LANES] = grid[q].astype(bf16)
    right_copy = partner(3, right.at[mine_half, :], right.at[mine_half, :])
    right_copy.start()
    swap_wait(9, recv1c)
    unpack(flat_c, 2, recv1c)
    left[0:64, :] = jnp.concatenate(run_of([(flat_a, 10, 9), (flat_c, 2, 0), (flat_c, 2, 1)]), axis=0).astype(bf16)
    right_copy.wait_recv()
    put_rows(pad_four, 4, 0, nt(left[0:64, :], right[...]))
    pack(pad_four, 4, send2a)
    swap_start(2, send2a, recv2a.at[0])
    swap_wait(1, recv1b)
    unpack(flat_b, 6, recv1b)
    for k in range(2):
        left[64 + 64 * k : 128 + 64 * k, :] = rows_at(flat_b, 6, 3 * k).astype(bf16)
    mixed_b = nt(left[64:192, :], right[...])
    for k in range(2):
        put_rows(flat_c, 6, 3 * k, mixed_b[64 * k : 64 * k + 64])
    pack(flat_c, 6, send2b)
    swap_start(3, send2b, recv2b.at[0])

    def middle(g, first, second, rows, k, dst):
        mixed = jnp.concatenate([get(first, rows, k), get(second, rows, k)], axis=0)
        mean = jnp.mean(mixed, 0, keepdims=True)
        var = jnp.mean(mixed * mixed, 0, keepdims=True) - mean * mean
        inverse = lax.rsqrt(var + epsilon)
        mixed_hat = (mixed - mean) * inverse
        mixed_norm = mixed_hat.astype(bf16)
        mixn[:, chunk(g)] = mixed_norm
        upstream = jnp.concatenate([cot_t[:, chunk(g)], cot_other[:, chunk(g)]], axis=0).astype(f32)
        d_proj = (upstream * gate_out[:, chunk(g)]).astype(bf16)
        dproj[:, chunk(g)] = d_proj[0:64]
        d_norm = nn(wo, d_proj)
        d_mean = jnp.mean(d_norm, 0, keepdims=True)
        d_cross = jnp.mean(d_norm * mixed_hat, 0, keepdims=True)
        put(dst, rows, k, inverse * (d_norm[0:64] - d_mean - mixed_hat[0:64] * d_cross))

    swap_wait(2, recv2a.at[0])
    mixed_copy_a = partner(4, recv2a.at[0], recv2a.at[1])
    mixed_copy_a.start()
    mixed_copy_a.wait_recv()
    unpack(flat_a, 4, recv2a.at[0])
    unpack(flat_b, 4, recv2a.at[1])
    for k in range(3):
        middle(k, flat_a, flat_b, 4, k, pad_four)
    pack(pad_four, 4, send3a)
    swap_start(4, send3a, recv3a)
    swap_wait(3, recv2b.at[0])
    mixed_copy_b = partner(8, recv2b.at[0], recv2b.at[1])
    mixed_copy_b.start()
    mixed_copy_b.wait_recv()
    unpack(flat_a, 6, recv2b.at[0])
    unpack(flat_b, 6, recv2b.at[1])
    for k in range(6):
        middle(3 + k, flat_a, flat_b, 6, k, flat_c)
    pack(flat_c, 6, send3b)
    swap_start(5, send3b, recv3b)
    for g in range(CHUNKS):
        proj_out = nn(wo_t[0:64], mixn[:, chunk(g)])
        gate = gate_out[0:64, chunk(g)]
        upstream = cot_t[:, chunk(g)].astype(f32)
        dgate[:, chunk(g)] = (upstream * proj_out * gate * (1.0 - gate)).astype(bf16)
        updated_ref[chunk(g), :] = jnp.transpose(gate * proj_out).astype(bf16)
    head_gate = nn(dgate[...], normed[...])
    head_out = nt(dproj[...], mixn[...])

    swap_wait(4, recv3a)
    unpack(flat_a, 4, recv3a)
    d_grid = rows_at(flat_a, 4, 0).astype(bf16)
    put_run([(flat_b, 2, 0), (flat_b, 2, 1), (flat_c, 6, 0)], eight(nn(d_grid, right[...])))
    pack(flat_b, 2, send4a)
    swap_start(6, send4a, recv4a)
    dr_sum[...] = tn(d_grid, left[0:64, :])
    swap_wait(5, recv3b)
    unpack(flat_a, 6, recv3b)
    d_grid = jnp.concatenate([rows_at(flat_a, 6, 3 * k) for k in range(2)], axis=0)
    dgrid_t[...] = jnp.transpose(d_grid).astype(bf16)
    dr_send[...] = (dr_sum[other_half, :] + nn(dgrid_t[other_half, :], left[64:192, :])).astype(bf16)
    dr_copy = partner(5, dr_send, dr_recv)
    dr_copy.start()
    d_left = nn(d_grid.astype(bf16), right[...])
    put_rows(flat_c, 6, 1, d_left[0:64])
    put_run([(flat_c, 6, 4), (flat_c, 6, 5), (pad_ten, 10, 0)], eight(d_left[64:128]))
    pack(flat_c, 6, send4b)
    swap_start(7, send4b, recv4b)
    d_right = dr_sum[mine_half, :] + nn(dgrid_t[mine_half, :], left[64:192, :])
    dr_copy.wait_recv()
    d_right = d_right + dr_recv[...].astype(f32)
    for q in range(3):
        grid[q] = d_right[:, LANES * q : LANES * q + LANES]
    for gg in range(3):
        arrays = [
            jnp.concatenate([grid[q, pl.ds(8 * gg + m, 8, stride=24), :] for q in range(3)], axis=1)
            for m in range(8)
        ]
        put_run([(pad_ten, 10, 1 + 3 * gg + q) for q in range(3)], arrays)
    pack(pad_ten, 10, send4c)
    swap_start(8, send4c, recv4c)

    def left_terms(g, d_left):
        gate_a, proj_a = acts[g, 0:64, :], acts[g, 64:128, :]
        dfour[0:64, chunk(g)] = (d_left * proj_a * gate_a * (1.0 - gate_a)).astype(bf16)
        dfour[64:128, chunk(g)] = (d_left * gate_a).astype(bf16)

    swap_wait(6, recv4a)
    unpack(flat_a, 2, recv4a)
    for g in range(2):
        left_terms(g, get(flat_a, 2, g))
    swap_wait(7, recv4b)
    unpack(flat_b, 6, recv4b)
    for g in range(6):
        left_terms(2 + g, get(flat_b, 6, g))
    edge_left = nn(dfour[0:128, 0:1024], normed[0:1024, :])
    swap_wait(8, recv4c)
    unpack(pad_ten, 10, recv4c)
    left_terms(8, get(pad_ten, 10, 0))
    for g in range(CHUNKS):
        d_right_g = get(pad_ten, 10, 1 + g)
        gate_b, proj_b = acts[g, 128:192, :], acts[g, 192:256, :]
        dfour[128:192, chunk(g)] = (d_right_g * proj_b * gate_b * (1.0 - gate_b)).astype(bf16)
        dfour[192:256, chunk(g)] = (d_right_g * gate_b).astype(bf16)
    edge_left += nn(dfour[0:128, 1024:1152], normed[1024:1152, :])
    edge_right = nn(dfour[128:256, :], normed[...])

    for k in range(2):
        put(flat_c, 6, k, edge_left[64 * k : 64 * k + 64])
        put(flat_c, 6, 2 + k, edge_right[64 * k : 64 * k + 64])
    put(flat_c, 6, 4, head_gate)
    put(flat_c, 6, 5, jnp.where(ch == 0, head_out, pltpu.roll(head_out, 64, 1)))
    pack(flat_c, 6, send5)
    e_me, _ = plane_peer(0, 0)
    for dx, dy in plane:
        e, device = plane_peer(dx, dy)
        group_copy(0, send5.at[e], recv5.at[e_me], device).start()
    pltpu.make_async_copy(send5.at[e_me], recv5.at[e_me], grecv_sem.at[0]).start()
    for g in range(CHUNKS):
        d_flat = tn(dfour[:, chunk(g)], w_four) + tn(dgate[:, chunk(g)], wgo_ref[...])
        df_send[chunk(g), :] = d_flat.astype(bf16)
    df_copy = partner(6, df_send, df_recv)
    df_copy.start()
    pltpu.make_async_copy(recv5, recv5, grecv_sem.at[0]).wait()
    sendz[...] = jnp.sum(recv5[...].astype(f32), 0).astype(bf16)
    for dz in (4, 3, 5, 2, 6, 1, 7):
        group_copy(1, sendz, recvz.at[z], line_peer(dz)).start()
    pltpu.make_async_copy(sendz, recvz.at[z], grecv_sem.at[1]).start()
    df_copy.wait_recv()
    for g in range(CHUNKS):
        grad_whole = df_send[chunk(g), :].astype(f32) + df_recv[chunk(g), :].astype(f32)
        hat_g = hat[chunk(g), :]
        grad_full = rstd1[chunk(g), :] * (
            grad_whole
            - jnp.mean(grad_whole, -1, keepdims=True)
            - hat_g * jnp.mean(grad_whole * hat_g, -1, keepdims=True)
        )
        grad_full = jnp.where(ch == 0, grad_full, pltpu.roll(grad_full, 64, 1))
        grad_ref[chunk(g), :] = grad_full[:, 0:64].astype(bf16)

    pltpu.make_async_copy(recvz, recvz, grecv_sem.at[1]).wait()
    send6[...] = jnp.sum(recvz[...].astype(f32), 0).astype(bf16)
    for dx, dy in plane:
        _, device = plane_peer(dx, dy)
        group_copy(2, send6, recv6.at[e_me], device).start()
    pltpu.make_async_copy(send6, recv6.at[e_me], grecv_sem.at[2]).start()
    pltpu.make_async_copy(recv6, recv6, grecv_sem.at[2]).wait()
    unpack(flat_c, 6, recv6)
    for k, g_ref in enumerate((g0_ref, g1_ref, g2_ref, g3_ref, g4_ref, g5_ref)):
        g_ref[...] = get(flat_c, 6, k) * (1.0 / 384)

    for n, dst in enumerate(
        (recv1a, recv1b, recv2a.at[0], recv2b.at[0], recv3a, recv3b, recv4a, recv4b, recv4c, recv1c)
    ):
        swap_drain(n, dst)
    pltpu.make_async_copy(recv5.at[pl.ds(0, 15)], recv5.at[pl.ds(0, 15)], gsend_sem.at[0]).wait()
    pltpu.make_async_copy(recvz.at[pl.ds(0, 7)], recvz.at[pl.ds(0, 7)], gsend_sem.at[1]).wait()
    pltpu.make_async_copy(recv6.at[pl.ds(0, 15)], recv6.at[pl.ds(0, 15)], gsend_sem.at[2]).wait()
    for copy in copies + [right_copy, mixed_copy_a, mixed_copy_b, dr_copy, df_copy]:
        copy.wait_send()


def write_kernel(*refs):
    copies = [pltpu.make_async_copy(refs[n], refs[8 + n], refs[16].at[n]) for n in range(8)]
    for copy in copies:
        copy.start()
    for copy in copies:
        copy.wait()


def on_device(pair, cotangent, w_gate_a, w_proj_a, w_gate_b, w_proj_b, w_gate_out, w_out):
    rows, cols, channels = pair.shape
    whole = pl.BlockSpec(memory_space=pltpu.VMEM)
    weights = [w.T for w in (w_gate_a, w_proj_a, w_gate_b, w_proj_b, w_gate_out, w_out)]
    vm = pltpu.VMEM
    one, two, three, five = [(64, n, 2, 128) for n in (1, 2, 3, 5)]
    sixteen, eight, block = (16, 24, 128), (8, 24, 128), (24, 128)
    shapes = [jax.ShapeDtypeStruct((PAIRS, 64), bf16)] * 2 + [jax.ShapeDtypeStruct((64, 128), f32)] * 6
    outs = pl.pallas_call(
        kernel,
        out_shape=shapes,
        in_specs=[pl.BlockSpec(memory_space=pltpu.HBM)] * 8,
        out_specs=[whole] * 8,
        scratch_shapes=[
            vm((PAIRS, 128), bf16), vm((PAIRS, 64), bf16), vm((384, 128), bf16),
            pltpu.SemaphoreType.DMA((10,)),
            vm((PAIRS, 128), bf16),
            vm((PAIRS, 128), f32),
            vm((PAIRS, 1), f32),
            vm((CHUNKS, 256, 128), f32),
            vm((768, 128), f32), vm((768, 128), f32), vm((384, 128), f32),
            vm((256, 128), f32), vm((640, 128), f32), vm((3, 192, 128), f32),
            vm(five, bf16), vm(five, bf16), vm(three, bf16), vm(three, bf16), vm(one, bf16), vm(one, bf16),
            vm(two, bf16), vm((2,) + two, bf16), vm(three, bf16), vm((2,) + three, bf16),
            vm(two, bf16), vm(two, bf16), vm(three, bf16), vm(three, bf16),
            vm(one, bf16), vm(one, bf16), vm(three, bf16), vm(three, bf16), vm(five, bf16), vm(five, bf16),
            vm(sixteen, bf16), vm(sixteen, bf16),
            vm(block, bf16), vm(eight, bf16),
            vm(block, bf16), vm(sixteen, bf16),
            vm((192, 384), bf16), vm((384, 384), bf16),
            vm((384, 128), bf16), vm((384, 384), f32), vm((192, 384), bf16), vm((192, 384), bf16),
            vm((PAIRS, 128), bf16), vm((PAIRS, 128), bf16),
            vm((64, 128), bf16), vm((64, 128), bf16),
            vm((64, PAIRS), bf16), vm((64, PAIRS), bf16),
            vm((128, PAIRS), f32),
            vm((64, PAIRS), bf16), vm((64, PAIRS), bf16),
            vm((128, PAIRS), bf16),
            vm((256, PAIRS), bf16),
            pltpu.SemaphoreType.DMA((10,)),
            pltpu.SemaphoreType.DMA((10,)),
            pltpu.SemaphoreType.DMA((9,)),
            pltpu.SemaphoreType.DMA((9,)),
            pltpu.SemaphoreType.DMA((3,)),
            pltpu.SemaphoreType.DMA((3,)),
        ],
        compiler_params=pltpu.CompilerParams(
            collective_id=0, has_side_effects=True, vmem_limit_bytes=40 << 20
        ),
    )(*[pltpu.with_memory_space_constraint(a, pltpu.HBM) for a in (pair.reshape(PAIRS, channels), cotangent.reshape(PAIRS, 64), *weights)])
    outs = pl.pallas_call(
        write_kernel,
        out_shape=shapes,
        in_specs=[whole] * 8,
        out_specs=[pl.BlockSpec(memory_space=pltpu.HBM)] * 8,
        scratch_shapes=[pltpu.SemaphoreType.DMA((8,))],
        compiler_params=pltpu.CompilerParams(vmem_limit_bytes=4 << 20),
    )(*outs)
    updated, grad_pair, ga, pa, gb, pb, go, out = outs
    return (
        updated.reshape(rows, cols, 64),
        grad_pair.reshape(rows, cols, 64),
        ga.T,
        pa.T,
        gb.T,
        pb.T,
        go.T,
        out.T,
    )


def solution(mesh):
    wide = P("row", "col", "ch")
    narrow = P(None, "ch")
    return jax.shard_map(
        on_device,
        mesh=mesh,
        in_specs=(P("row", "col", None), wide) + (narrow,) * 6,
        out_specs=(wide, wide) + (narrow,) * 6,
        check_vma=False,
    )
```

```python
import jax
import jax.numpy as jnp
from jax import lax
from jax.experimental import pallas as pl
from jax.experimental.pallas import tpu as pltpu
from jax.sharding import PartitionSpec as P

LOGICAL = pl.DeviceIdType.LOGICAL
epsilon = 1e-05
f32, bf16 = jnp.float32, jnp.bfloat16
PAIRS, CHUNKS, LANES = 1152, 9, 128


def nn(a, b):
    return lax.dot_general(a, b, (((1,), (0,)), ((), ())), preferred_element_type=f32)


def nt(a, b):
    return lax.dot_general(a, b, (((1,), (1,)), ((), ())), preferred_element_type=f32)


def tn(a, b):
    return lax.dot_general(a, b, (((0,), (0,)), ((), ())), preferred_element_type=f32)


def sigmoid(x):
    return 1.0 / (1.0 + jnp.exp(-x))


def hops(d):
    return min(d[0], 8 - d[0]) + min(d[1], 4 - d[1]) + d[2]


FAR_FIRST = sorted(
    [(dz, dy, dx) for dz in range(8) for dy in range(4) for dx in range(2) if dz + dy + dx],
    key=lambda d: -hops(d),
)


def trade(arrays):
    arrays = list(arrays)
    part = lax.broadcasted_iota(jnp.int32, arrays[0].shape, 1) // 48
    for bit in (1, 2, 4):
        high = (part & bit) != 0
        for c in range(8):
            if c & bit == 0:
                a, b = arrays[c], arrays[c | bit]
                arrays[c] = jnp.where(high, pltpu.roll(b, 48 * bit, 1), a)
                arrays[c | bit] = jnp.where(high, b, pltpu.roll(a, 384 - 48 * bit, 1))
    return arrays


def kernel(
    pair_hbm, cot_hbm, wga_hbm, wpa_hbm, wgb_hbm, wpb_hbm, wgo_hbm, wo_hbm,
    updated_ref, grad_ref, g0_ref, g1_ref, g2_ref, g3_ref, g4_ref, g5_ref,
    pair_ref, cot_ref, weights, load_sem, normed, hat, rstd1, acts, flat_a, flat_b, flat_c, pad_four, pad_ten, grid,
    send1a, recv1a, send1b, recv1b, send1c, recv1c, send2a, recv2a, send2b, recv2b, send3a, recv3a, send3b, recv3b,
    send4a, recv4a, send4b, recv4b, send4c, recv4c,
    send5, recv5, sendz, recvz, send6, recv6,
    left, right, dgrid_t, dr_sum, dr_send, dr_recv, df_send, df_recv,
    wgo_other, wo_other, cot_t, cot_other, gate_out, dproj, dgate, mixn, dfour,
    send_sem, recv_sem, psend_sem, precv_sem, gsend_sem, grecv_sem,
):
    loads = [
        pltpu.make_async_copy(pair_hbm.at[rows, :], pair_ref.at[rows, :], load_sem.at[n])
        for n, rows in enumerate(pl.ds(384 * k, 384) for k in range(3))
    ]
    loads += [
        pltpu.make_async_copy(src, weights.at[pl.ds(64 * n, 64), :], load_sem.at[3 + n])
        for n, src in enumerate((wga_hbm, wpa_hbm, wgb_hbm, wpb_hbm, wgo_hbm, wo_hbm))
    ]
    loads.append(pltpu.make_async_copy(cot_hbm, cot_ref, load_sem.at[9]))
    wgo_ref, wo_ref = weights.at[pl.ds(256, 64), :], weights.at[pl.ds(320, 64), :]

    row, col, ch = lax.axis_index("row"), lax.axis_index("col"), lax.axis_index("ch")
    x, y, z = row // 4, col // 2, (col % 2) * 4 + row % 4
    slot = (row % 8) * 8 + col
    half = row // 8
    own = half == ch
    other = row * 16 + col * 2 + 1 - ch

    slot_z = [((z + dz) % 8 % 4) * 8 + (z + dz) % 8 // 4 for dz in range(8)]
    slot_y = [((y + dy) % 4) * 2 for dy in range(4)]
    slot_x = [((x + dx) % 2) * 32 for dx in range(2)]
    base = 128 * ch + half

    def peer(t):
        return base + 2 * t

    barrier = pltpu.get_barrier_semaphore()
    pl.semaphore_signal(barrier, inc=1, device_id=other, device_id_type=LOGICAL)

    def each_peer(act):
        for dz, dy, dx in FAR_FIRST:
            act(slot_z[dz] + slot_y[dy] + slot_x[dx])

    plane = [(2, 2), (2, 1), (2, 3), (1, 2), (3, 2), (2, 0), (0, 2), (1, 1), (1, 3), (3, 1), (3, 3)]
    plane += [(1, 0), (3, 0), (0, 1), (0, 3)]

    def plane_peer(dx, dy):
        x_to, y_to = (x + dx) % 4, (y + dy) % 4
        return x_to * 4 + y_to, (x_to * 4 + row % 4) * 16 + (y_to * 2 + col % 2) * 2 + ch

    def line_peer(dz):
        z_to = (z + dz) % 8
        return (x * 4 + z_to % 4) * 16 + (y * 2 + z_to // 4) * 2 + ch

    def greet(device):
        pl.semaphore_signal(barrier, inc=1, device_id=device, device_id_type=LOGICAL)

    each_peer(lambda t: greet(peer(t)))

    @pl.when(jnp.logical_not(own))
    def _():
        greet(peer(slot))

    for load in loads:
        load.start()
    for dx, dy in plane:
        greet(plane_peer(dx, dy)[1])
    for dz in (4, 3, 5, 2, 6, 1, 7):
        greet(line_peer(dz))

    def swap_start(n, src, dst):
        def copy(t):
            return pltpu.make_async_remote_copy(
                src_ref=src.at[t],
                dst_ref=dst.at[slot],
                send_sem=send_sem.at[n],
                recv_sem=recv_sem.at[n],
                device_id=peer(t),
                device_id_type=LOGICAL,
            )

        each_peer(lambda t: copy(t).start())

        @pl.when(own)
        def _():
            pltpu.make_async_copy(src.at[slot], dst.at[slot], recv_sem.at[n]).start()

        @pl.when(jnp.logical_not(own))
        def _():
            copy(slot).start()

    def swap_wait(n, dst):
        pltpu.make_async_copy(dst, dst, recv_sem.at[n]).wait()

    def swap_drain(n, dst):
        @pl.when(own)
        def _():
            some = dst.at[pl.ds(0, 63)]
            pltpu.make_async_copy(some, some, send_sem.at[n]).wait()

        @pl.when(jnp.logical_not(own))
        def _():
            pltpu.make_async_copy(dst, dst, send_sem.at[n]).wait()

    def group_copy(n, src, dst, device):
        return pltpu.make_async_remote_copy(
            src_ref=src,
            dst_ref=dst,
            send_sem=gsend_sem.at[n],
            recv_sem=grecv_sem.at[n],
            device_id=device,
            device_id_type=LOGICAL,
        )

    def partner(n, src, dst):
        return pltpu.make_async_remote_copy(
            src_ref=src,
            dst_ref=dst,
            send_sem=psend_sem.at[n],
            recv_sem=precv_sem.at[n],
            device_id=other,
            device_id_type=LOGICAL,
        )

    def put(flat, rows, k, value):
        flat[pl.ds(k, 64, stride=rows), :] = value

    def get(flat, rows, k):
        return flat[pl.ds(k, 64, stride=rows), :]

    def pack(flat, rows, dst):
        dst[...] = flat[0 : 64 * rows, :].astype(bf16).reshape(dst.shape)

    def unpack(flat, rows, src):
        flat[0 : 64 * rows, :] = src[...].reshape(64 * rows, LANES).astype(f32)

    def run_of(three):
        def piece(flat, rows, k, c):
            return flat[pl.ds(c * rows + k, 8, stride=8 * rows), :]

        return trade([jnp.concatenate([piece(*at, c) for at in three], axis=1) for c in range(8)])

    def rows_at(flat, rows, k):
        return jnp.concatenate(run_of([(flat, rows, k + q) for q in range(3)]), axis=0)

    def put_run(three, arrays):
        for c, array in enumerate(trade(arrays)):
            for q, (flat, rows, k) in enumerate(three):
                flat[pl.ds(c * rows + k, 8, stride=8 * rows), :] = array[:, LANES * q : LANES * q + LANES]

    def eight(grid):
        return [grid[8 * m : 8 * m + 8] for m in range(8)]

    def put_rows(flat, rows, k, grid):
        put_run([(flat, rows, k + q) for q in range(3)], eight(grid))

    def chunk(g):
        return pl.ds(g * LANES, LANES)

    for load in loads[0:9]:
        load.wait()
    w_four = weights[0:256, :]
    for g in range(CHUNKS):
        values = pair_ref[chunk(g), :].astype(f32)
        centred = values - jnp.mean(values, -1, keepdims=True)
        spread = jnp.mean(centred * centred, -1, keepdims=True)
        inverse = lax.rsqrt(spread + epsilon)
        hat_g = centred * inverse
        hat[chunk(g), :] = hat_g
        rstd1[chunk(g), :] = inverse
        normed_g = hat_g.astype(bf16)
        normed[chunk(g), :] = normed_g
        projected = nt(w_four, normed_g)
        gate_a = sigmoid(projected[0:64])
        proj_a = projected[64:128]
        gate_b = sigmoid(projected[128:192])
        proj_b = projected[192:256]
        acts[g, 0:64, :] = gate_a
        acts[g, 64:128, :] = proj_a
        acts[g, 128:192, :] = gate_b
        acts[g, 192:256, :] = proj_b
        put(flat_a, 10, g, gate_b * proj_b)
        put(*((flat_a, 10, 9) if g == 0 else (pad_ten, 2, g - 1) if g < 3 else (flat_b, 6, g - 3)), gate_a * proj_a)
    pack(flat_a, 10, send1a)
    pack(pad_ten, 2, send1c)
    pack(flat_b, 6, send1b)
    put(pad_four, 4, 3, jnp.zeros((64, LANES), f32))

    @pl.when(own)
    def _():
        pl.semaphore_wait(barrier, 86)

    @pl.when(jnp.logical_not(own))
    def _():
        pl.semaphore_wait(barrier, 87)

    swap_start(0, send1a, recv1a)

    copies = [partner(0, wgo_ref, wgo_other), partner(1, wo_ref, wo_other)]
    for copy in copies:
        copy.start()
    loads[9].wait()
    for g in range(CHUNKS):
        cot_t[:, chunk(g)] = jnp.transpose(cot_ref[chunk(g), :].astype(f32)).astype(bf16)
    copies.append(partner(2, cot_t, cot_other))
    copies[2].start()
    for copy in copies:
        copy.wait_recv()
    wgo = jnp.concatenate([wgo_ref[...], wgo_other[...]], axis=0)
    for g in range(CHUNKS):
        gate_out[:, chunk(g)] = sigmoid(nt(wgo, normed[chunk(g), :]))
    mine_rows = pl.ds(pl.multiple_of(ch * 64, 64), 64)
    wo_cols = jnp.concatenate([wo_ref[...], wo_other[...]], axis=0).astype(f32)
    wo_t = jnp.where(ch == 0, wo_cols, pltpu.roll(wo_cols, 64, 1))
    wo = jnp.transpose(wo_t).astype(bf16)
    wo_t = wo_t.astype(bf16)

    swap_start(9, send1c, recv1c)
    swap_start(1, send1b, recv1b)
    swap_wait(0, recv1a)
    mine_half = pl.ds(pl.multiple_of(ch * 192, 192), 192)
    other_half = pl.ds(pl.multiple_of((1 - ch) * 192, 192), 192)
    unpack(flat_a, 10, recv1a)
    for gg in range(3):
        for m, array in enumerate(run_of([(flat_a, 10, 3 * gg + q) for q in range(3)])):
            for q in range(3):
                grid[q, pl.ds(8 * gg + m, 8, stride=24), :] = array[:, LANES * q : LANES * q + LANES]
    for q in range(3):
        right[mine_half, LANES * q : LANES * q + LANES] = grid[q].astype(bf16)
    right_copy = partner(3, right.at[mine_half, :], right.at[mine_half, :])
    right_copy.start()
    swap_wait(9, recv1c)
    unpack(flat_c, 2, recv1c)
    left[0:64, :] = jnp.concatenate(run_of([(flat_a, 10, 9), (flat_c, 2, 0), (flat_c, 2, 1)]), axis=0).astype(bf16)
    right_copy.wait_recv()
    put_rows(pad_four, 4, 0, nt(left[0:64, :], right[...]))
    pack(pad_four, 4, send2a)
    swap_start(2, send2a, recv2a.at[0])
    swap_wait(1, recv1b)
    unpack(flat_b, 6, recv1b)
    for k in range(2):
        left[64 + 64 * k : 128 + 64 * k, :] = rows_at(flat_b, 6, 3 * k).astype(bf16)
    mixed_b = nt(left[64:192, :], right[...])
    for k in range(2):
        put_rows(flat_c, 6, 3 * k, mixed_b[64 * k : 64 * k + 64])
    pack(flat_c, 6, send2b)
    swap_start(3, send2b, recv2b.at[0])

    def middle(g, first, second, rows, k, dst):
        mixed = jnp.concatenate([get(first, rows, k), get(second, rows, k)], axis=0)
        mean = jnp.mean(mixed, 0, keepdims=True)
        var = jnp.mean(mixed * mixed, 0, keepdims=True) - mean * mean
        inverse = lax.rsqrt(var + epsilon)
        mixed_hat = (mixed - mean) * inverse
        mixed_norm = mixed_hat.astype(bf16)
        mixn[:, chunk(g)] = mixed_norm
        upstream = jnp.concatenate([cot_t[:, chunk(g)], cot_other[:, chunk(g)]], axis=0).astype(f32)
        d_proj = (upstream * gate_out[:, chunk(g)]).astype(bf16)
        dproj[:, chunk(g)] = d_proj[0:64]
        d_norm = nn(wo, d_proj)
        d_mean = jnp.mean(d_norm, 0, keepdims=True)
        d_cross = jnp.mean(d_norm * mixed_hat, 0, keepdims=True)
        put(dst, rows, k, inverse * (d_norm[0:64] - d_mean - mixed_hat[0:64] * d_cross))

    swap_wait(2, recv2a.at[0])
    mixed_copy_a = partner(4, recv2a.at[0], recv2a.at[1])
    mixed_copy_a.start()
    mixed_copy_a.wait_recv()
    unpack(flat_a, 4, recv2a.at[0])
    unpack(flat_b, 4, recv2a.at[1])
    for k in range(3):
        middle(k, flat_a, flat_b, 4, k, pad_four)
    pack(pad_four, 4, send3a)
    swap_start(4, send3a, recv3a)
    swap_wait(3, recv2b.at[0])
    mixed_copy_b = partner(8, recv2b.at[0], recv2b.at[1])
    mixed_copy_b.start()
    mixed_copy_b.wait_recv()
    unpack(flat_a, 6, recv2b.at[0])
    unpack(flat_b, 6, recv2b.at[1])
    for k in range(6):
        middle(3 + k, flat_a, flat_b, 6, k, flat_c)
    pack(flat_c, 6, send3b)
    swap_start(5, send3b, recv3b)
    for g in range(CHUNKS):
        proj_out = nn(wo_t[0:64], mixn[:, chunk(g)])
        gate = gate_out[0:64, chunk(g)]
        upstream = cot_t[:, chunk(g)].astype(f32)
        dgate[:, chunk(g)] = (upstream * proj_out * gate * (1.0 - gate)).astype(bf16)
        updated_ref[chunk(g), :] = jnp.transpose(gate * proj_out).astype(bf16)
    head_gate = nn(dgate[...], normed[...])
    head_out = nt(dproj[...], mixn[...])

    swap_wait(4, recv3a)
    unpack(flat_a, 4, recv3a)
    d_grid = rows_at(flat_a, 4, 0).astype(bf16)
    put_run([(flat_b, 2, 0), (flat_b, 2, 1), (flat_c, 6, 0)], eight(nn(d_grid, right[...])))
    pack(flat_b, 2, send4a)
    swap_start(6, send4a, recv4a)
    dr_sum[...] = tn(d_grid, left[0:64, :])
    swap_wait(5, recv3b)
    unpack(flat_a, 6, recv3b)
    d_grid = jnp.concatenate([rows_at(flat_a, 6, 3 * k) for k in range(2)], axis=0)
    dgrid_t[...] = jnp.transpose(d_grid).astype(bf16)
    dr_send[...] = (dr_sum[other_half, :] + nn(dgrid_t[other_half, :], left[64:192, :])).astype(bf16)
    dr_copy = partner(5, dr_send, dr_recv)
    dr_copy.start()
    d_left = nn(d_grid.astype(bf16), right[...])
    put_rows(flat_c, 6, 1, d_left[0:64])
    put_run([(flat_c, 6, 4), (flat_c, 6, 5), (pad_ten, 10, 0)], eight(d_left[64:128]))
    pack(flat_c, 6, send4b)
    swap_start(7, send4b, recv4b)
    d_right = dr_sum[mine_half, :] + nn(dgrid_t[mine_half, :], left[64:192, :])
    dr_copy.wait_recv()
    d_right = d_right + dr_recv[...].astype(f32)
    for q in range(3):
        grid[q] = d_right[:, LANES * q : LANES * q + LANES]
    for gg in range(3):
        arrays = [
            jnp.concatenate([grid[q, pl.ds(8 * gg + m, 8, stride=24), :] for q in range(3)], axis=1)
            for m in range(8)
        ]
        put_run([(pad_ten, 10, 1 + 3 * gg + q) for q in range(3)], arrays)
    pack(pad_ten, 10, send4c)
    swap_start(8, send4c, recv4c)

    def left_terms(g, d_left):
        gate_a, proj_a = acts[g, 0:64, :], acts[g, 64:128, :]
        dfour[0:64, chunk(g)] = (d_left * proj_a * gate_a * (1.0 - gate_a)).astype(bf16)
        dfour[64:128, chunk(g)] = (d_left * gate_a).astype(bf16)

    swap_wait(6, recv4a)
    unpack(flat_a, 2, recv4a)
    for g in range(2):
        left_terms(g, get(flat_a, 2, g))
    swap_wait(7, recv4b)
    unpack(flat_b, 6, recv4b)
    for g in range(6):
        left_terms(2 + g, get(flat_b, 6, g))
    edge_left = nn(dfour[0:128, 0:1024], normed[0:1024, :])
    swap_wait(8, recv4c)
    unpack(pad_ten, 10, recv4c)
    left_terms(8, get(pad_ten, 10, 0))
    for g in range(CHUNKS):
        d_right_g = get(pad_ten, 10, 1 + g)
        gate_b, proj_b = acts[g, 128:192, :], acts[g, 192:256, :]
        dfour[128:192, chunk(g)] = (d_right_g * proj_b * gate_b * (1.0 - gate_b)).astype(bf16)
        dfour[192:256, chunk(g)] = (d_right_g * gate_b).astype(bf16)
    edge_left += nn(dfour[0:128, 1024:1152], normed[1024:1152, :])
    edge_right = nn(dfour[128:256, :], normed[...])

    for k in range(2):
        put(flat_c, 6, k, edge_left[64 * k : 64 * k + 64])
        put(flat_c, 6, 2 + k, edge_right[64 * k : 64 * k + 64])
    put(flat_c, 6, 4, head_gate)
    put(flat_c, 6, 5, jnp.where(ch == 0, head_out, pltpu.roll(head_out, 64, 1)))
    pack(flat_c, 6, send5)
    e_me, _ = plane_peer(0, 0)
    for dx, dy in plane:
        e, device = plane_peer(dx, dy)
        group_copy(0, send5.at[e], recv5.at[e_me], device).start()
    pltpu.make_async_copy(send5.at[e_me], recv5.at[e_me], grecv_sem.at[0]).start()
    for g in range(CHUNKS):
        d_flat = tn(dfour[:, chunk(g)], w_four) + tn(dgate[:, chunk(g)], wgo_ref[...])
        df_send[chunk(g), :] = d_flat.astype(bf16)
    df_copy = partner(6, df_send, df_recv)
    df_copy.start()
    pltpu.make_async_copy(recv5, recv5, grecv_sem.at[0]).wait()
    sendz[...] = jnp.sum(recv5[...].astype(f32), 0).astype(bf16)
    for dz in (4, 3, 5, 2, 6, 1, 7):
        group_copy(1, sendz, recvz.at[z], line_peer(dz)).start()
    pltpu.make_async_copy(sendz, recvz.at[z], grecv_sem.at[1]).start()
    df_copy.wait_recv()
    for g in range(CHUNKS):
        grad_whole = df_send[chunk(g), :].astype(f32) + df_recv[chunk(g), :].astype(f32)
        hat_g = hat[chunk(g), :]
        grad_full = rstd1[chunk(g), :] * (
            grad_whole
            - jnp.mean(grad_whole, -1, keepdims=True)
            - hat_g * jnp.mean(grad_whole * hat_g, -1, keepdims=True)
        )
        grad_full = jnp.where(ch == 0, grad_full, pltpu.roll(grad_full, 64, 1))
        grad_ref[chunk(g), :] = grad_full[:, 0:64].astype(bf16)

    pltpu.make_async_copy(recvz, recvz, grecv_sem.at[1]).wait()
    send6[...] = jnp.sum(recvz[...].astype(f32), 0).astype(bf16)
    for dx, dy in plane:
        _, device = plane_peer(dx, dy)
        group_copy(2, send6, recv6.at[e_me], device).start()
    pltpu.make_async_copy(send6, recv6.at[e_me], grecv_sem.at[2]).start()
    pltpu.make_async_copy(recv6, recv6, grecv_sem.at[2]).wait()
    unpack(flat_c, 6, recv6)
    for k, g_ref in enumerate((g0_ref, g1_ref, g2_ref, g3_ref, g4_ref, g5_ref)):
        g_ref[...] = get(flat_c, 6, k) * (1.0 / 384)

    for n, dst in enumerate(
        (recv1a, recv1b, recv2a.at[0], recv2b.at[0], recv3a, recv3b, recv4a, recv4b, recv4c, recv1c)
    ):
        swap_drain(n, dst)
    pltpu.make_async_copy(recv5.at[pl.ds(0, 15)], recv5.at[pl.ds(0, 15)], gsend_sem.at[0]).wait()
    pltpu.make_async_copy(recvz.at[pl.ds(0, 7)], recvz.at[pl.ds(0, 7)], gsend_sem.at[1]).wait()
    pltpu.make_async_copy(recv6.at[pl.ds(0, 15)], recv6.at[pl.ds(0, 15)], gsend_sem.at[2]).wait()
    for copy in copies + [right_copy, mixed_copy_a, mixed_copy_b, dr_copy, df_copy]:
        copy.wait_send()


def write_kernel(*refs):
    copies = [pltpu.make_async_copy(refs[n], refs[8 + n], refs[16].at[n]) for n in range(8)]
    for copy in copies:
        copy.start()
    for copy in copies:
        copy.wait()


def on_device(pair, cotangent, w_gate_a, w_proj_a, w_gate_b, w_proj_b, w_gate_out, w_out):
    rows, cols, channels = pair.shape
    whole = pl.BlockSpec(memory_space=pltpu.VMEM)
    weights = [w.T for w in (w_gate_a, w_proj_a, w_gate_b, w_proj_b, w_gate_out, w_out)]
    vm = pltpu.VMEM
    one, two, three, five = [(64, n, 2, 128) for n in (1, 2, 3, 5)]
    sixteen, eight, block = (16, 24, 128), (8, 24, 128), (24, 128)
    shapes = [jax.ShapeDtypeStruct((PAIRS, 64), bf16)] * 2 + [jax.ShapeDtypeStruct((64, 128), f32)] * 6
    outs = pl.pallas_call(
        kernel,
        out_shape=shapes,
        in_specs=[pl.BlockSpec(memory_space=pltpu.HBM)] * 8,
        out_specs=[whole] * 8,
        scratch_shapes=[
            vm((PAIRS, 128), bf16), vm((PAIRS, 64), bf16), vm((384, 128), bf16),
            pltpu.SemaphoreType.DMA((10,)),
            vm((PAIRS, 128), bf16),
            vm((PAIRS, 128), f32),
            vm((PAIRS, 1), f32),
            vm((CHUNKS, 256, 128), f32),
            vm((768, 128), f32), vm((768, 128), f32), vm((384, 128), f32),
            vm((256, 128), f32), vm((640, 128), f32), vm((3, 192, 128), f32),
            vm(five, bf16), vm(five, bf16), vm(three, bf16), vm(three, bf16), vm(one, bf16), vm(one, bf16),
            vm(two, bf16), vm((2,) + two, bf16), vm(three, bf16), vm((2,) + three, bf16),
            vm(two, bf16), vm(two, bf16), vm(three, bf16), vm(three, bf16),
            vm(one, bf16), vm(one, bf16), vm(three, bf16), vm(three, bf16), vm(five, bf16), vm(five, bf16),
            vm(sixteen, bf16), vm(sixteen, bf16),
            vm(block, bf16), vm(eight, bf16),
            vm(block, bf16), vm(sixteen, bf16),
            vm((192, 384), bf16), vm((384, 384), bf16),
            vm((384, 128), bf16), vm((384, 384), f32), vm((192, 384), bf16), vm((192, 384), bf16),
            vm((PAIRS, 128), bf16), vm((PAIRS, 128), bf16),
            vm((64, 128), bf16), vm((64, 128), bf16),
            vm((64, PAIRS), bf16), vm((64, PAIRS), bf16),
            vm((128, PAIRS), f32),
            vm((64, PAIRS), bf16), vm((64, PAIRS), bf16),
            vm((128, PAIRS), bf16),
            vm((256, PAIRS), bf16),
            pltpu.SemaphoreType.DMA((10,)),
            pltpu.SemaphoreType.DMA((10,)),
            pltpu.SemaphoreType.DMA((9,)),
            pltpu.SemaphoreType.DMA((9,)),
            pltpu.SemaphoreType.DMA((3,)),
            pltpu.SemaphoreType.DMA((3,)),
        ],
        compiler_params=pltpu.CompilerParams(
            collective_id=0, has_side_effects=True, vmem_limit_bytes=40 << 20
        ),
    )(*[pltpu.with_memory_space_constraint(a, pltpu.HBM) for a in (pair.reshape(PAIRS, channels), cotangent.reshape(PAIRS, 64), *weights)])
    outs = pl.pallas_call(
        write_kernel,
        out_shape=shapes,
        in_specs=[whole] * 8,
        out_specs=[pl.BlockSpec(memory_space=pltpu.HBM)] * 8,
        scratch_shapes=[pltpu.SemaphoreType.DMA((8,))],
        compiler_params=pltpu.CompilerParams(vmem_limit_bytes=4 << 20),
    )(*outs)
    updated, grad_pair, ga, pa, gb, pb, go, out = outs
    return (
        updated.reshape(rows, cols, 64),
        grad_pair.reshape(rows, cols, 64),
        ga.T,
        pa.T,
        gb.T,
        pb.T,
        go.T,
        out.T,
    )


def solution(mesh):
    wide = P("row", "col", "ch")
    narrow = P(None, "ch")
    return jax.shard_map(
        on_device,
        mesh=mesh,
        in_specs=(P("row", "col", None), wide) + (narrow,) * 6,
        out_specs=(wide, wide) + (narrow,) * 6,
        check_vma=False,
    )
```
